32 devices in a mesh: seq: 8 (over y, x, core), head: 4 (over z).
Axes of the slice: x: 2, y: 2, z: 4, core: 2. Of those that a mesh axis runs over, the one named last changes fastest.
Arguments:
- hidden_in: float32 [4096, 768], P('seq'), may hold values from -6 to 6
- grad_out: float32 [4096, 768], P('seq'), may hold values from -6 to 6
- doc_lengths: int32 [3], replicated, may hold values from 1 to 2048, as said below
- norm_gain: float32 [2, 768], replicated, may hold values from 0.5 to 1.5
- proj_z: float32 [2, 768, 1536], P(None, 'seq', 'head'), may hold values from -0.21875 to 0.21875
- proj_x: float32 [2, 768, 1536], P(None, 'seq', 'head'), may hold values from -0.21875 to 0.21875
- proj_bc: float32 [2, 768, 256], P(None, 'seq', 'head'), may hold values from -0.21875 to 0.21875
- proj_dt: float32 [2, 768, 24], P(None, 'seq', 'head'), may hold values from -0.21875 to 0.21875
- conv_x_kernel: float32 [2, 4, 1536], P(None, None, 'head'), may hold values from -3 to 3
- conv_x_bias: float32 [2, 1536], P(None, 'head'), may hold values from -0.5 to 0.5
- conv_bc_kernel: float32 [2, 4, 256], P(None, None, 'head'), may hold values from -3 to 3
- conv_bc_bias: float32 [2, 256], P(None, 'head'), may hold values from -0.5 to 0.5
- dt_bias: float32 [2, 24], P(None, 'head'), may hold values from -6 to -3
- a_log: float32 [2, 24], P(None, 'head'), may hold values from -3 to 2
- skip_gain: float32 [2, 24], P(None, 'head'), may hold values from 0.5 to 1.5
- gate_gain: float32 [2, 1536], P(None, 'head'), may hold values from 0.5 to 1.5
- proj_out: float32 [2, 768, 1536], P(None, 'seq', 'head'), may hold values from -0.15625 to 0.15625
Outputs:
- hidden_out: float32 [4096, 768], P('seq')
- grad_hidden: float32 [4096, 768], P('seq')
- grad_norm_gain: float32 [2, 768], replicated
- grad_proj_z: float32 [2, 768, 1536], P(None, 'seq', 'head')
- grad_proj_x: float32 [2, 768, 1536], P(None, 'seq', 'head')
- grad_proj_bc: float32 [2, 768, 256], P(None, 'seq', 'head')
- grad_proj_dt: float32 [2, 768, 24], P(None, 'seq', 'head')
- grad_conv_x_kernel: float32 [2, 4, 1536], P(None, None, 'head')
- grad_conv_x_bias: float32 [2, 1536], P(None, 'head')
- grad_conv_bc_kernel: float32 [2, 4, 256], P(None, None, 'head')
- grad_conv_bc_bias: float32 [2, 256], P(None, 'head')
- grad_dt_bias: float32 [2, 24], P(None, 'head')
- grad_a_log: float32 [2, 24], P(None, 'head')
- grad_skip_gain: float32 [2, 24], P(None, 'head')
- grad_gate_gain: float32 [2, 1536], P(None, 'head')
- grad_proj_out: float32 [2, 768, 1536], P(None, 'seq', 'head')
The draws below stay inside these ranges and needn't reach their ends.
Inputs may be any that keep to these rules, and one draw needn't show every extreme that they name: `doc_lengths`: the 3 lengths sum to 4096, and the longest is exactly 2048.
All inputs are finite; a program needn't handle non-finite values.
Results may differ from the reference program's by a relative error of at most 0.0003.
Values sent between devices are 32-bit elements; how exact they have to be, the bound alone decides.
A program may use at most 192 MiB of HBM per device.

```python
import jax
import jax.numpy as jnp
from jax import lax

D = 768
HEADS = 24
HEADDIM = 64
STATE = 128
KERNEL = 4
LAYERS = 2
BLOCK = 256
INNER = 1536
TOKENS = 4096
NSEQ = 3
MOST = 2048


def split_amount(key, amount_all, count_pieces):
    weights = jax.random.randint(key, (count_pieces,), 900, 1001).astype(jnp.int32)
    running = jnp.cumsum(weights).astype(jnp.int32)
    bounds = amount_all * running // running[-1]
    before = jnp.concatenate([jnp.zeros((1,), jnp.int32), bounds[:-1]])
    return (bounds - before).astype(jnp.int32)


def draw_doc_lengths(key, part):
    key_offset = jax.random.fold_in(key, 11)
    key_left = jax.random.fold_in(key, 12)
    key_right = jax.random.fold_in(key, 13)
    offset_draw = jax.random.randint(key_offset, (), -(MOST // 8), MOST // 8 + 1).astype(jnp.int32)
    left_amount = TOKENS // 2 - MOST // 2 + offset_draw
    right_amount = TOKENS - MOST - left_amount
    left_count = (NSEQ - 1) // 2
    right_count = NSEQ - 1 - left_count
    longest = jnp.full((1,), MOST, jnp.int32)
    return jnp.concatenate([split_amount(key_left, left_amount, left_count), longest, split_amount(key_right, right_amount, right_count)]).astype(jnp.int32)


def block_levels(rng, shape, shards, low, top_value):
    level, own = 1.0, jax.random.fold_in(rng, 6)
    for dim, shards_of in shards:
        heights = jnp.exp(jax.random.uniform(jax.random.fold_in(own, dim), (shards_of,), jnp.float32, low / len(shards), top_value / len(shards)))
        level = level * jnp.repeat(heights, shape[dim] // shards_of).reshape([-1 if axis == dim else 1 for axis in range(len(shape))])
    return level


def scatter_about(rng, extent, scale, bound, shards=(), kind=jnp.bfloat16):
    drawn = scale * jax.random.normal(rng, extent, jnp.float32)
    if shards:
        drawn = drawn * block_levels(rng, extent, shards, -0.22, 0.18)
    return jnp.clip(drawn, -bound, bound).astype(kind)


def setup_inputs(seed: int = 0) -> dict:
    key_list = jax.random.split(jax.random.key(seed), 18)
    hidden_in = scatter_about(key_list[0], (TOKENS, D), 1.0, 6.0, ((0, 8),), jnp.float32)
    grad_out = scatter_about(key_list[1], (TOKENS, D), 1.0, 6.0, ((0, 8),), jnp.float32)
    doc_lengths = draw_doc_lengths(jax.random.fold_in(key_list[17], 71), 0)
    norm_gain = jnp.clip(1.0 + 0.1 * jax.random.normal(key_list[3], (LAYERS, D), jnp.float32), 0.5, 1.5)
    proj_z = scatter_about(key_list[4], (LAYERS, D, INNER), D ** -0.5, 0.21875, ((1, 8), (2, 4)), jnp.float32)
    proj_x = scatter_about(key_list[5], (LAYERS, D, INNER), D ** -0.5, 0.21875, ((1, 8), (2, 4)), jnp.float32)
    proj_bc = scatter_about(key_list[6], (LAYERS, D, 2 * STATE), D ** -0.5, 0.21875, ((1, 8), (2, 4)), jnp.float32)
    proj_dt = scatter_about(key_list[7], (LAYERS, D, HEADS), D ** -0.5, 0.21875, ((1, 8), (2, 4)), jnp.float32)
    conv_x_kernel = scatter_about(key_list[8], (LAYERS, KERNEL, INNER), KERNEL ** -0.5, 3.0, ((2, 4),), jnp.float32)
    conv_x_bias = jnp.clip(jax.random.uniform(key_list[9], (LAYERS, INNER), jnp.float32, -0.5, 0.5) * block_levels(key_list[9], (LAYERS, INNER), ((1, 4),), -0.4, 0.0), -0.5, 0.5)
    conv_bc_kernel = scatter_about(key_list[10], (LAYERS, KERNEL, 2 * STATE), KERNEL ** -0.5, 3.0, ((2, 4),), jnp.float32)
    conv_bc_bias = jnp.clip(jax.random.uniform(key_list[11], (LAYERS, 2 * STATE), jnp.float32, -0.5, 0.5) * block_levels(key_list[11], (LAYERS, 2 * STATE), ((1, 4),), -0.4, 0.0), -0.5, 0.5)
    dt_bias = jnp.clip(-6.0 + 3.0 * jax.random.uniform(key_list[12], (LAYERS, HEADS), jnp.float32) ** block_levels(key_list[12], (LAYERS, HEADS), ((1, 4),), -0.2, 0.2), -6.0, -3.0)
    a_log = jnp.clip(-3.0 + 5.0 * jax.random.uniform(key_list[13], (LAYERS, HEADS), jnp.float32) ** block_levels(key_list[13], (LAYERS, HEADS), ((1, 4),), -0.2, 0.2), -3.0, 2.0)
    skip_gain = jnp.clip(0.5 + 1.0 * jax.random.uniform(key_list[14], (LAYERS, HEADS), jnp.float32) ** block_levels(key_list[14], (LAYERS, HEADS), ((1, 4),), -0.2, 0.2), 0.5, 1.5)
    gate_gain = jnp.clip(1.0 + 0.1 * jax.random.normal(key_list[15], (LAYERS, INNER), jnp.float32), 0.5, 1.5)
    proj_out = scatter_about(key_list[16], (LAYERS, D, INNER), INNER ** -0.5, 0.15625, ((1, 8), (2, 4)), jnp.float32)
    return dict(hidden_in=hidden_in, grad_out=grad_out, doc_lengths=doc_lengths, norm_gain=norm_gain, proj_z=proj_z, proj_x=proj_x, proj_bc=proj_bc, proj_dt=proj_dt, conv_x_kernel=conv_x_kernel, conv_x_bias=conv_x_bias, conv_bc_kernel=conv_bc_kernel, conv_bc_bias=conv_bc_bias, dt_bias=dt_bias, a_log=a_log, skip_gain=skip_gain, gate_gain=gate_gain, proj_out=proj_out)


EPS = 1e-05
NEG_FILL = -1e+30

def matmul_high(left, right):
    return jnp.dot(left, right, precision=lax.Precision.HIGHEST, preferred_element_type=jnp.float32)

def swish_act(values):
    return values * jax.nn.sigmoid(values)

def rms_scale(values):
    return lax.rsqrt(lax.optimization_barrier(jnp.mean(values * values, axis=-1, keepdims=True)) + EPS)

def segment_ids(doc_lengths, positions):
    lengths = doc_lengths.astype(jnp.int32)
    ends = jnp.cumsum(lengths).astype(jnp.int32)
    starts = ends - lengths
    return lax.optimization_barrier(jnp.sum((positions[:, None] >= starts[None, :]).astype(jnp.int32), axis=1)).astype(jnp.int32) - 1

def depthwise_conv(extended, seg_ext, seg_now, kernel, bias):
    count = seg_now.shape[0]
    total = jnp.zeros((count, extended.shape[1]), jnp.float32) + bias[None, :]
    for offset in range(KERNEL):
        keep = (seg_ext[offset:offset + count] == seg_now).astype(jnp.float32)
        total = total + kernel[offset][None, :] * extended[offset:offset + count] * keep[:, None]
    return swish_act(total)

def decay_rates(dt_raw, dt_bias, a_log):
    step_size = jax.nn.softplus(dt_raw + dt_bias)
    return (step_size, -step_size * jnp.exp(a_log))

def block_step(state, seg_prev, values, step_size, log_decay, b_matrix, c_matrix, seg_now):
    count, width = values.shape
    heads = step_size.shape[1]
    head_dim = width // heads
    cum_decay = jnp.cumsum(log_decay, axis=0)
    order = jnp.arange(count)
    allowed = (order[:, None] >= order[None, :]) & (seg_now[:, None] == seg_now[None, :])
    spans = cum_decay.T[:, :, None] - cum_decay.T[:, None, :]
    decays = jnp.exp(jnp.where(allowed[None], spans, NEG_FILL))
    intersection = matmul_high(c_matrix, b_matrix.T)
    scores = decays * intersection[None] * step_size.T[:, None, :]
    per_head = values.reshape(count, heads, head_dim)
    output = jnp.einsum('hts,shp->thp', scores, per_head, precision=lax.Precision.HIGHEST).reshape(count, width)
    enter = jnp.exp(cum_decay) * (seg_now == seg_prev).astype(jnp.float32)[:, None]
    output = output + jnp.repeat(enter, head_dim, axis=1) * matmul_high(c_matrix, state.T)
    keep_end = (seg_now == seg_now[-1]).astype(jnp.float32)
    weight_end = jnp.exp(cum_decay[-1][None, :] - cum_decay) * step_size * keep_end[:, None]
    weighted = values * jnp.repeat(weight_end, head_dim, axis=1)
    carry = jnp.exp(cum_decay[-1]) * (seg_now[-1] == seg_prev).astype(jnp.float32)
    state = state * jnp.repeat(carry, head_dim)[:, None] + jnp.einsum('tc,tn->cn', weighted, b_matrix, precision=lax.Precision.HIGHEST)
    return (state, seg_now[-1], output)

def ssd_scan(values, step_size, log_decay, b_matrix, c_matrix, seg_now):
    count = values.shape[0]
    blocks = count // BLOCK

    def one_block(carry, pieces):
        state, seg_prev = carry
        state, seg_last, output = block_step(state, seg_prev, *pieces)
        return ((state, seg_last), output)
    pieces = tuple((array_in.reshape((blocks, BLOCK) + array_in.shape[1:]) for array_in in (values, step_size, log_decay, b_matrix, c_matrix, seg_now)))
    start = (jnp.zeros((values.shape[1], STATE), jnp.float32), jnp.zeros((), jnp.int32))
    _, outputs = lax.scan(jax.checkpoint(one_block), start, pieces)
    return outputs.reshape(count, values.shape[1])

def pad_front(raw):
    return jnp.concatenate([jnp.zeros((KERNEL - 1, raw.shape[1]), jnp.float32), raw], axis=0)

def layer_forward(hidden, seg_ext, seg_now, params):
    norm_gain, proj_z, proj_x, proj_bc, proj_dt, conv_x_kernel, conv_x_bias, conv_bc_kernel, conv_bc_bias, dt_bias, a_log, skip_gain, gate_gain, proj_out = params
    normed = hidden * rms_scale(hidden) * norm_gain[None, :]
    gate_in = matmul_high(normed, proj_z)
    x_raw = matmul_high(normed, proj_x)
    bc_raw = matmul_high(normed, proj_bc)
    dt_raw = matmul_high(normed, proj_dt)
    values = depthwise_conv(pad_front(x_raw), seg_ext, seg_now, conv_x_kernel, conv_x_bias)
    bc_act = depthwise_conv(pad_front(bc_raw), seg_ext, seg_now, conv_bc_kernel, conv_bc_bias)
    step_size, log_decay = decay_rates(dt_raw, dt_bias, a_log)
    mixed = ssd_scan(values, step_size, log_decay, bc_act[:, :STATE], bc_act[:, STATE:], seg_now)
    mixed = mixed + jnp.repeat(skip_gain, HEADDIM)[None, :] * values
    gated = mixed * swish_act(gate_in)
    normed_out = gated * rms_scale(gated) * gate_gain[None, :]
    return hidden + matmul_high(normed_out, proj_out.T)

def reference(hidden_in, grad_out, doc_lengths, norm_gain, proj_z, proj_x, proj_bc, proj_dt, conv_x_kernel, conv_x_bias, conv_bc_kernel, conv_bc_bias, dt_bias, a_log, skip_gain, gate_gain, proj_out):
    positions = jnp.arange(-(KERNEL - 1), TOKENS, dtype=jnp.int32)
    seg_ext = segment_ids(doc_lengths, positions)
    seg_now = seg_ext[KERNEL - 1:]
    weights = (norm_gain, proj_z, proj_x, proj_bc, proj_dt, conv_x_kernel, conv_x_bias, conv_bc_kernel, conv_bc_bias, dt_bias, a_log, skip_gain, gate_gain, proj_out)

    def one_layer(hidden, params):
        return layer_forward(hidden, seg_ext, seg_now, params)
    layer_ckpt = jax.checkpoint(one_layer)

    def whole(hidden, params_all):
        for layer_idx in range(LAYERS):
            hidden = layer_ckpt(hidden, tuple((tensor[layer_idx] for tensor in params_all)))
        return hidden
    hidden_out, pullback = jax.vjp(whole, hidden_in, weights)
    grad_hidden, grads = pullback(grad_out)
    g_norm, g_z, g_x, g_bc, g_dt, g_cxk, g_cxb, g_cbk, g_cbb, g_dtb, g_alog, g_skip, g_gate, g_out = grads
    return (hidden_out, grad_hidden, g_norm, g_z, g_x, g_bc, g_dt, g_cxk, g_cxb, g_cbk, g_cbb, g_dtb, g_alog, g_skip, g_gate, g_out)
```

```python
import functools

import jax
import jax.numpy as jnp
from jax import lax
from jax.experimental import pallas as pl
from jax.experimental.pallas import tpu as pltpu
from jax.sharding import PartitionSpec as P

STATE = 128
KERNEL = 4
BLOCK = 256
MESHID = pl.DeviceIdType.MESH
VM = pl.BlockSpec(memory_space=pltpu.VMEM)
HB = pl.BlockSpec(memory_space=pl.ANY)


EPS = 1e-05
NEG_FILL = -1e30
EXACT = lax.Precision.HIGHEST
FAST = lax.Precision.HIGH
WIDE = 128


def mm(left, right, dims=((1,), (0,)), precision=FAST):
    return lax.dot_general(left, right, (dims, ((), ())), precision=precision, preferred_element_type=jnp.float32)


ROWS_T = ((1,), (1,))
COLS_T = ((0,), (0,))


def sigmoid(v):
    return 1.0 / (1.0 + jnp.exp(-v))


def softplus(v):
    small = jnp.exp(-jnp.abs(v))
    one = 1.0 + small
    exact = jnp.where(one == 1.0, small, small * jnp.log(one) / jnp.where(one == 1.0, 1.0, one - 1.0))
    return jnp.maximum(v, 0.0) + exact


def spread_heads(per_head, heads, dim):
    rows = per_head.shape[0]
    return jnp.concatenate([jnp.broadcast_to(per_head[:, h : h + 1], (rows, dim)) for h in range(heads)], axis=1)


def scaled_rows(state, factors, heads):
    dim = state.shape[0] // heads
    return jnp.concatenate([state[h * dim : (h + 1) * dim] * factors[:, h : h + 1] for h in range(heads)], axis=0)


def head_sums(wide, heads):
    width = wide.shape[1]
    dim = width // heads
    row = lax.broadcasted_iota(jnp.int32, (width, WIDE), 0)
    col = lax.broadcasted_iota(jnp.int32, (width, WIDE), 1)
    pick = ((row >= col * dim) & (row < (col + 1) * dim)).astype(jnp.float32)
    return mm(wide, pick, precision=EXACT)


def lower_of(rows):
    return lax.broadcasted_iota(jnp.int32, (rows, rows), 0) >= lax.broadcasted_iota(jnp.int32, (rows, rows), 1)


def normed_of(h, gain):
    r = lax.rsqrt(jnp.mean(h * h, axis=1, keepdims=True) + EPS)
    return h * r * gain


def conv_total(raw_ref, cw_ref, masks_ref, at, rows):
    total = cw_ref[KERNEL : KERNEL + 1, :] + cw_ref[KERNEL - 1 : KERNEL, :] * raw_ref[8 + at : 8 + at + rows, :]
    for k in range(KERNEL - 1):
        first = 8 + at - (KERNEL - 1) + k
        total = total + cw_ref[k : k + 1, :] * (raw_ref[first : first + rows, :] * masks_ref[at : at + rows, k : k + 1])
    return total


def front_kernel(heads, block, hidden, tail, gain, wz, wx, wside, cw, hp, masks, segrow, cmask, z_o, raw_o, dt_o, act_o, cum_o, y_o, st_o, carry_o, dev_o):
    count, inner = z_o.shape
    dim = inner // heads
    wide_bc = 2 * STATE
    t = normed_of(tail[...], gain[...])
    raw_o[0:8, :inner] = mm(t, wx[...])
    raw_o[0:8, inner:] = mm(t, wside[:, :wide_bc])
    lower = lower_of(block)
    lower_f = lower.astype(jnp.float32)
    carry_o[...] = jnp.zeros_like(carry_o)
    state = decay = None
    for b in range(count // block):
        at = b * block
        own = slice(at, at + block)
        n = normed_of(hidden[own, :], gain[...])
        z_o[own, :] = mm(n, wz[...])
        raw_o[8 + at : 8 + at + block, :inner] = mm(n, wx[...])
        side = mm(n, wside[...])
        raw_o[8 + at : 8 + at + block, inner:] = side[:, :wide_bc]
        dt = side[:, wide_bc:]
        dt_o[own, :] = dt
        total = conv_total(raw_o, cw, masks, at, block)
        act = total * sigmoid(total)
        act_o[own, :] = act
        values, bm, cm = act[:, :inner], act[:, inner : inner + STATE], act[:, inner + STATE :]
        step = softplus(dt + hp[0:1, :])
        cum = mm(lower_f, -step * jnp.exp(hp[1:2, :]), precision=EXACT)
        cum_o[own, :] = cum
        cum_t = cum.T
        allowed = lower & (masks[own, 5:6] == segrow[0:1, own])
        scores = mm(cm, bm, ROWS_T)
        last = cum[block - 1 : block, :]
        leave = jnp.exp(last - cum) * masks[own, 4:5]
        ys, ws = [], []
        for h in range(heads):
            v = values[:, h * dim : (h + 1) * dim]
            x = v * step[:, h : h + 1]
            spans = cum[:, h : h + 1] - cum_t[h : h + 1, :]
            s = jnp.exp(jnp.where(allowed, spans, NEG_FILL)) * scores
            ys.append(mm(s, x) + hp[2:3, h : h + 1] * v)
            ws.append(x * leave[:, h : h + 1])
        y_o[own, :] = jnp.concatenate(ys, axis=1)
        states = mm(jnp.concatenate(ws, axis=1), bm, COLS_T)
        st_o[b * inner : (b + 1) * inner, :] = states
        carry = jnp.exp(last) * cmask[b : b + 1, :]
        carry_o[b : b + 1, :] = carry
        state = states if b == 0 else scaled_rows(state, carry, heads) + states
        decay = carry if b == 0 else decay * carry
    dev_o[:inner, :] = state
    dev_o[inner:, :] = jnp.broadcast_to(decay, (8, WIDE))


def mix_kernel(heads, block, last_layer, pieces, before, y, act, cum, masks, st, carry, z, ggain, wout, grad, rows_o, e_o, mixed_o, entry_o):
    count, inner = z.shape
    dim = inner // heads
    state = jnp.zeros((inner, STATE), jnp.float32)
    for j in range(pieces.shape[0]):
        later = scaled_rows(state, pieces[j, inner : inner + 1, :], heads) + pieces[j, :inner, :]
        state = jnp.where(before[j : j + 1, :] > 0.5, later, state)
    cols = []
    for b in range(count // block):
        at = b * block
        own = slice(at, at + block)
        entry_o[b * inner : (b + 1) * inner, :] = state
        enter = jnp.exp(cum[own, :]) * masks[own, 3:4]
        read = mm(act[own, inner + STATE :], state, ROWS_T)
        mixed = y[own, :] + spread_heads(enter, heads, dim) * read
        mixed_o[own, :] = mixed
        zz = z[own, :]
        gated = mixed * (zz * sigmoid(zz))
        out = mm(gated * ggain[...], wout[...], ROWS_T)
        rows_o[own, :] = out
        squares = jnp.sum(gated * gated, axis=1, keepdims=True)
        if last_layer:
            dots = jnp.sum(grad[own, :] * out, axis=1, keepdims=True)
        else:
            dots = jnp.zeros_like(squares)
        lane = lax.broadcasted_iota(jnp.int32, (block, WIDE), 1)
        both = jnp.where(lane == 0, squares, jnp.where(lane == 1, dots, 0.0))
        e_o[:, own] = both.T[0:8, :]
        state = scaled_rows(state, carry[b : b + 1, :], heads) + st[b * inner : (b + 1) * inner, :]


def gate_back_kernel(heads, block, inner_all, last_layer, grad, e, sums, act, cum, masks, carry, z, ggain, wout, mixed, entry, dmix_o, dz_o, de_o, dc_o, dentry_o, dstate_o, dwout_o, dgg_o):
    count, inner = z.shape
    dim = inner // heads
    ggain_sum = jnp.zeros((1, inner), jnp.float32)
    for b in range(count // block):
        at = b * block
        own = slice(at, at + block)
        et = jnp.concatenate([e[:, own], jnp.zeros((WIDE - 8, block), jnp.float32)], axis=0).T
        scale = lax.rsqrt(et[:, 0:1] / inner_all + EPS)
        dh = grad[own, :]
        if last_layer:
            gs = et[:, 1:2]
        else:
            gs = jnp.sum(dh * sums[own, :], axis=1, keepdims=True)
        dsq = gs * (-0.5 / inner_all) * scale * scale * scale
        drows = scale * dh
        dgg = mm(drows, wout[...])
        zz = z[own, :]
        sg = sigmoid(zz)
        sil = zz * sg
        mx = mixed[own, :]
        gated = mx * sil
        ggain_sum = ggain_sum + jnp.sum(dgg * gated, axis=0, keepdims=True)
        dgated = dgg * ggain[...] + 2.0 * dsq * gated
        part = mm(drows, gated * ggain[...], COLS_T)
        if b == 0:
            dwout_o[...] = part
        else:
            dwout_o[...] += part
        dmix = dgated * sil
        dmix_o[own, :] = dmix
        dz_o[own, :] = dgated * mx * (sg * (1.0 + zz * (1.0 - sg)))
        enter = jnp.exp(cum[own, :]) * masks[own, 3:4]
        cm = act[own, inner + STATE :]
        en = entry[b * inner : (b + 1) * inner, :]
        read = mm(cm, en, ROWS_T)
        de_o[own, :] = enter * head_sums(dmix * read, heads)
        dread = dmix * spread_heads(enter, heads, dim)
        dc_o[own, :] = mm(dread, en)
        dentry_o[b * inner : (b + 1) * inner, :] = mm(dread, cm, COLS_T)
    dgg_o[...] = jnp.broadcast_to(ggain_sum, dgg_o.shape)
    blocks = count // block
    g = dentry_o[(blocks - 1) * inner :, :]
    for b in range(blocks - 2, -1, -1):
        g = dentry_o[b * inner : (b + 1) * inner, :] + scaled_rows(g, carry[b : b + 1, :], heads)
    dstate_o[...] = g


def scan_back_kernel(heads, block, pieces, gpieces, after, dmix, act, raw, dt, cum, de, dc, dentry, entry, carry, masks, segrow, cw, hp, draw_o, ddt_o, dcw_o, dhp_o, dtot):
    count, inner = dmix.shape
    dim = inner // heads
    g = jnp.zeros((inner, STATE), jnp.float32)
    for j in range(gpieces.shape[0] - 1, -1, -1):
        later = scaled_rows(g, pieces[j, inner : inner + 1, :], heads) + gpieces[j]
        g = jnp.where(after[j : j + 1, :] > 0.5, later, g)
    lower = lower_of(block)
    lower_f = lower.astype(jnp.float32)
    sub = lax.broadcasted_iota(jnp.int32, (block, WIDE), 0)
    a_exp = jnp.exp(hp[1:2, :])
    bias_sum = alog_sum = skip_sum = jnp.zeros((1, WIDE), jnp.float32)
    for b in range(count // block - 1, -1, -1):
        at = b * block
        own = slice(at, at + block)
        values, bm, cm = act[own, :inner], act[own, inner : inner + STATE], act[own, inner + STATE :]
        shifted = dt[own, :] + hp[0:1, :]
        step = softplus(shifted)
        cm_cum = cum[own, :]
        cum_t = cm_cum.T
        allowed = lower & (masks[own, 5:6] == segrow[0:1, own])
        scores = mm(cm, bm, ROWS_T)
        last = cm_cum[block - 1 : block, :]
        leave = jnp.exp(last - cm_cum) * masks[own, 4:5]
        carry_b = carry[b : b + 1, :]
        en = entry[b * inner : (b + 1) * inner, :]
        dw = mm(bm, g, ROWS_T)
        dscores = jnp.zeros((block, block), jnp.float32)
        dxs, ws, rowsums, colsums, dcs = [], [], [], [], []
        for h in range(heads):
            cut = slice(h * dim, (h + 1) * dim)
            x = values[:, cut] * step[:, h : h + 1]
            dy = dmix[own, cut]
            spans = cm_cum[:, h : h + 1] - cum_t[h : h + 1, :]
            decays = jnp.exp(jnp.where(allowed, spans, NEG_FILL))
            s = decays * scores
            ds = mm(dy, x, ROWS_T)
            dscores = dscores + ds * decays
            dspan = ds * s
            rowsums.append(jnp.sum(dspan, axis=1, keepdims=True))
            colsums.append(jnp.sum(dspan, axis=0, keepdims=True))
            dxs.append(mm(s, dy, COLS_T) + dw[:, cut] * leave[:, h : h + 1])
            ws.append(x * leave[:, h : h + 1])
            dcs.append(jnp.sum(jnp.sum(g[cut, :] * en[cut, :], axis=1, keepdims=True), axis=0, keepdims=True))
        pad = jnp.zeros((block, WIDE - heads), jnp.float32)
        rowsum = jnp.concatenate(rowsums + [pad], axis=1)
        colsum = jnp.concatenate(colsums + [jnp.zeros((WIDE - heads, block), jnp.float32)], axis=0).T
        dcarry = jnp.concatenate(dcs + [jnp.zeros((1, WIDE - heads), jnp.float32)], axis=1)
        dx = jnp.concatenate(dxs, axis=1)
        w = jnp.concatenate(ws, axis=1)
        dleave = head_sums(dw * w, heads)
        dlast = jnp.sum(dleave, axis=0, keepdims=True) + dcarry * carry_b
        dcum = rowsum - colsum + de[own, :] - dleave + jnp.where(sub == block - 1, dlast, 0.0)
        dld = mm(lower_f, dcum, COLS_T, EXACT)
        dstep = head_sums(dx * values, heads) - dld * a_exp
        alog_sum = alog_sum - jnp.sum(dld * step, axis=0, keepdims=True) * a_exp
        ddt = dstep * sigmoid(shifted)
        ddt_o[own, :] = ddt
        bias_sum = bias_sum + jnp.sum(ddt, axis=0, keepdims=True)
        dy_all = dmix[own, :]
        skip_sum = skip_sum + jnp.sum(head_sums(dy_all * values, heads), axis=0, keepdims=True)
        dval = dx * spread_heads(step, heads, dim) + dy_all * spread_heads(hp[2:3, :], heads, dim)
        db = mm(w, g) + mm(dscores, cm, COLS_T)
        dcm = dc[own, :] + mm(dscores, bm)
        total = conv_total(raw, cw, masks, at, block)
        sg = sigmoid(total)
        dsil = sg * (1.0 + total * (1.0 - sg))
        dtot[own, :inner] = dval * dsil[:, :inner]
        dtot[own, inner : inner + STATE] = db * dsil[:, inner : inner + STATE]
        dtot[own, inner + STATE :] = dcm * dsil[:, inner + STATE :]
        g = dentry[b * inner : (b + 1) * inner, :] + scaled_rows(g, carry_b, heads)
    dhp_o[...] = jnp.concatenate([bias_sum, alog_sum, skip_sum, jnp.zeros((5, WIDE), jnp.float32)], axis=0)
    dall = dtot[...]
    draw_o[0:8, :] = jnp.zeros_like(draw_o[0:8, :])
    draw_o[8:, :] = cw[KERNEL - 1 : KERNEL, :] * dall
    dk = []
    for k in range(KERNEL - 1):
        kept = dall * masks[:, k : k + 1]
        first = 8 - (KERNEL - 1) + k
        dk.append(jnp.sum(kept * raw[first : first + count, :], axis=0, keepdims=True))
        draw_o[first : first + count, :] = draw_o[first : first + count, :] + cw[k : k + 1, :] * kept
    dk.append(jnp.sum(dall * raw[8:, :], axis=0, keepdims=True))
    dk.append(jnp.sum(dall, axis=0, keepdims=True))
    dcw_o[...] = jnp.concatenate(dk + [jnp.zeros((7 - KERNEL, dall.shape[1]), jnp.float32)], axis=0)


def front_back_kernel(block, hidden, tail, gain, wz, wx, wside, dz, draw, ddt, dh_o, dtail_o, dwz_o, dwx_o, dwside_o, dgain_o):
    count, inner = dz.shape
    wide_bc = 2 * STATE

    def back(h, dn):
        r = lax.rsqrt(jnp.mean(h * h, axis=1, keepdims=True) + EPS)
        hr = h * r
        g = dn * gain[...]
        dgain = jnp.sum(dn * hr, axis=0, keepdims=True)
        return r * (g - hr * jnp.mean(g * hr, axis=1, keepdims=True)), dgain, hr * gain[...]

    dr = draw[0:8, :]
    dn = mm(dr[:, :inner], wx[...], ROWS_T) + mm(dr[:, inner:], wside[:, :wide_bc], ROWS_T)
    dtail, dgain, nt = back(tail[...], dn)
    dtail_o[...] = dtail
    dwx_o[...] = mm(nt, dr[:, :inner], COLS_T)
    dwside_o[:, :wide_bc] = mm(nt, dr[:, inner:], COLS_T)
    dwside_o[:, wide_bc:] = jnp.zeros_like(dwside_o[:, wide_bc:])
    for b in range(count // block):
        at = b * block
        own = slice(at, at + block)
        dzb = dz[own, :]
        drb = draw[8 + at : 8 + at + block, :]
        side = jnp.concatenate([drb[:, inner:], ddt[own, :]], axis=1)
        dn = mm(dzb, wz[...], ROWS_T) + mm(drb[:, :inner], wx[...], ROWS_T) + mm(side, wside[...], ROWS_T)
        dh, dg, n = back(hidden[own, :], dn)
        dh_o[own, :] = dh
        dgain = dgain + dg
        part = mm(n, dzb, COLS_T)
        if b == 0:
            dwz_o[...] = part
        else:
            dwz_o[...] += part
        dwx_o[...] += mm(n, drb[:, :inner], COLS_T)
        dwside_o[...] += mm(n, side, COLS_T)
    dgain_o[...] = jnp.broadcast_to(dgain, dgain_o.shape)


def f32(*shape):
    return jax.ShapeDtypeStruct(shape, jnp.float32)


def kernel_call(kernel, name, outs, args, scratch=()):
    return pl.pallas_call(
        kernel,
        out_shape=outs,
        in_specs=[VM] * len(args),
        out_specs=[VM] * len(outs),
        scratch_shapes=list(scratch),
        compiler_params=pltpu.CompilerParams(vmem_limit_bytes=56 * 1024 * 1024),
        name=name,
    )(*args)


def greet(peers, axis):
    bar = pltpu.get_barrier_semaphore()
    for p in peers:
        pl.semaphore_signal(bar, inc=1, device_id={axis: p}, device_id_type=MESHID)
    pl.semaphore_wait(bar, len(peers))


def line_reduce_kernel(n, step, d1, d2, window, x_ref, e_ref, o_ref, eo_ref, inl, inr, egot, sl, sr, rl, rr, es, er, el):
    z = lax.axis_index("head")
    count = x_ref.shape[0] // step
    greet([lax.rem(z + k, n) for k in range(1, n)], "head")
    own_e = pltpu.make_async_copy(e_ref, egot.at[z], el)
    own_e.start()

    def extra(k):
        return pltpu.make_async_remote_copy(src_ref=e_ref, dst_ref=egot.at[z], send_sem=es.at[k], recv_sem=er.at[k],
            device_id={"head": lax.rem(z + k, n)}, device_id_type=MESHID)
    for k in range(1, n):
        extra(k).start()
    low = (n - 1) // 2
    def rows(c):
        return pl.ds(pl.multiple_of(c * step, 8), step)
    def root(c):
        return low + lax.rem(c, 2) if n % 2 == 0 else jnp.int32(low)
    def right(src, dst, c):
        return pltpu.make_async_remote_copy(src_ref=src.at[rows(c)], dst_ref=dst.at[rows(c)], send_sem=sr.at[c], recv_sem=rl.at[c],
            device_id={"head": z + 1}, device_id_type=MESHID)
    def left(src, dst, c):
        return pltpu.make_async_remote_copy(src_ref=src.at[rows(c)], dst_ref=dst.at[rows(c)], send_sem=sl.at[c], recv_sem=rr.at[c],
            device_id={"head": z - 1}, device_id_type=MESHID)
    def forward_step(c):
        r = root(c)
        @pl.when((z < r) & (z == 0))
        def _():
            right(x_ref, inl, c).start()
        @pl.when((z < r) & (z > 0))
        def _():
            right(x_ref, inl, c).wait_recv()
            inl[rows(c), :] = inl[rows(c), :] + x_ref[rows(c), :]
            right(inl, inl, c).start()
        @pl.when((z > r) & (z == n - 1))
        def _():
            left(x_ref, inr, c).start()
        @pl.when((z > r) & (z < n - 1))
        def _():
            left(x_ref, inr, c).wait_recv()
            inr[rows(c), :] = inr[rows(c), :] + x_ref[rows(c), :]
            left(inr, inr, c).start()
    def root_step(c):
        @pl.when(z == root(c))
        def _():
            @pl.when(z > 0)
            def _():
                right(x_ref, inl, c).wait_recv()
            @pl.when(z == 0)
            def _():
                inl[rows(c), :] = jnp.zeros_like(inl[rows(c), :])
            @pl.when(z < n - 1)
            def _():
                left(x_ref, inr, c).wait_recv()
            @pl.when(z == n - 1)
            def _():
                inr[rows(c), :] = jnp.zeros_like(inr[rows(c), :])
            o_ref[rows(c), :] = x_ref[rows(c), :] + inl[rows(c), :] + inr[rows(c), :]
            @pl.when(z > 0)
            def _():
                left(o_ref, o_ref, c).start()
            @pl.when(z < n - 1)
            def _():
                right(o_ref, o_ref, c).start()
    def spread_step(c):
        r = root(c)
        @pl.when(z < r)
        def _():
            left(o_ref, o_ref, c).wait_recv()
            @pl.when(z > 0)
            def _():
                left(o_ref, o_ref, c).start()
        @pl.when(z > r)
        def _():
            right(o_ref, o_ref, c).wait_recv()
            @pl.when(z < n - 1)
            def _():
                right(o_ref, o_ref, c).start()
    def sent(c, to_right, to_left):
        @pl.when(to_right & (z < n - 1))
        def _():
            right(o_ref, o_ref, c).wait_send()
        @pl.when(to_left & (z > 0))
        def _():
            left(o_ref, o_ref, c).wait_send()
    stages = [
        (0, forward_step, lambda c: sent(c, z < root(c), z > root(c))),
        (d1, root_step, lambda c: sent(c, z == root(c), z == root(c))),
        (d2, spread_step, lambda c: sent(c, z > root(c), z < root(c))),
    ]
    def body(t, carry):
        for lag, step_of, sent_of in stages:
            c = t - lag
            @pl.when((c >= window) & (c < count + window))
            def _():
                sent_of(c - window)
            @pl.when((c >= 0) & (c < count))
            def _():
                step_of(c)
        return carry
    lax.fori_loop(0, count + d2 + window, body, 0)
    own_e.wait()
    for k in range(1, n):
        extra(k).wait()
    total = egot[0]
    for k in range(1, n):
        total = total + egot[k]
    eo_ref[...] = total


def line_reduce(x, e, cid, parts=16, d1=6, d2=14, window=3):
    n = lax.axis_size("head")
    step = x.shape[0] // parts
    return pl.pallas_call(
        functools.partial(line_reduce_kernel, n, step, d1, d2, window),
        out_shape=[f32(*x.shape), f32(*e.shape)],
        in_specs=[VM] * 2,
        out_specs=[VM] * 2,
        scratch_shapes=[pltpu.VMEM(x.shape, x.dtype), pltpu.VMEM(x.shape, x.dtype), pltpu.VMEM((n,) + e.shape, e.dtype)]
        + [pltpu.SemaphoreType.DMA((parts,))] * 4
        + [pltpu.SemaphoreType.DMA((n,))] * 2
        + [pltpu.SemaphoreType.DMA],
        compiler_params=pltpu.CompilerParams(collective_id=cid, has_side_effects=True, vmem_limit_bytes=40 * 1024 * 1024),
        name="line_reduce",
    )(x, e)


def seq_place(n):
    me = lax.axis_index("seq")
    chips = n // 2
    core, chip = lax.rem(me, 2), me // 2
    return me, chips, core, chip, me + 1 - 2 * core


def seq_greet(chips, core, chip, sib):
    bar = pltpu.get_barrier_semaphore()
    pl.semaphore_signal(bar, inc=1, device_id={"seq": sib}, device_id_type=MESHID)
    for k in range(1, chips):
        pl.semaphore_signal(bar, inc=1, device_id={"seq": lax.rem(chip + k, chips) * 2 + core}, device_id_type=MESHID)
    pl.semaphore_wait(bar, chips)


def gather_kernel(n, number, *refs):
    xs, os, (ss, rs, fs, fr, ls) = refs[:number], refs[number : 2 * number], refs[2 * number :]
    me, chips, core, chip, sib = seq_place(n)
    seq_greet(chips, core, chip, sib)

    def at(i, owner):
        rows = xs[i].shape[0]
        return os[i].at[pl.ds(pl.multiple_of(owner * rows, 8), rows)]

    def back(k):
        return lax.rem(chip - k + chips, chips) * 2 + core

    def local(i):
        return pltpu.make_async_copy(xs[i], at(i, me), ls.at[i])

    def across(i, k):
        return pltpu.make_async_remote_copy(src_ref=xs[i], dst_ref=at(i, me), send_sem=ss.at[i, k], recv_sem=rs.at[i, k],
            device_id={"seq": lax.rem(chip + k, chips) * 2 + core}, device_id_type=MESHID)

    def over(i, k):
        return pltpu.make_async_remote_copy(src_ref=xs[i] if k == 0 else at(i, back(k)), dst_ref=at(i, back(k)), send_sem=fs.at[i, k], recv_sem=fr.at[i, k],
            device_id={"seq": sib}, device_id_type=MESHID)

    pairs = [(i, k) for k in range(1, chips) for i in range(number)]
    for i, k in pairs:
        across(i, k).start()
    for i in range(number):
        over(i, 0).start()
        local(i).start()
    for i, k in pairs:
        across(i, k).wait_recv()
        over(i, k).start()
    for i in range(number):
        for k in range(chips):
            over(i, k).wait_recv()
    for i, k in pairs:
        across(i, k).wait_send()
    for i in range(number):
        for k in range(chips):
            over(i, k).wait_send()
        local(i).wait()


def seq_gather(xs, cid, spec=None):
    n = lax.axis_size("seq")
    number = len(xs)
    spec = spec or HB
    return pl.pallas_call(
        functools.partial(gather_kernel, n, number),
        out_shape=[f32(n * x.shape[0], x.shape[1]) for x in xs],
        in_specs=[spec] * number,
        out_specs=[spec] * number,
        scratch_shapes=[pltpu.SemaphoreType.DMA((number, n // 2))] * 4 + [pltpu.SemaphoreType.DMA((number,))],
        compiler_params=pltpu.CompilerParams(collective_id=cid, has_side_effects=True),
        name="seq_gather",
    )(*xs)


def direct_gather_kernel(n, axis, x_ref, o_ref, ss, rs, ls):
    me = lax.axis_index(axis)
    greet([lax.rem(me + k, n) for k in range(1, n)], axis)
    local = pltpu.make_async_copy(x_ref, o_ref.at[me], ls)

    def across(k):
        return pltpu.make_async_remote_copy(src_ref=x_ref, dst_ref=o_ref.at[me], send_sem=ss.at[k], recv_sem=rs.at[k],
            device_id={axis: lax.rem(me + k, n)}, device_id_type=MESHID)

    for k in range(1, n):
        across(k).start()
    local.start()
    for k in range(1, n):
        across(k).wait()
    local.wait()


def direct_gather(x, axis, cid):
    n = lax.axis_size(axis)
    return pl.pallas_call(
        functools.partial(direct_gather_kernel, n, axis),
        out_shape=f32(n, *x.shape),
        in_specs=[HB],
        out_specs=HB,
        scratch_shapes=[pltpu.SemaphoreType.DMA((n,))] * 2 + [pltpu.SemaphoreType.DMA],
        compiler_params=pltpu.CompilerParams(collective_id=cid, has_side_effects=True),
        name="direct_gather_" + axis,
    )(x)


def direct_sum_kernel(n, axis, scatter, x_ref, o_ref, got, ss, rs, ls):
    me = lax.axis_index(axis)
    greet([lax.rem(me + k, n) for k in range(1, n)], axis)

    def piece(owner):
        return x_ref.at[owner] if scatter else x_ref

    local = pltpu.make_async_copy(piece(me), got.at[me], ls)

    def across(k):
        peer = lax.rem(me + k, n)
        return pltpu.make_async_remote_copy(src_ref=piece(peer), dst_ref=got.at[me], send_sem=ss.at[k], recv_sem=rs.at[k],
            device_id={axis: peer}, device_id_type=MESHID)

    for k in range(1, n):
        across(k).start()
    local.start()
    for k in range(1, n):
        across(k).wait()
    local.wait()
    total = got[0]
    for k in range(1, n):
        total = total + got[k]
    o_ref[...] = total


def direct_sum(x, axis, cid, scatter=False):
    n = lax.axis_size(axis)
    shape = x.shape[1:] if scatter else x.shape
    return pl.pallas_call(
        functools.partial(direct_sum_kernel, n, axis, scatter),
        out_shape=f32(*shape),
        in_specs=[VM],
        out_specs=VM,
        scratch_shapes=[pltpu.VMEM((n,) + shape, x.dtype)] + [pltpu.SemaphoreType.DMA((n,))] * 2 + [pltpu.SemaphoreType.DMA],
        compiler_params=pltpu.CompilerParams(collective_id=cid, has_side_effects=True),
        name="direct_sum_" + axis,
    )(x)


def scatter_kernel(n, number, *refs):
    gs, os, mids, gots = (refs[i * number : (i + 1) * number] for i in range(4))
    cs, cr, ss, rs = refs[4 * number :]
    me, chips, core, chip, sib = seq_place(n)
    seq_greet(chips, core, chip, sib)

    def block(i, k, c):
        rows = os[i].shape[0]
        return pl.ds(pl.multiple_of((lax.rem(chip + k, chips) * 2 + c) * rows, 8), rows)

    def over(i, k):
        return pltpu.make_async_remote_copy(src_ref=gs[i].at[block(i, k, 1 - core)], dst_ref=mids[i].at[k], send_sem=cs.at[i, k], recv_sem=cr.at[i, k],
            device_id={"seq": sib}, device_id_type=MESHID)

    def across(i, k):
        return pltpu.make_async_remote_copy(src_ref=mids[i].at[k], dst_ref=gots[i].at[k], send_sem=ss.at[i, k], recv_sem=rs.at[i, k],
            device_id={"seq": lax.rem(chip + k, chips) * 2 + core}, device_id_type=MESHID)

    pairs = [(i, k) for k in list(range(1, chips)) + [0] for i in range(number)]
    for i, k in pairs:
        over(i, k).start()
    for i, k in pairs:
        over(i, k).wait_recv()
        mids[i][k] = mids[i][k] + gs[i][block(i, k, core), :]
        if k:
            across(i, k).start()
    for i in range(number):
        total = mids[i][0]
        for k in range(1, chips):
            across(i, k).wait_recv()
            total = total + gots[i][k]
        os[i][...] = total
    for i, k in pairs:
        over(i, k).wait_send()
        if k:
            across(i, k).wait_send()


def seq_scatter(gs, cid):
    n = lax.axis_size("seq")
    chips = n // 2
    number = len(gs)
    outs = [(g.shape[0] // n, g.shape[1]) for g in gs]
    return pl.pallas_call(
        functools.partial(scatter_kernel, n, number),
        out_shape=[f32(*o) for o in outs],
        in_specs=[VM] * number,
        out_specs=[VM] * number,
        scratch_shapes=[pltpu.VMEM((chips,) + o, jnp.float32) for o in outs] * 2 + [pltpu.SemaphoreType.DMA((number, chips))] * 4,
        compiler_params=pltpu.CompilerParams(collective_id=cid, has_side_effects=True, vmem_limit_bytes=56 * 1024 * 1024),
        name="seq_scatter",
    )(*gs)


def shifted(array, by):
    count = lax.axis_size("seq")
    pairs = [(i, i + by) for i in range(count) if 0 <= i + by < count]
    return lax.ppermute(array, "seq", pairs)


def padded(array, rows, columns):
    return jnp.pad(array, ((0, rows - array.shape[0]), (0, columns - array.shape[1])))


def body(
    hidden_in, grad_out, doc_lengths, norm_gain, proj_z, proj_x, proj_bc, proj_dt, conv_x_kernel, conv_x_bias,
    conv_bc_kernel, conv_bc_bias, dt_bias, a_log, skip_gain, gate_gain, proj_out,
):
    count, width = hidden_in.shape
    layers, rows_loc, inner = proj_z.shape
    bc_loc = proj_bc.shape[2]
    heads = proj_dt.shape[2]
    n_seq, n_head = lax.axis_size("seq"), lax.axis_size("head")
    inner_all = inner * n_head
    bc_all = 2 * STATE
    block = min(BLOCK, count)
    blocks = count // block
    mine = lax.axis_index("seq")

    order = jnp.arange(doc_lengths.shape[0])
    starts = jnp.sum(jnp.where(order[None, :] < order[:, None], doc_lengths[None, :], 0), axis=1)
    margin = KERNEL - 1
    positions = mine * count + jnp.arange(-margin, count, dtype=jnp.int32)
    seg_ext = jnp.sum((positions[:, None] >= starts[None, :]).astype(jnp.int32), axis=1) - 1
    seg = seg_ext[margin:]
    seg_blocks = seg.reshape(blocks, block)
    before = jnp.concatenate([seg_ext[margin - 1 : margin], seg_blocks[:-1, -1]])
    last = seg_blocks[:, -1]
    masks = jnp.stack(
        [seg_ext[k : k + count] == seg for k in range(margin)]
        + [seg == jnp.repeat(before, block), seg == jnp.repeat(last, block), seg, seg, seg],
        axis=1,
    ).astype(jnp.float32)
    segrow = jnp.broadcast_to(seg.astype(jnp.float32)[None], (8, count))
    cmask = jnp.broadcast_to(jnp.pad((last == before).astype(jnp.float32), (0, 8 - blocks))[:, None], (8, WIDE))
    places = jnp.arange(n_seq)
    earlier = jnp.broadcast_to((places < mine).astype(jnp.float32)[:, None], (n_seq, WIDE))
    following = jnp.broadcast_to((places > mine).astype(jnp.float32)[:, None], (n_seq, WIDE))

    own = jnp.concatenate([proj_bc, conv_bc_kernel, conv_bc_bias[:, None]], axis=1)
    own = own.reshape(-1, bc_loc)
    own = padded(own, -(-own.shape[0] // 8) * 8, bc_loc)
    columns = direct_gather(own, "head", 1)[:, : layers * (rows_loc + KERNEL + 1)]
    columns = columns.transpose(1, 0, 2).reshape(layers, rows_loc + KERNEL + 1, bc_all)
    side_width = bc_all + WIDE
    sides = [
        jnp.concatenate([columns[l, :rows_loc], jnp.pad(proj_dt[l], ((0, 0), (0, WIDE - heads)))], axis=1)
        for l in range(layers)
    ]
    wz, wx, wside, wout = ([None] * layers for _ in range(4))
    wz[0], wx[0], *wside = seq_gather([proj_z[0], proj_x[0]] + sides, 2)
    rest = lax.all_gather(
        jnp.concatenate([proj_out[0]] + [p for l in range(1, layers) for p in (proj_z[l], proj_x[l], proj_out[l])], axis=1),
        "seq", axis=0, tiled=True,
    )
    wout[0] = rest[:, :inner]
    for l in range(1, layers):
        wz[l], wx[l], wout[l] = (rest[:, (3 * l - 2 + i) * inner : (3 * l - 1 + i) * inner] for i in range(3))
    gains = [norm_gain[l : l + 1] for l in range(layers)]
    ggains = [gate_gain[l : l + 1] for l in range(layers)]
    hps = [padded(jnp.stack([dt_bias[l], a_log[l], skip_gain[l]]), 8, WIDE) for l in range(layers)]
    cws = [
        padded(
            jnp.concatenate(
                [
                    jnp.concatenate([conv_x_kernel[l], conv_x_bias[l : l + 1]], axis=0),
                    columns[l, rows_loc:],
                ],
                axis=1,
            ),
            8, inner + bc_all,
        )
        for l in range(layers)
    ]

    hidden = hidden_in
    saved = []
    sums = None
    for l in range(layers):
        tail = shifted(hidden[count - 8 :], 1)
        z, raw, dt, act, cum, y, st, carry, dev = kernel_call(
            functools.partial(front_kernel, heads, block), "front",
            [f32(count, inner), f32(count + 8, inner + bc_all), f32(count, WIDE), f32(count, inner + bc_all), f32(count, WIDE),
             f32(count, inner), f32(blocks * inner, STATE), f32(8, WIDE), f32(inner + 8, STATE)],
            [hidden, tail, gains[l], wz[l], wx[l], wside[l], cws[l], hps[l], masks, segrow, cmask],
        )
        [pieces] = seq_gather([dev], 10 + 10 * l)
        pieces = pieces.reshape(n_seq, inner + 8, STATE)
        final = l == layers - 1
        rows, e, mixed, entry = kernel_call(
            functools.partial(mix_kernel, heads, block, final), "mix",
            [f32(count, width), f32(8, count), f32(count, inner), f32(blocks * inner, STATE)],
            [pieces, earlier, y, act, cum, masks, st, carry, z, ggains[l], wout[l], grad_out],
        )
        hidden_l = hidden
        if final:
            e = direct_sum(e, "head", 11 + 10 * l)
            last_rows = lax.rsqrt(e[0] / inner_all + EPS)[:, None] * rows
            sums = grad_out
        else:
            sums, e = line_reduce(rows, e, 11 + 10 * l)
            hidden = hidden + lax.rsqrt(e[0] / inner_all + EPS)[:, None] * sums
        saved.append((hidden_l, tail, z, raw, dt, act, cum, carry, pieces, mixed, entry, e, sums))

    grad = grad_out
    big, small, shared = ([None] * layers for _ in range(3))
    for l in reversed(range(layers)):
        final = l == layers - 1
        hidden_l, tail, z, raw, dt, act, cum, carry, pieces, mixed, entry, e, sums = saved[l]
        dmix, dz, de, dc, dentry, dstate, dwout, dggain = kernel_call(
            functools.partial(gate_back_kernel, heads, block, inner_all, final), "gate_back",
            [f32(count, inner), f32(count, inner), f32(count, WIDE), f32(count, STATE), f32(blocks * inner, STATE), f32(inner, STATE),
             f32(width, inner), f32(8, inner)],
            [grad, e, sums, act, cum, masks, carry, z, ggains[l], wout[l], mixed, entry],
        )
        [gpieces] = seq_gather([dstate], 12 + 10 * l)
        if final:
            gpieces, last_rows = lax.optimization_barrier((gpieces, last_rows))
            hidden_out = hidden + lax.psum(last_rows, "head")
        draw, ddt, dcw, dhp = kernel_call(
            functools.partial(scan_back_kernel, heads, block), "scan_back",
            [f32(count + 8, inner + bc_all), f32(count, WIDE), f32(8, inner + bc_all), f32(8, WIDE)],
            [pieces, gpieces.reshape(n_seq, inner, STATE), following, dmix, act, raw, dt, cum, de, dc, dentry, entry, carry, masks, segrow, cws[l], hps[l]],
            [pltpu.VMEM((count, inner + bc_all), jnp.float32)],
        )
        part, dtail, dwz, dwx, dwside, dgain = kernel_call(
            functools.partial(front_back_kernel, block), "front_back",
            [f32(count, width), f32(8, width), f32(width, inner), f32(width, inner), f32(width, side_width), f32(8, width)],
            [hidden_l, tail, gains[l], wz[l], wx[l], wside[l], dz, draw, ddt],
        )
        part = part.at[count - 8 :].add(shifted(dtail, -1))
        shared[l] = jnp.concatenate([dgain[0], dcw[: KERNEL + 1, inner:].reshape(-1)])
        small[l] = jnp.concatenate([dcw[: KERNEL + 1, :inner].reshape(-1), dggain[0], dhp[:3, :heads].reshape(-1)])
        if l > 0:
            e = jnp.zeros((8, WIDE), jnp.float32)
            if final:
                part, hidden_out = lax.optimization_barrier((part, hidden_out))
            wide = lax.psum_scatter(jnp.concatenate([dwz, dwx, dwout, dwside], axis=1), "seq", scatter_dimension=0, tiled=True)
            big[l] = (wide[:, :inner], wide[:, inner : 2 * inner], wide[:, 2 * inner : 3 * inner], wide[:, 3 * inner :])
        else:
            e = packed(jnp.concatenate(shared))
            big[l] = seq_scatter([dwz, dwx, dwout, dwside], 13)
        summed, e = line_reduce(part, e, 14 + 10 * l)
        grad = grad + summed

    share = shared[0].shape[0]
    e = e.reshape(-1)
    flat = [jnp.concatenate([e[l * share : (l + 1) * share], small[l]]) for l in range(layers)]
    total = direct_sum(packed(jnp.concatenate(flat)), "seq", 3).reshape(-1)[: layers * flat[0].shape[0]].reshape(layers, -1)
    bcs = jnp.concatenate([big[l][3][:, :bc_all].reshape(rows_loc, n_head, bc_loc) for l in range(layers)], axis=2).transpose(1, 0, 2)
    bcs = direct_sum(bcs, "head", 4, scatter=True)

    sizes = [width, KERNEL * bc_all, bc_all, KERNEL * inner, inner, inner, heads, heads, heads]
    places = [sum(sizes[:i]) for i in range(len(sizes))]
    ngain, cbk, cbb, cxk, cxb, ggain, dbias, alog, skip = (total[:, p : p + s] for p, s in zip(places, sizes))
    offset = lax.axis_index("head") * bc_loc
    cbk = lax.dynamic_slice_in_dim(cbk.reshape(layers, KERNEL, bc_all), offset, bc_loc, axis=2)
    cbb = lax.dynamic_slice_in_dim(cbb, offset, bc_loc, axis=1)
    return (
        hidden_out,
        grad,
        ngain,
        jnp.stack([b[0] for b in big]),
        jnp.stack([b[1] for b in big]),
        jnp.stack([bcs[:, l * bc_loc : (l + 1) * bc_loc] for l in range(layers)]),
        jnp.stack([b[3][:, bc_all : bc_all + heads] for b in big]),
        cxk.reshape(layers, KERNEL, inner),
        cxb,
        cbk,
        cbb,
        dbias,
        alog,
        skip,
        ggain,
        jnp.stack([b[2] for b in big]),
    )


def packed(flat):
    rows = -(-flat.shape[0] // (8 * WIDE)) * 8
    return jnp.pad(flat, (0, rows * WIDE - flat.shape[0])).reshape(rows, WIDE)


def solution(mesh):
    in_specs = (
        P("seq", None),
        P("seq", None),
        P(),
        P(),
        P(None, "seq", "head"),
        P(None, "seq", "head"),
        P(None, "seq", "head"),
        P(None, "seq", "head"),
        P(None, None, "head"),
        P(None, "head"),
        P(None, None, "head"),
        P(None, "head"),
        P(None, "head"),
        P(None, "head"),
        P(None, "head"),
        P(None, "head"),
        P(None, "seq", "head"),
    )
    out_specs = (
        P("seq", None),
        P("seq", None),
        P(),
        P(None, "seq", "head"),
        P(None, "seq", "head"),
        P(None, "seq", "head"),
        P(None, "seq", "head"),
        P(None, None, "head"),
        P(None, "head"),
        P(None, None, "head"),
        P(None, "head"),
        P(None, "head"),
        P(None, "head"),
        P(None, "head"),
        P(None, "head"),
        P(None, "seq", "head"),
    )
    return jax.shard_map(body, mesh=mesh, in_specs=in_specs, out_specs=out_specs, check_vma=False)
```

```python
import functools

import jax
import jax.numpy as jnp
from jax import lax
from jax.experimental import pallas as pl
from jax.experimental.pallas import tpu as pltpu
from jax.sharding import PartitionSpec as P

STATE = 128
KERNEL = 4
BLOCK = 256
MESHID = pl.DeviceIdType.MESH
VM = pl.BlockSpec(memory_space=pltpu.VMEM)
HB = pl.BlockSpec(memory_space=pl.ANY)


EPS = 1e-05
NEG_FILL = -1e30
EXACT = lax.Precision.HIGHEST
FAST = lax.Precision.HIGH
WIDE = 128


def mm(left, right, dims=((1,), (0,)), precision=FAST):
    return lax.dot_general(left, right, (dims, ((), ())), precision=precision, preferred_element_type=jnp.float32)


ROWS_T = ((1,), (1,))
COLS_T = ((0,), (0,))


def sigmoid(v):
    return 1.0 / (1.0 + jnp.exp(-v))


def softplus(v):
    small = jnp.exp(-jnp.abs(v))
    one = 1.0 + small
    exact = jnp.where(one == 1.0, small, small * jnp.log(one) / jnp.where(one == 1.0, 1.0, one - 1.0))
    return jnp.maximum(v, 0.0) + exact


def spread_heads(per_head, heads, dim):
    rows = per_head.shape[0]
    return jnp.concatenate([jnp.broadcast_to(per_head[:, h : h + 1], (rows, dim)) for h in range(heads)], axis=1)


def scaled_rows(state, factors, heads):
    dim = state.shape[0] // heads
    return jnp.concatenate([state[h * dim : (h + 1) * dim] * factors[:, h : h + 1] for h in range(heads)], axis=0)


def head_sums(wide, heads):
    width = wide.shape[1]
    dim = width // heads
    row = lax.broadcasted_iota(jnp.int32, (width, WIDE), 0)
    col = lax.broadcasted_iota(jnp.int32, (width, WIDE), 1)
    pick = ((row >= col * dim) & (row < (col + 1) * dim)).astype(jnp.float32)
    return mm(wide, pick, precision=EXACT)


def lower_of(rows):
    return lax.broadcasted_iota(jnp.int32, (rows, rows), 0) >= lax.broadcasted_iota(jnp.int32, (rows, rows), 1)


def normed_of(h, gain):
    r = lax.rsqrt(jnp.mean(h * h, axis=1, keepdims=True) + EPS)
    return h * r * gain


def conv_total(raw_ref, cw_ref, masks_ref, at, rows):
    total = cw_ref[KERNEL : KERNEL + 1, :] + cw_ref[KERNEL - 1 : KERNEL, :] * raw_ref[8 + at : 8 + at + rows, :]
    for k in range(KERNEL - 1):
        first = 8 + at - (KERNEL - 1) + k
        total = total + cw_ref[k : k + 1, :] * (raw_ref[first : first + rows, :] * masks_ref[at : at + rows, k : k + 1])
    return total


def front_kernel(layer, heads, block, hidden, tail, gains, wz, wx, wside, cw, hp, masks, segrow, cmask, z_o, raw_o, dt_o, act_o, cum_o, y_o, st_o, carry_o, dev_o):
    count, inner = z_o.shape
    dim = inner // heads
    wide_bc = 2 * STATE
    gain = gains[layer : layer + 1, :]
    t = normed_of(tail[...], gain)
    raw_o[0:8, :inner] = mm(t, wx[...])
    raw_o[0:8, inner:] = mm(t, wside[:, :wide_bc])
    lower = lower_of(block)
    lower_f = lower.astype(jnp.float32)
    carry_o[...] = jnp.zeros_like(carry_o)
    state = decay = None
    for b in range(count // block):
        at = b * block
        own = slice(at, at + block)
        n = normed_of(hidden[own, :], gain)
        z_o[own, :] = mm(n, wz[...])
        raw_o[8 + at : 8 + at + block, :inner] = mm(n, wx[...])
        side = mm(n, wside[...])
        raw_o[8 + at : 8 + at + block, inner:] = side[:, :wide_bc]
        dt = side[:, wide_bc:]
        dt_o[own, :] = dt
        total = conv_total(raw_o, cw, masks, at, block)
        act = total * sigmoid(total)
        act_o[own, :] = act
        values, bm, cm = act[:, :inner], act[:, inner : inner + STATE], act[:, inner + STATE :]
        step = softplus(dt + hp[0:1, :])
        cum = mm(lower_f, -step * jnp.exp(hp[1:2, :]), precision=EXACT)
        cum_o[own, :] = cum
        cum_t = cum.T
        allowed = lower & (masks[own, 5:6] == segrow[0:1, own])
        scores = mm(cm, bm, ROWS_T)
        last = cum[block - 1 : block, :]
        leave = jnp.exp(last - cum) * masks[own, 4:5]
        ys, ws = [], []
        for h in range(heads):
            v = values[:, h * dim : (h + 1) * dim]
            x = v * step[:, h : h + 1]
            spans = cum[:, h : h + 1] - cum_t[h : h + 1, :]
            s = jnp.exp(jnp.where(allowed, spans, NEG_FILL)) * scores
            ys.append(mm(s, x) + hp[2:3, h : h + 1] * v)
            ws.append(x * leave[:, h : h + 1])
        y_o[own, :] = jnp.concatenate(ys, axis=1)
        states = mm(jnp.concatenate(ws, axis=1), bm, COLS_T)
        st_o[b * inner : (b + 1) * inner, :] = states
        carry = jnp.exp(last) * cmask[b : b + 1, :]
        carry_o[b : b + 1, :] = carry
        state = states if b == 0 else scaled_rows(state, carry, heads) + states
        decay = carry if b == 0 else decay * carry
    dev_o[:inner, :] = state
    dev_o[inner:, :] = jnp.broadcast_to(decay, (8, WIDE))


def mix_kernel(layer, heads, block, last_layer, pieces, before, y, act, cum, masks, st, carry, z, ggains, wout, grad, rows_o, e_o, mixed_o, entry_o):
    count, inner = z.shape
    dim = inner // heads
    ggain = ggains[layer : layer + 1, :]
    state = jnp.zeros((inner, STATE), jnp.float32)
    for j in range(pieces.shape[0]):
        later = scaled_rows(state, pieces[j, inner : inner + 1, :], heads) + pieces[j, :inner, :]
        state = jnp.where(before[j : j + 1, :] > 0.5, later, state)
    cols = []
    for b in range(count // block):
        at = b * block
        own = slice(at, at + block)
        entry_o[b * inner : (b + 1) * inner, :] = state
        enter = jnp.exp(cum[own, :]) * masks[own, 3:4]
        read = mm(act[own, inner + STATE :], state, ROWS_T)
        mixed = y[own, :] + spread_heads(enter, heads, dim) * read
        mixed_o[own, :] = mixed
        zz = z[own, :]
        gated = mixed * (zz * sigmoid(zz))
        out = mm(gated * ggain, wout[...], ROWS_T)
        rows_o[own, :] = out
        squares = jnp.sum(gated * gated, axis=1, keepdims=True)
        if last_layer:
            dots = jnp.sum(grad[own, :] * out, axis=1, keepdims=True)
        else:
            dots = jnp.zeros_like(squares)
        lane = lax.broadcasted_iota(jnp.int32, (block, WIDE), 1)
        both = jnp.where(lane == 0, squares, jnp.where(lane == 1, dots, 0.0))
        e_o[:, own] = both.T[0:8, :]
        state = scaled_rows(state, carry[b : b + 1, :], heads) + st[b * inner : (b + 1) * inner, :]


def gate_back_kernel(layer, heads, block, inner_all, last_layer, grad, e, sums, act, cum, masks, carry, z, ggains, wout, mixed, entry, dmix_o, dz_o, de_o, dc_o, dentry_o, dstate_o, dwout_o, dgg_o, *scaled):
    count, inner = z.shape
    dim = inner // heads
    ggain = ggains[layer : layer + 1, :]
    ggain_sum = jnp.zeros((1, inner), jnp.float32)
    for b in range(count // block):
        at = b * block
        own = slice(at, at + block)
        et = jnp.concatenate([e[:, own], jnp.zeros((WIDE - 8, block), jnp.float32)], axis=0).T
        scale = lax.rsqrt(et[:, 0:1] / inner_all + EPS)
        dh = grad[own, :]
        if last_layer:
            gs = et[:, 1:2]
            half = scaled[0].shape[0]
            for i in range(len(scaled)):
                low, high = max(at, i * half), min(at + block, (i + 1) * half)
                if low < high:
                    scaled[i][low - i * half : high - i * half, :] = scale[low - at : high - at] * sums[low:high, :]
        else:
            gs = jnp.sum(dh * sums[own, :], axis=1, keepdims=True)
        dsq = gs * (-0.5 / inner_all) * scale * scale * scale
        drows = scale * dh
        dgg = mm(drows, wout[...])
        zz = z[own, :]
        sg = sigmoid(zz)
        sil = zz * sg
        mx = mixed[own, :]
        gated = mx * sil
        ggain_sum = ggain_sum + jnp.sum(dgg * gated, axis=0, keepdims=True)
        dgated = dgg * ggain + 2.0 * dsq * gated
        part = mm(drows, gated * ggain, COLS_T)
        if b == 0:
            dwout_o[...] = part
        else:
            dwout_o[...] += part
        dmix = dgated * sil
        dmix_o[own, :] = dmix
        dz_o[own, :] = dgated * mx * (sg * (1.0 + zz * (1.0 - sg)))
        enter = jnp.exp(cum[own, :]) * masks[own, 3:4]
        cm = act[own, inner + STATE :]
        en = entry[b * inner : (b + 1) * inner, :]
        read = mm(cm, en, ROWS_T)
        de_o[own, :] = enter * head_sums(dmix * read, heads)
        dread = dmix * spread_heads(enter, heads, dim)
        dc_o[own, :] = mm(dread, en)
        dentry_o[b * inner : (b + 1) * inner, :] = mm(dread, cm, COLS_T)
    dgg_o[...] = jnp.broadcast_to(ggain_sum, dgg_o.shape)
    blocks = count // block
    g = dentry_o[(blocks - 1) * inner :, :]
    for b in range(blocks - 2, -1, -1):
        g = dentry_o[b * inner : (b + 1) * inner, :] + scaled_rows(g, carry[b : b + 1, :], heads)
    dstate_o[...] = g


def scan_back_kernel(heads, block, pieces, gpieces, after, dmix, act, raw, dt, cum, de, dc, dentry, entry, carry, masks, segrow, cw, hp, draw_o, ddt_o, dcw_o, dhp_o, dtot):
    count, inner = dmix.shape
    dim = inner // heads
    g = jnp.zeros((inner, STATE), jnp.float32)
    for j in range(gpieces.shape[0] - 1, -1, -1):
        later = scaled_rows(g, pieces[j, inner : inner + 1, :], heads) + gpieces[j]
        g = jnp.where(after[j : j + 1, :] > 0.5, later, g)
    lower = lower_of(block)
    lower_f = lower.astype(jnp.float32)
    sub = lax.broadcasted_iota(jnp.int32, (block, WIDE), 0)
    a_exp = jnp.exp(hp[1:2, :])
    bias_sum = alog_sum = skip_sum = jnp.zeros((1, WIDE), jnp.float32)
    for b in range(count // block - 1, -1, -1):
        at = b * block
        own = slice(at, at + block)
        values, bm, cm = act[own, :inner], act[own, inner : inner + STATE], act[own, inner + STATE :]
        shifted = dt[own, :] + hp[0:1, :]
        step = softplus(shifted)
        cm_cum = cum[own, :]
        cum_t = cm_cum.T
        allowed = lower & (masks[own, 5:6] == segrow[0:1, own])
        scores = mm(cm, bm, ROWS_T)
        last = cm_cum[block - 1 : block, :]
        leave = jnp.exp(last - cm_cum) * masks[own, 4:5]
        carry_b = carry[b : b + 1, :]
        en = entry[b * inner : (b + 1) * inner, :]
        dw = mm(bm, g, ROWS_T)
        dscores = jnp.zeros((block, block), jnp.float32)
        dxs, ws, rowsums, colsums, dcs = [], [], [], [], []
        for h in range(heads):
            cut = slice(h * dim, (h + 1) * dim)
            x = values[:, cut] * step[:, h : h + 1]
            dy = dmix[own, cut]
            spans = cm_cum[:, h : h + 1] - cum_t[h : h + 1, :]
            decays = jnp.exp(jnp.where(allowed, spans, NEG_FILL))
            s = decays * scores
            ds = mm(dy, x, ROWS_T)
            dscores = dscores + ds * decays
            dspan = ds * s
            rowsums.append(jnp.sum(dspan, axis=1, keepdims=True))
            colsums.append(jnp.sum(dspan, axis=0, keepdims=True))
            dxs.append(mm(s, dy, COLS_T) + dw[:, cut] * leave[:, h : h + 1])
            ws.append(x * leave[:, h : h + 1])
            dcs.append(jnp.sum(jnp.sum(g[cut, :] * en[cut, :], axis=1, keepdims=True), axis=0, keepdims=True))
        pad = jnp.zeros((block, WIDE - heads), jnp.float32)
        rowsum = jnp.concatenate(rowsums + [pad], axis=1)
        colsum = jnp.concatenate(colsums + [jnp.zeros((WIDE - heads, block), jnp.float32)], axis=0).T
        dcarry = jnp.concatenate(dcs + [jnp.zeros((1, WIDE - heads), jnp.float32)], axis=1)
        dx = jnp.concatenate(dxs, axis=1)
        w = jnp.concatenate(ws, axis=1)
        dleave = head_sums(dw * w, heads)
        dlast = jnp.sum(dleave, axis=0, keepdims=True) + dcarry * carry_b
        dcum = rowsum - colsum + de[own, :] - dleave + jnp.where(sub == block - 1, dlast, 0.0)
        dld = mm(lower_f, dcum, COLS_T, EXACT)
        dstep = head_sums(dx * values, heads) - dld * a_exp
        alog_sum = alog_sum - jnp.sum(dld * step, axis=0, keepdims=True) * a_exp
        ddt = dstep * sigmoid(shifted)
        ddt_o[own, :] = ddt
        bias_sum = bias_sum + jnp.sum(ddt, axis=0, keepdims=True)
        dy_all = dmix[own, :]
        skip_sum = skip_sum + jnp.sum(head_sums(dy_all * values, heads), axis=0, keepdims=True)
        dval = dx * spread_heads(step, heads, dim) + dy_all * spread_heads(hp[2:3, :], heads, dim)
        db = mm(w, g) + mm(dscores, cm, COLS_T)
        dcm = dc[own, :] + mm(dscores, bm)
        total = conv_total(raw, cw, masks, at, block)
        sg = sigmoid(total)
        dsil = sg * (1.0 + total * (1.0 - sg))
        dtot[own, :inner] = dval * dsil[:, :inner]
        dtot[own, inner : inner + STATE] = db * dsil[:, inner : inner + STATE]
        dtot[own, inner + STATE :] = dcm * dsil[:, inner + STATE :]
        g = dentry[b * inner : (b + 1) * inner, :] + scaled_rows(g, carry_b, heads)
    dhp_o[...] = jnp.concatenate([bias_sum, alog_sum, skip_sum, jnp.zeros((5, WIDE), jnp.float32)], axis=0)
    dall = dtot[...]
    draw_o[0:8, :] = jnp.zeros_like(draw_o[0:8, :])
    draw_o[8:, :] = cw[KERNEL - 1 : KERNEL, :] * dall
    dk = []
    for k in range(KERNEL - 1):
        kept = dall * masks[:, k : k + 1]
        first = 8 - (KERNEL - 1) + k
        dk.append(jnp.sum(kept * raw[first : first + count, :], axis=0, keepdims=True))
        draw_o[first : first + count, :] = draw_o[first : first + count, :] + cw[k : k + 1, :] * kept
    dk.append(jnp.sum(dall * raw[8:, :], axis=0, keepdims=True))
    dk.append(jnp.sum(dall, axis=0, keepdims=True))
    dcw_o[...] = jnp.concatenate(dk + [jnp.zeros((7 - KERNEL, dall.shape[1]), jnp.float32)], axis=0)


def front_back_kernel(layer, block, hidden, tail, gains, wz, wx, wside, dz, draw, ddt, dcw, dhp, dggain, *refs):
    *later, dh_o, dtail_o, dwz_o, dwx_o, dwside_o, small_o = refs
    count, inner = dz.shape
    width = hidden.shape[1]
    wide_bc = 2 * STATE
    gain = gains[layer : layer + 1, :]

    def back(h, dn):
        r = lax.rsqrt(jnp.mean(h * h, axis=1, keepdims=True) + EPS)
        hr = h * r
        g = dn * gain
        dgain = jnp.sum(dn * hr, axis=0, keepdims=True)
        return r * (g - hr * jnp.mean(g * hr, axis=1, keepdims=True)), dgain, hr * gain

    dr = draw[0:8, :]
    dn = mm(dr[:, :inner], wx[...], ROWS_T) + mm(dr[:, inner:], wside[:, :wide_bc], ROWS_T)
    dtail, dgain, nt = back(tail[...], dn)
    dtail_o[...] = dtail
    dwx_o[...] = mm(nt, dr[:, :inner], COLS_T)
    dwside_o[:, :wide_bc] = mm(nt, dr[:, inner:], COLS_T)
    dwside_o[:, wide_bc:] = jnp.zeros_like(dwside_o[:, wide_bc:])
    for b in range(count // block):
        at = b * block
        own = slice(at, at + block)
        dzb = dz[own, :]
        drb = draw[8 + at : 8 + at + block, :]
        side = jnp.concatenate([drb[:, inner:], ddt[own, :]], axis=1)
        dn = mm(dzb, wz[...], ROWS_T) + mm(drb[:, :inner], wx[...], ROWS_T) + mm(side, wside[...], ROWS_T)
        dh, dg, n = back(hidden[own, :], dn)
        dh_o[own, :] = dh
        dgain = dgain + dg
        part = mm(n, dzb, COLS_T)
        if b == 0:
            dwz_o[...] = part
        else:
            dwz_o[...] += part
        dwx_o[...] += mm(n, drb[:, :inner], COLS_T)
        dwside_o[...] += mm(n, side, COLS_T)
    small_o[0:8, :] = jnp.zeros((8, small_o.shape[1]), jnp.float32)
    small_o[0 : KERNEL + 1, :wide_bc] = dcw[0 : KERNEL + 1, inner:]
    small_o[0 : KERNEL + 1, wide_bc : wide_bc + inner] = dcw[0 : KERNEL + 1, :inner]
    small_o[0:3, -WIDE:] = dhp[0:3, :]
    small_o[5:6, wide_bc : wide_bc + inner] = dggain[0:1, :]
    for i in range(width // wide_bc):
        small_o[5 + i : 6 + i, :wide_bc] = dgain[:, i * wide_bc : (i + 1) * wide_bc]
    for i in range(len(later)):
        small_o[8 + 8 * i : 16 + 8 * i, :] = later[i][...]


def f32(*shape):
    return jax.ShapeDtypeStruct(shape, jnp.float32)


def kernel_call(kernel, name, outs, args, scratch=()):
    return pl.pallas_call(
        kernel,
        out_shape=outs,
        in_specs=[VM] * len(args),
        out_specs=[VM] * len(outs),
        scratch_shapes=list(scratch),
        compiler_params=pltpu.CompilerParams(vmem_limit_bytes=56 * 1024 * 1024),
        name=name,
    )(*args)


def greet(peers, axis):
    bar = pltpu.get_barrier_semaphore()
    for p in peers:
        pl.semaphore_signal(bar, inc=1, device_id={axis: p}, device_id_type=MESHID)
    pl.semaphore_wait(bar, len(peers))


def exchange_kernel(spec, *refs):
    n, seq, ats, ns, bc_loc, inner_all, step, (d1, d2, window) = spec
    ng = len(ats)
    forward = inner_all > 0
    full = bc_loc > 0
    refs = list(refs)

    def take(number):
        out = refs[:number]
        del refs[:number]
        return out

    x_ref, e_ref, base = take(3)
    gx, sx = take(ng), take(ns)
    if full:
        sidex, f_ref = take(2)
    o_ref, eo_ref = take(2)
    go, so = take(ng), take(ns)
    if forward:
        hidden_o, tail_o = take(2)
    if full:
        bco, fo_ref = take(2)
    inl, inr = take(2)
    tailgot = None if forward else take(1)[0]
    egot, mids, gots = take(1)[0], take(ns), take(ns)
    if full:
        fgot, shgot, sh, bcs, bcgot = take(5)
    sl, sr, rl, rr, es, er, el, ts, tr = take(9)
    if ng:
        gs, gr, gfs, gfr, gl = take(5)
    if ns:
        cs, cr, ss, rs = take(4)
    if full:
        fs, fr, bs, br, bl, hs, hr, hl = take(8)
    z = lax.axis_index("head")
    me, chips, core, chip, sib = seq_place(seq)
    count = x_ref.shape[0] // step
    bar = pltpu.get_barrier_semaphore()
    for k in range(1, n):
        pl.semaphore_signal(bar, inc=1, device_id={"head": lax.rem(z + k, n)}, device_id_type=MESHID)
    for k in range(1, seq):
        pl.semaphore_signal(bar, inc=1, device_id={"seq": lax.rem(me + k, seq)}, device_id_type=MESHID)
    pl.semaphore_wait(bar, n - 1 + seq - 1)

    def head_sum(src, got, dst, send, recv, near):
        own = pltpu.make_async_copy(src, got.at[z], near)
        far = [
            pltpu.make_async_remote_copy(src_ref=src, dst_ref=got.at[z], send_sem=send.at[k], recv_sem=recv.at[k],
                device_id={"head": lax.rem(z + k, n)}, device_id_type=MESHID)
            for k in range(1, n)
        ]

        def start():
            own.start()
            for copy in far:
                copy.start()

        def end():
            own.wait()
            for copy in far:
                copy.wait()
            total = got[0]
            for k in range(1, n):
                total = total + got[k]
            dst[...] = total

        return start, end

    start_extra, end_extra = head_sum(e_ref, egot, eo_ref, es, er, el)

    def tail_copy():
        if forward:
            return pltpu.make_async_remote_copy(src_ref=hidden_o.at[pl.ds(x_ref.shape[0] - 8, 8)], dst_ref=tail_o, send_sem=ts, recv_sem=tr,
                device_id={"seq": me + 1}, device_id_type=MESHID)
        return pltpu.make_async_remote_copy(src_ref=eo_ref, dst_ref=tailgot, send_sem=ts, recv_sem=tr,
            device_id={"seq": me - 1}, device_id_type=MESHID)

    def back_tail():
        end_extra()

        @pl.when(me > 0)
        def _():
            tail_copy().start()

    if full:
        start_shared, end_shared = head_sum(sh, shgot, sh, hs, hr, hl)

    def small(k):
        return pltpu.make_async_remote_copy(src_ref=f_ref, dst_ref=fgot.at[me], send_sem=fs.at[k], recv_sem=fr.at[k],
            device_id={"seq": lax.rem(me + k, seq)}, device_id_type=MESHID)

    def end_small():
        for k in range(1, seq):
            small(k).wait()
        total = fgot[0]
        for k in range(1, seq):
            total = total + fgot[k]
        fo_ref[...] = total
        sh[...] = total[:, : sh.shape[1]]
        start_shared()

    def peer(k):
        return {"seq": lax.rem(chip + k, chips) * 2 + core}

    def source(i):
        return gx[i] if ats[i] is None else gx[i].at[ats[i]]

    def g_at(i, owner):
        rows = go[i].shape[0] // seq
        return go[i].at[pl.ds(pl.multiple_of(owner * rows, 8), rows)]

    def back(k):
        return lax.rem(chip - k + chips, chips) * 2 + core

    def g_local(i):
        return pltpu.make_async_copy(source(i), g_at(i, me), gl.at[i])

    def g_across(i, k):
        return pltpu.make_async_remote_copy(src_ref=source(i), dst_ref=g_at(i, me), send_sem=gs.at[i, k], recv_sem=gr.at[i, k],
            device_id=peer(k), device_id_type=MESHID)

    def g_over(i, k):
        return pltpu.make_async_remote_copy(src_ref=source(i) if k == 0 else g_at(i, back(k)), dst_ref=g_at(i, back(k)),
            send_sem=gfs.at[i, k], recv_sem=gfr.at[i, k], device_id={"seq": sib}, device_id_type=MESHID)

    g_pairs = [(i, k) for k in range(1, chips) for i in range(ng)]

    def g_start():
        for i, k in g_pairs:
            g_across(i, k).start()
        for i in range(ng):
            g_over(i, 0).start()
            g_local(i).start()

    def g_forward():
        for i, k in g_pairs:
            g_across(i, k).wait_recv()
            g_over(i, k).start()

    def g_end():
        for i in range(ng):
            for k in range(chips):
                g_over(i, k).wait()
            g_local(i).wait()
        for i, k in g_pairs:
            g_across(i, k).wait_send()

    def block(i, k, c):
        rows = so[i].shape[0]
        return pl.ds(pl.multiple_of((lax.rem(chip + k, chips) * 2 + c) * rows, 8), rows)

    def s_over(i, k):
        return pltpu.make_async_remote_copy(src_ref=sx[i].at[block(i, k, 1 - core)], dst_ref=mids[i].at[k], send_sem=cs.at[i, k], recv_sem=cr.at[i, k],
            device_id={"seq": sib}, device_id_type=MESHID)

    def s_across(i, k):
        return pltpu.make_async_remote_copy(src_ref=mids[i].at[k], dst_ref=gots[i].at[k], send_sem=ss.at[i, k], recv_sem=rs.at[i, k],
            device_id=peer(k), device_id_type=MESHID)

    def s_start():
        for i in range(ns):
            for k in range(chips):
                s_over(i, k).start()

    def s_middle(i):
        for k in list(range(1, chips)) + [0]:
            s_over(i, k).wait_recv()
            mids[i][k] = mids[i][k] + sx[i][block(i, k, core), :]
            if k:
                s_across(i, k).start()

    def s_final(i):
        total = mids[i][0]
        for k in range(1, chips):
            s_across(i, k).wait_recv()
            total = total + gots[i][k]
        so[i][...] = total

    def s_drain():
        for i in range(ns):
            for k in range(chips):
                s_over(i, k).wait_send()
                if k:
                    s_across(i, k).wait_send()

    def b_own():
        return pltpu.make_async_copy(bcs.at[z], bcgot.at[z], bl)

    def b_across(k):
        to = lax.rem(z + k, n)
        return pltpu.make_async_remote_copy(src_ref=bcs.at[to], dst_ref=bcgot.at[z], send_sem=bs.at[k], recv_sem=br.at[k],
            device_id={"head": to}, device_id_type=MESHID)

    def b_start():
        s_final(0)
        for p in range(n):
            cut = slice(p * bc_loc, (p + 1) * bc_loc)
            bcs[p] = jnp.concatenate([so[0][:, cut], sidex[:, cut]], axis=1)
        b_own().start()
        for k in range(1, n):
            b_across(k).start()

    def b_end():
        b_own().wait()
        for k in range(1, n):
            b_across(k).wait()
        total = bcgot[0]
        for k in range(1, n):
            total = total + bcgot[k]
        bco[...] = total

    low = (n - 1) // 2
    def rows(c):
        return pl.ds(pl.multiple_of(c * step, 8), step)
    def root(c):
        return low + lax.rem(c, 2) if n % 2 == 0 else jnp.int32(low)
    def right(src, dst, c):
        return pltpu.make_async_remote_copy(src_ref=src.at[rows(c)], dst_ref=dst.at[rows(c)], send_sem=sr.at[c], recv_sem=rl.at[c],
            device_id={"head": z + 1}, device_id_type=MESHID)
    def left(src, dst, c):
        return pltpu.make_async_remote_copy(src_ref=src.at[rows(c)], dst_ref=dst.at[rows(c)], send_sem=sl.at[c], recv_sem=rr.at[c],
            device_id={"head": z - 1}, device_id_type=MESHID)
    def forward_step(c):
        r = root(c)
        @pl.when((z < r) & (z == 0))
        def _():
            right(x_ref, inl, c).start()
        @pl.when((z < r) & (z > 0))
        def _():
            right(x_ref, inl, c).wait_recv()
            inl[rows(c), :] = inl[rows(c), :] + x_ref[rows(c), :]
            right(inl, inl, c).start()
        @pl.when((z > r) & (z == n - 1))
        def _():
            left(x_ref, inr, c).start()
        @pl.when((z > r) & (z < n - 1))
        def _():
            left(x_ref, inr, c).wait_recv()
            inr[rows(c), :] = inr[rows(c), :] + x_ref[rows(c), :]
            left(inr, inr, c).start()
    def root_step(c):
        @pl.when(z == root(c))
        def _():
            @pl.when(z > 0)
            def _():
                right(x_ref, inl, c).wait_recv()
            @pl.when(z == 0)
            def _():
                inl[rows(c), :] = jnp.zeros_like(inl[rows(c), :])
            @pl.when(z < n - 1)
            def _():
                left(x_ref, inr, c).wait_recv()
            @pl.when(z == n - 1)
            def _():
                inr[rows(c), :] = jnp.zeros_like(inr[rows(c), :])
            total = x_ref[rows(c), :] + inl[rows(c), :] + inr[rows(c), :]
            o_ref[rows(c), :] = total if forward else total + base[rows(c), :]
            @pl.when(z > 0)
            def _():
                left(o_ref, o_ref, c).start()
            @pl.when(z < n - 1)
            def _():
                right(o_ref, o_ref, c).start()
    def spread_step(c):
        r = root(c)
        @pl.when((z < r) & (z > 0))
        def _():
            left(o_ref, o_ref, c).wait_recv()
            left(o_ref, o_ref, c).start()
        @pl.when((z > r) & (z < n - 1))
        def _():
            right(o_ref, o_ref, c).wait_recv()
            right(o_ref, o_ref, c).start()

    def end_step(c, carry):
        r = root(c)
        @pl.when((z < r) & (z == 0))
        def _():
            left(o_ref, o_ref, c).wait_recv()
        @pl.when((z > r) & (z == n - 1))
        def _():
            right(o_ref, o_ref, c).wait_recv()
        return carry

    def sent(c, to_right, to_left):
        @pl.when(to_right & (z < n - 1))
        def _():
            right(o_ref, o_ref, c).wait_send()
        @pl.when(to_left & (z > 0))
        def _():
            left(o_ref, o_ref, c).wait_send()
    stages = [
        (0, forward_step, lambda c: sent(c, z < root(c), z > root(c))),
        (d1, root_step, lambda c: sent(c, z == root(c), z == root(c))),
        (d2, spread_step, lambda c: sent(c, z > root(c), z < root(c))),
    ]
    planned = []
    start_extra()
    if not forward:
        planned.append((6, back_tail))
    if full:
        fgot_own = pltpu.make_async_copy(f_ref, fgot.at[me], hl)
        fgot_own.start()
        for k in range(1, seq):
            small(k).start()
        fgot_own.wait()
        planned.append((7, end_small))
    if ng:
        g_start()
        planned.append((count, g_forward))
    if ns:
        s_start()
        for i in range(ns):
            planned.append((1 + i, functools.partial(s_middle, i)))
        if full:
            planned.append((min(8, count), b_start))

    def nth(i):
        return jnp.where(z <= low, i + 1 - 2 * lax.rem(i, 2), i)

    def body(t, carry):
        for lag, step_of, sent_of in stages:
            i = t - lag
            @pl.when((i >= window) & (i < count + window))
            def _():
                sent_of(nth(i - window))
            @pl.when((i >= 0) & (i < count))
            def _():
                step_of(nth(i))
        for when, run in planned:
            pl.when(t == when)(run)
        return carry
    lax.fori_loop(0, count + d2 + window, body, 0)
    for i in range(1 if full else 0, ns):
        s_final(i)
    lax.fori_loop(0, count, end_step, 0)
    if ng:
        g_end()
    s_drain()
    if full:
        b_end()
        end_shared()
        fo_ref[:, : sh.shape[1]] = sh[...]
    if forward:
        end_extra()
        size = x_ref.shape[0]
        square = jnp.concatenate([eo_ref[...], jnp.zeros((WIDE - 8, size), jnp.float32)], axis=0).T
        hidden_o[...] = base[...] + lax.rsqrt(square[:, 0:1] / inner_all + EPS) * o_ref[...]

        @pl.when(me < seq - 1)
        def _():
            tail_copy().start()

        @pl.when(me == 0)
        def _():
            tail_o[...] = jnp.zeros_like(tail_o)

        @pl.when(me > 0)
        def _():
            tail_copy().wait_recv()

        @pl.when(me < seq - 1)
        def _():
            tail_copy().wait_send()
    else:
        @pl.when(me < seq - 1)
        def _():
            tail_copy().wait_recv()
            last = pl.ds(x_ref.shape[0] - 8, 8)
            o_ref[last, :] = o_ref[last, :] + tailgot[...]

        @pl.when(me > 0)
        def _():
            tail_copy().wait_send()


def exchange(x, e, base, cid, gathers=(), scatters=(), full=(), bc_loc=0, inner_all=0, parts=16, order=(2, 5, 3)):
    n, seq = lax.axis_size("head"), lax.axis_size("seq")
    chips = seq // 2
    ng, ns = len(gathers), len(scatters)
    outs = [(g.shape[0] // seq, g.shape[1]) for g in scatters]
    g_shapes = [g.shape[-2:] for g, _ in gathers]
    shapes = [x.shape, e.shape] + [(seq * r, c) for r, c in g_shapes] + outs
    spaces = [VM, VM] + [HB] * ng + [VM] * ns
    dma = pltpu.SemaphoreType.DMA
    vm = lambda *shape: pltpu.VMEM(shape, jnp.float32)
    scratch = [vm(*x.shape), vm(*x.shape)] + ([] if inner_all else [vm(*e.shape)]) + [vm(n, *e.shape)] + [vm(chips, *o) for o in outs] * 2
    if inner_all:
        shapes += [x.shape, (8, x.shape[1])]
        spaces += [VM] * 2
    if full:
        f, bc = full[1], (outs[0][0], 2 * bc_loc)
        shared = (f.shape[0], 2 * STATE)
        shapes += [bc, f.shape]
        spaces += [VM] * 2
        scratch += [vm(seq, *f.shape), vm(n, *shared), vm(*shared), vm(n, *bc), vm(n, *bc)]
    scratch += [dma((parts,))] * 4 + [dma((n,))] * 2 + [dma] * 3
    if ng:
        scratch += [dma((ng, chips))] * 4 + [dma((ng,))]
    if ns:
        scratch += [dma((ns, chips))] * 4
    if full:
        scratch += [dma((seq,))] * 2 + [dma((n,))] * 2 + [dma] + [dma((n,))] * 2 + [dma]
    spec = (n, seq, tuple(at for _, at in gathers), ns, bc_loc, inner_all, x.shape[0] // parts, order)
    res = pl.pallas_call(
        functools.partial(exchange_kernel, spec),
        out_shape=[f32(*s) for s in shapes],
        in_specs=[VM] * 3 + [HB] * ng + [VM] * (ns + len(full)),
        out_specs=spaces,
        scratch_shapes=scratch,
        compiler_params=pltpu.CompilerParams(collective_id=cid, has_side_effects=True, vmem_limit_bytes=56 * 1024 * 1024),
        name="exchange",
    )(x, e, base, *[g for g, _ in gathers], *scatters, *full)
    return res[0], res[1], res[2 : 2 + ng], res[2 + ng : 2 + ng + ns], res[2 + ng + ns :]


def bookkeeping(me, lengths, block, masks_o, segrow_o, cmask_o, earlier_o, later_o):
    count = masks_o.shape[0]
    base = me * count

    def segment(position):
        start = jnp.int32(0)
        total = jnp.full(position.shape, -1, jnp.int32)
        for d in range(lengths.shape[0]):
            total = total + (position >= start).astype(jnp.int32)
            start = start + lengths[d]
        return total

    row = lax.broadcasted_iota(jnp.int32, masks_o.shape, 0)
    lane = lax.broadcasted_iota(jnp.int32, masks_o.shape, 1)
    first = row - lax.rem(row, block)
    margin = KERNEL - 1
    at = jnp.where(lane < margin, row - margin + lane, jnp.where(lane == 3, first - 1, jnp.where(lane == 4, first + block - 1, row)))
    seg = segment(base + at)
    own = segment(base + row)
    masks_o[...] = jnp.where(lane < 5, (seg == own).astype(jnp.float32), own.astype(jnp.float32))
    segrow_o[...] = segment(base + lax.broadcasted_iota(jnp.int32, segrow_o.shape, 1)).astype(jnp.float32)
    first = lax.broadcasted_iota(jnp.int32, cmask_o.shape, 0) * block
    cmask_o[...] = (segment(base + first - 1) == segment(base + first + block - 1)).astype(jnp.float32)
    place = lax.broadcasted_iota(jnp.int32, earlier_o.shape, 0)
    earlier_o[...] = (place < me).astype(jnp.float32)
    later_o[...] = (place > me).astype(jnp.float32)


def opening_kernel(n, seq, block, lengths, z_ref, x_ref, bc_ref, ck_ref, cb_ref, dt_ref, h_ref, cxk, cxb, dtb, alog, skip, *refs):
    wz_o, wx_o, side_o, own_o, tail_o, hp_o, cw_o, *books = refs[:12]
    bc_got, ck_got, cb_got, side, hs, hr, hl, ss, rs, fs, fr, ls, ts, tr = refs[12:]
    layers, rows, heads = dt_ref.shape
    z = lax.axis_index("head")
    me, chips, core, chip, sib = seq_place(seq)
    count = h_ref.shape[0]
    bar = pltpu.get_barrier_semaphore()
    for k in range(1, n):
        pl.semaphore_signal(bar, inc=1, device_id={"head": lax.rem(z + k, n)}, device_id_type=MESHID)
    for k in range(1, seq):
        pl.semaphore_signal(bar, inc=1, device_id={"seq": lax.rem(me + k, seq)}, device_id_type=MESHID)
    pl.semaphore_wait(bar, n - 1 + seq - 1)
    columns = [(bc_ref, bc_got), (ck_ref, ck_got), (cb_ref, cb_got)]

    def own(i):
        return pltpu.make_async_copy(columns[i][0], columns[i][1].at[z], hl.at[i])

    def head(i, k):
        return pltpu.make_async_remote_copy(src_ref=columns[i][0], dst_ref=columns[i][1].at[z], send_sem=hs.at[i, k], recv_sem=hr.at[i, k],
            device_id={"head": lax.rem(z + k, n)}, device_id_type=MESHID)

    srcs = [z_ref.at[0], x_ref.at[0], side]
    dsts = [wz_o, wx_o, side_o]
    number = len(srcs)

    def at(i, owner):
        return dsts[i].at[pl.ds(pl.multiple_of(owner * rows, 8), rows)]

    def back(k):
        return lax.rem(chip - k + chips, chips) * 2 + core

    def local(i):
        return pltpu.make_async_copy(srcs[i], at(i, me), ls.at[i])

    def across(i, k):
        return pltpu.make_async_remote_copy(src_ref=srcs[i], dst_ref=at(i, me), send_sem=ss.at[i, k], recv_sem=rs.at[i, k],
            device_id={"seq": lax.rem(chip + k, chips) * 2 + core}, device_id_type=MESHID)

    def over(i, k):
        return pltpu.make_async_remote_copy(src_ref=srcs[i] if k == 0 else at(i, back(k)), dst_ref=at(i, back(k)), send_sem=fs.at[i, k], recv_sem=fr.at[i, k],
            device_id={"seq": sib}, device_id_type=MESHID)

    def tail():
        return pltpu.make_async_remote_copy(src_ref=h_ref.at[pl.ds(count - 8, 8)], dst_ref=tail_o, send_sem=ts, recv_sem=tr,
            device_id={"seq": me + 1}, device_id_type=MESHID)

    def send(i):
        for k in range(1, chips):
            across(i, k).start()
        over(i, 0).start()
        local(i).start()

    for i in range(3):
        for k in range(1, n):
            head(i, k).start()
        own(i).start()

    @pl.when(me < seq - 1)
    def _():
        tail().start()

    @pl.when(me == 0)
    def _():
        tail_o[...] = jnp.zeros_like(tail_o)

    send(0)
    send(1)
    for i in range(3):
        own(i).wait()
        for k in range(1, n):
            head(i, k).wait()
    pad = jnp.zeros((rows, WIDE - heads), jnp.float32)
    for l in range(layers):
        whole = jnp.concatenate([bc_got[p, l] for p in range(n)] + [dt_ref[l], pad], axis=1)
        if l == 0:
            side[...] = whole
            send(2)
        else:
            own_o[(l - 1) * rows : l * rows, :] = whole
    inner = cxb.shape[1]
    for l in range(layers):
        taps = jnp.concatenate([cxk[l]] + [ck_got[p, l] for p in range(n)], axis=1)
        bias = jnp.concatenate([cxb[l : l + 1, :]] + [cb_got[p, l : l + 1, :] for p in range(n)], axis=1)
        cw_o[8 * l : 8 * l + 8, :] = jnp.concatenate([taps, bias, jnp.zeros((7 - KERNEL, inner + 2 * STATE), jnp.float32)], axis=0)
        heads_of = jnp.concatenate([dtb[l : l + 1, :], alog[l : l + 1, :], skip[l : l + 1, :], jnp.zeros((5, heads), jnp.float32)], axis=0)
        hp_o[8 * l : 8 * l + 8, :] = jnp.concatenate([heads_of, jnp.zeros((8, WIDE - heads), jnp.float32)], axis=1)
    bookkeeping(me, lengths, block, *books)
    pairs = [(i, k) for i in range(number) for k in range(1, chips)]
    for i, k in pairs:
        across(i, k).wait_recv()
        over(i, k).start()
    for i in range(number):
        for k in range(chips):
            over(i, k).wait()
        local(i).wait()
    for i, k in pairs:
        across(i, k).wait_send()

    @pl.when(me > 0)
    def _():
        tail().wait_recv()

    @pl.when(me < seq - 1)
    def _():
        tail().wait_send()


def opening(lengths, proj_z, proj_x, proj_bc, ck, cb, proj_dt, hidden, cxk, cxb, dtb, alog, skip, cid):
    n, seq = lax.axis_size("head"), lax.axis_size("seq")
    layers, rows, inner = proj_z.shape
    chips = seq // 2
    count, width = hidden.shape
    side = 2 * STATE + WIDE
    full = rows * seq
    dma = pltpu.SemaphoreType.DMA
    smem = pl.BlockSpec(memory_space=pltpu.SMEM)
    return pl.pallas_call(
        functools.partial(opening_kernel, n, seq, min(BLOCK, count)),
        out_shape=[f32(full, inner), f32(full, inner), f32(full, side), f32((layers - 1) * rows, side), f32(8, width),
                   f32(8 * layers, WIDE), f32(8 * layers, inner + 2 * STATE), f32(count, 8), f32(8, count), f32(8, WIDE), f32(seq, WIDE), f32(seq, WIDE)],
        in_specs=[smem, HB, HB, HB, HB, HB, VM, HB] + [VM] * 5,
        out_specs=[HB, HB, HB] + [VM] * 9,
        scratch_shapes=[pltpu.VMEM((n,) + a.shape, jnp.float32) for a in (proj_bc, ck, cb)] + [pltpu.VMEM((rows, side), jnp.float32)]
        + [dma((3, n))] * 2 + [dma((3,))] + [dma((3, chips))] * 4 + [dma((3,)), dma, dma],
        compiler_params=pltpu.CompilerParams(collective_id=cid, has_side_effects=True),
        name="opening",
    )(lengths, proj_z, proj_x, proj_bc, ck, cb, proj_dt, hidden, cxk, cxb, dtb, alog, skip)


def finish_kernel(n, e, bcs, hidden, half0, half1, grad, *refs):
    z = lax.axis_index("head")
    big = refs[:8]
    (hidden_o, grad_o, ngain_o, z_o, x_o, bc_o, dt_o, cxk_o, cxb_o, cbk_o, cbb_o, dtb_o, alog_o, skip_o, ggain_o, out_o) = refs[8:]
    half = half0.shape[0]
    hidden_o[0:half, :] = hidden[0:half, :] + half0[...]
    hidden_o[half:, :] = hidden[half:, :] + half1[...]
    grad_o[...] = grad[...]
    inner, heads, bc_loc = z_o.shape[2], dt_o.shape[2], bc_o.shape[2]
    bc = 2 * STATE
    for l in range(2):
        side, gz, gx, gout = big[4 * l : 4 * l + 4]
        z_o[l], x_o[l], out_o[l] = gz[...], gx[...], gout[...]
        bc_o[l] = bcs[:, l * bc_loc : (l + 1) * bc_loc]
        dt_o[l] = side[:, bc : bc + heads]
        s = e[8 * l : 8 * l + 8, :]
        for i in range(ngain_o.shape[1] // bc):
            ngain_o[l : l + 1, i * bc : (i + 1) * bc] = s[5 + i : 6 + i, :bc]
        cxk_o[l] = s[0:KERNEL, bc : bc + inner]
        cxb_o[l : l + 1, :] = s[KERNEL : KERNEL + 1, bc : bc + inner]
        ggain_o[l : l + 1, :] = s[5:6, bc : bc + inner]
        mine = jnp.zeros((8, bc_loc), jnp.float32)
        for p in range(n):
            mine = jnp.where(z == p, s[:, p * bc_loc : (p + 1) * bc_loc], mine)
        cbk_o[l] = mine[0:KERNEL]
        cbb_o[l : l + 1, :] = mine[KERNEL : KERNEL + 1]
        last = s[:, -WIDE:]
        dtb_o[l : l + 1, :] = last[0:1, :heads]
        alog_o[l : l + 1, :] = last[1:2, :heads]
        skip_o[l : l + 1, :] = last[2:3, :heads]


def seq_place(n):
    me = lax.axis_index("seq")
    chips = n // 2
    core, chip = lax.rem(me, 2), me // 2
    return me, chips, core, chip, me + 1 - 2 * core


def seq_greet(chips, core, chip, sib):
    bar = pltpu.get_barrier_semaphore()
    pl.semaphore_signal(bar, inc=1, device_id={"seq": sib}, device_id_type=MESHID)
    for k in range(1, chips):
        pl.semaphore_signal(bar, inc=1, device_id={"seq": lax.rem(chip + k, chips) * 2 + core}, device_id_type=MESHID)
    pl.semaphore_wait(bar, chips)


def gather_kernel(n, number, *refs):
    xs, os, (ss, rs, fs, fr, ls) = refs[:number], refs[number : 2 * number], refs[2 * number :]
    me, chips, core, chip, sib = seq_place(n)
    seq_greet(chips, core, chip, sib)

    def at(i, owner):
        rows = xs[i].shape[0]
        return os[i].at[pl.ds(pl.multiple_of(owner * rows, 8), rows)]

    def back(k):
        return lax.rem(chip - k + chips, chips) * 2 + core

    def local(i):
        return pltpu.make_async_copy(xs[i], at(i, me), ls.at[i])

    def across(i, k):
        return pltpu.make_async_remote_copy(src_ref=xs[i], dst_ref=at(i, me), send_sem=ss.at[i, k], recv_sem=rs.at[i, k],
            device_id={"seq": lax.rem(chip + k, chips) * 2 + core}, device_id_type=MESHID)

    def over(i, k):
        return pltpu.make_async_remote_copy(src_ref=xs[i] if k == 0 else at(i, back(k)), dst_ref=at(i, back(k)), send_sem=fs.at[i, k], recv_sem=fr.at[i, k],
            device_id={"seq": sib}, device_id_type=MESHID)

    pairs = [(i, k) for k in range(1, chips) for i in range(number)]
    for i, k in pairs:
        across(i, k).start()
    for i in range(number):
        over(i, 0).start()
        local(i).start()
    for i, k in pairs:
        across(i, k).wait_recv()
        over(i, k).start()
    for i in range(number):
        for k in range(chips):
            over(i, k).wait_recv()
    for i, k in pairs:
        across(i, k).wait_send()
    for i in range(number):
        for k in range(chips):
            over(i, k).wait_send()
        local(i).wait()


def seq_gather(xs, cid, spec=None):
    n = lax.axis_size("seq")
    number = len(xs)
    spec = spec or HB
    return pl.pallas_call(
        functools.partial(gather_kernel, n, number),
        out_shape=[f32(n * x.shape[0], x.shape[1]) for x in xs],
        in_specs=[spec] * number,
        out_specs=[spec] * number,
        scratch_shapes=[pltpu.SemaphoreType.DMA((number, n // 2))] * 4 + [pltpu.SemaphoreType.DMA((number,))],
        compiler_params=pltpu.CompilerParams(collective_id=cid, has_side_effects=True),
        name="seq_gather",
    )(*xs)


def direct_sum_kernel(n, axis, scatter, x_ref, o_ref, got, ss, rs, ls):
    me = lax.axis_index(axis)
    greet([lax.rem(me + k, n) for k in range(1, n)], axis)

    def piece(owner):
        return x_ref.at[owner] if scatter else x_ref

    local = pltpu.make_async_copy(piece(me), got.at[me], ls)

    def across(k):
        peer = lax.rem(me + k, n)
        return pltpu.make_async_remote_copy(src_ref=piece(peer), dst_ref=got.at[me], send_sem=ss.at[k], recv_sem=rs.at[k],
            device_id={axis: peer}, device_id_type=MESHID)

    for k in range(1, n):
        across(k).start()
    local.start()
    for k in range(1, n):
        across(k).wait()
    local.wait()
    total = got[0]
    for k in range(1, n):
        total = total + got[k]
    o_ref[...] = total


def direct_sum(x, axis, cid, scatter=False):
    n = lax.axis_size(axis)
    shape = x.shape[1:] if scatter else x.shape
    return pl.pallas_call(
        functools.partial(direct_sum_kernel, n, axis, scatter),
        out_shape=f32(*shape),
        in_specs=[VM],
        out_specs=VM,
        scratch_shapes=[pltpu.VMEM((n,) + shape, x.dtype)] + [pltpu.SemaphoreType.DMA((n,))] * 2 + [pltpu.SemaphoreType.DMA],
        compiler_params=pltpu.CompilerParams(collective_id=cid, has_side_effects=True),
        name="direct_sum_" + axis,
    )(x)


def body(
    hidden_in, grad_out, doc_lengths, norm_gain, proj_z, proj_x, proj_bc, proj_dt, conv_x_kernel, conv_x_bias,
    conv_bc_kernel, conv_bc_bias, dt_bias, a_log, skip_gain, gate_gain, proj_out,
):
    count, width = hidden_in.shape
    layers, rows_loc, inner = proj_z.shape
    bc_loc = proj_bc.shape[2]
    heads = proj_dt.shape[2]
    n_seq, n_head = lax.axis_size("seq"), lax.axis_size("head")
    inner_all = inner * n_head
    bc_all = 2 * STATE
    block = min(BLOCK, count)
    blocks = count // block
    mine = lax.axis_index("seq")

    (wz0, wx0, side0, side_own, tail, hp, cw, masks, segrow, cmask, earlier, following) = opening(
        doc_lengths, proj_z, proj_x, proj_bc, conv_bc_kernel, conv_bc_bias, proj_dt, hidden_in,
        conv_x_kernel, conv_x_bias, dt_bias, a_log, skip_gain, 2,
    )
    wz, wx, wside, wout = [wz0], [wx0], [side0], [lax.all_gather(proj_out[0], "seq", axis=0, tiled=True)]
    cws = [cw[8 * l : 8 * l + 8] for l in range(layers)]
    hps = [hp[8 * l : 8 * l + 8] for l in range(layers)]

    hidden = hidden_in
    saved = []
    sums = None
    for l in range(layers):
        z, raw, dt, act, cum, y, st, carry, dev = kernel_call(
            functools.partial(front_kernel, l, heads, block), "front",
            [f32(count, inner), f32(count + 8, inner + bc_all), f32(count, WIDE), f32(count, inner + bc_all), f32(count, WIDE),
             f32(count, inner), f32(blocks * inner, STATE), f32(8, WIDE), f32(inner + 8, STATE)],
            [hidden, tail, norm_gain, wz[l], wx[l], wside[l], cws[l], hps[l], masks, segrow, cmask],
        )
        [pieces] = seq_gather([dev], 10 + 10 * l)
        pieces = pieces.reshape(n_seq, inner + 8, STATE)
        final = l == layers - 1
        rows, e, mixed, entry = kernel_call(
            functools.partial(mix_kernel, l, heads, block, final), "mix",
            [f32(count, width), f32(8, count), f32(count, inner), f32(blocks * inner, STATE)],
            [pieces, earlier, y, act, cum, masks, st, carry, z, gate_gain, wout[l], grad_out],
        )
        hidden_l, tail_l = hidden, tail
        if final:
            e = direct_sum(e, "head", 11 + 10 * l)
            sums = rows
        else:
            sums, e, weights, _, (hidden, tail) = exchange(
                rows, e, hidden, 11 + 10 * l, inner_all=inner_all,
                gathers=[(proj_z, l + 1), (proj_x, l + 1), (proj_out, l + 1), (side_own[l * rows_loc : (l + 1) * rows_loc], None)],
            )
            for held, new in zip((wz, wx, wout, wside), weights):
                held.append(new)
        saved.append((hidden_l, tail_l, z, raw, dt, act, cum, carry, pieces, mixed, entry, e, sums))

    grad = grad_out
    big = [None] * layers
    small, out_parts = [], []
    half = count // 2
    for l in reversed(range(layers)):
        final = l == layers - 1
        hidden_l, tail, z, raw, dt, act, cum, carry, pieces, mixed, entry, e, sums = saved[l]
        dmix, dz, de, dc, dentry, dstate, dwout, dggain, *scaled = kernel_call(
            functools.partial(gate_back_kernel, l, heads, block, inner_all, final), "gate_back",
            [f32(count, inner), f32(count, inner), f32(count, WIDE), f32(count, STATE), f32(blocks * inner, STATE), f32(inner, STATE),
             f32(width, inner), f32(8, inner)] + [f32(half, width)] * (2 if final else 0),
            [grad, e, sums, act, cum, masks, carry, z, gate_gain, wout[l], mixed, entry],
        )
        [gpieces] = seq_gather([dstate], 12 + 10 * l)
        if final:
            scaled_rows_of = scaled
            out_parts.append(lax.psum(scaled[0], "head"))
        draw, ddt, dcw, dhp = kernel_call(
            functools.partial(scan_back_kernel, heads, block), "scan_back",
            [f32(count + 8, inner + bc_all), f32(count, WIDE), f32(8, inner + bc_all), f32(8, WIDE)],
            [pieces, gpieces.reshape(n_seq, inner, STATE), following, dmix, act, raw, dt, cum, de, dc, dentry, entry, carry, masks, segrow, cws[l], hps[l]],
            [pltpu.VMEM((count, inner + bc_all), jnp.float32)],
        )
        part, dtail, dwz, dwx, dwside, smalls = kernel_call(
            functools.partial(front_back_kernel, l, block), "front_back",
            [f32(count, width), f32(8, width), f32(width, inner), f32(width, inner), f32(width, bc_all + WIDE),
             f32(8 * (layers - l), max(width, bc_all + inner + WIDE))],
            [hidden_l, tail, norm_gain, wz[l], wx[l], wside[l], dz, draw, ddt, dcw, dhp, dggain] + small,
        )
        small = [smalls]
        part, out_parts = lax.optimization_barrier((part, out_parts))
        grads = [dwside, dwz, dwx, dwout]
        if l > 0:
            grad, _, _, big[l], _ = exchange(part, dtail, grad, 14 + 10 * l, scatters=grads)
            late, grad = lax.optimization_barrier((scaled_rows_of[1], grad))
            out_parts.append(lax.psum(late, "head"))
        else:
            grad, _, _, big[l], (bcs, e) = exchange(part, dtail, grad, 14, scatters=grads, full=(big[1][0], smalls), bc_loc=bc_loc)
    outs = [
        (count, width), (count, width), (layers, width), proj_z.shape, proj_x.shape, proj_bc.shape, proj_dt.shape, conv_x_kernel.shape,
        conv_x_bias.shape, conv_bc_kernel.shape, conv_bc_bias.shape, dt_bias.shape, a_log.shape, skip_gain.shape, gate_gain.shape, proj_out.shape,
    ]
    return tuple(
        kernel_call(
            functools.partial(finish_kernel, n_head), "finish", [f32(*o) for o in outs],
            [e, bcs, hidden, *out_parts, grad, *big[0], *big[1]],
        )
    )


def solution(mesh):
    in_specs = (
        P("seq", None),
        P("seq", None),
        P(),
        P(),
        P(None, "seq", "head"),
        P(None, "seq", "head"),
        P(None, "seq", "head"),
        P(None, "seq", "head"),
        P(None, None, "head"),
        P(None, "head"),
        P(None, None, "head"),
        P(None, "head"),
        P(None, "head"),
        P(None, "head"),
        P(None, "head"),
        P(None, "head"),
        P(None, "seq", "head"),
    )
    out_specs = (
        P("seq", None),
        P("seq", None),
        P(),
        P(None, "seq", "head"),
        P(None, "seq", "head"),
        P(None, "seq", "head"),
        P(None, "seq", "head"),
        P(None, None, "head"),
        P(None, "head"),
        P(None, None, "head"),
        P(None, "head"),
        P(None, "head"),
        P(None, "head"),
        P(None, "head"),
        P(None, "head"),
        P(None, "seq", "head"),
    )
    return jax.shard_map(body, mesh=mesh, in_specs=in_specs, out_specs=out_specs, check_vma=False)
```

```python
import functools

import jax
import jax.numpy as jnp
from jax import lax
from jax.experimental import pallas as pl
from jax.experimental.pallas import tpu as pltpu
from jax.sharding import PartitionSpec as P

STATE = 128
KERNEL = 4
BLOCK = 256
MESHID = pl.DeviceIdType.MESH
VM = pl.BlockSpec(memory_space=pltpu.VMEM)
HB = pl.BlockSpec(memory_space=pl.ANY)


EPS = 1e-05
NEG_FILL = -1e30
EXACT = lax.Precision.HIGHEST
FAST = lax.Precision.HIGH
WIDE = 128


def mm(left, right, dims=((1,), (0,)), precision=FAST):
    return lax.dot_general(left, right, (dims, ((), ())), precision=precision, preferred_element_type=jnp.float32)


ROWS_T = ((1,), (1,))
COLS_T = ((0,), (0,))


def sigmoid(v):
    return 1.0 / (1.0 + jnp.exp(-v))


def softplus(v):
    small = jnp.exp(-jnp.abs(v))
    one = 1.0 + small
    exact = jnp.where(one == 1.0, small, small * jnp.log(one) / jnp.where(one == 1.0, 1.0, one - 1.0))
    return jnp.maximum(v, 0.0) + exact


def spread_heads(per_head, heads, dim):
    rows = per_head.shape[0]
    return jnp.concatenate([jnp.broadcast_to(per_head[:, h : h + 1], (rows, dim)) for h in range(heads)], axis=1)


def scaled_rows(state, factors, heads):
    dim = state.shape[0] // heads
    return jnp.concatenate([state[h * dim : (h + 1) * dim] * factors[:, h : h + 1] for h in range(heads)], axis=0)


def head_sums(wide, heads):
    width = wide.shape[1]
    dim = width // heads
    row = lax.broadcasted_iota(jnp.int32, (width, WIDE), 0)
    col = lax.broadcasted_iota(jnp.int32, (width, WIDE), 1)
    pick = ((row >= col * dim) & (row < (col + 1) * dim)).astype(jnp.float32)
    return mm(wide, pick, precision=EXACT)


def lower_of(rows):
    return lax.broadcasted_iota(jnp.int32, (rows, rows), 0) >= lax.broadcasted_iota(jnp.int32, (rows, rows), 1)


def normed_of(h, gain):
    r = lax.rsqrt(jnp.mean(h * h, axis=1, keepdims=True) + EPS)
    return h * r * gain


def conv_total(raw_ref, cw_ref, masks_ref, at, rows):
    total = cw_ref[KERNEL : KERNEL + 1, :] + cw_ref[KERNEL - 1 : KERNEL, :] * raw_ref[8 + at : 8 + at + rows, :]
    for k in range(KERNEL - 1):
        first = 8 + at - (KERNEL - 1) + k
        total = total + cw_ref[k : k + 1, :] * (raw_ref[first : first + rows, :] * masks_ref[at : at + rows, k : k + 1])
    return total


def gather_ops(place, src, slot, sems):
    me, chips, core, chip, sib = place
    ss, rs, fs, fr, ls = sems

    def back(k):
        return lax.rem(chip - k + chips, chips) * 2 + core

    def across(k):
        return pltpu.make_async_remote_copy(src_ref=src, dst_ref=slot(me), send_sem=ss.at[k], recv_sem=rs.at[k],
            device_id={"seq": lax.rem(chip + k, chips) * 2 + core}, device_id_type=MESHID)

    def over(k):
        return pltpu.make_async_remote_copy(src_ref=src if k == 0 else slot(back(k)), dst_ref=slot(back(k)), send_sem=fs.at[k], recv_sem=fr.at[k],
            device_id={"seq": sib}, device_id_type=MESHID)

    local = pltpu.make_async_copy(src, slot(me), ls)

    def start():
        for k in range(1, chips):
            across(k).start()
        over(0).start()
        local.start()

    def forward():
        for k in range(1, chips):
            across(k).wait_recv()
            over(k).start()

    def end():
        for k in range(chips):
            over(k).wait()
        for k in range(1, chips):
            across(k).wait_send()
        local.wait()

    return start, forward, end


def gather_sems(chips):
    return [pltpu.SemaphoreType.DMA((chips,))] * 4 + [pltpu.SemaphoreType.DMA]


def signal_peers(place, heads):
    me, chips, core, chip, sib = place
    bar = pltpu.get_barrier_semaphore()
    pl.semaphore_signal(bar, inc=1, device_id={"seq": sib}, device_id_type=MESHID)
    for k in range(1, chips):
        pl.semaphore_signal(bar, inc=1, device_id={"seq": lax.rem(chip + k, chips) * 2 + core}, device_id_type=MESHID)
    if heads:
        z = lax.axis_index("head")
        for k in range(1, heads):
            pl.semaphore_signal(bar, inc=1, device_id={"head": lax.rem(z + k, heads)}, device_id_type=MESHID)
        return chips + heads - 1
    return chips


def forward_kernel(layer, heads, block, last_layer, n_seq, hidden, tail, gains, wz, wx, wside, cw, hp, masks, segrow, cmask, before, ggains, wout_in, grad, *refs):
    refs = list(refs)
    z_o, raw_o, dt_o, act_o, cum_o, carry_o, decays_o, e_o, mixed_o, entry_o, *rows_o = refs[: 12 if last_layer else 11]
    first = layer == 0
    refs = refs[12 if last_layer else 11 :]
    wout = refs.pop(0) if first else wout_in
    nrm, lv, st, y, dev, pieces = refs[:6]
    refs = refs[6:]
    place = seq_place(n_seq)
    expected = signal_peers(place, 0)
    start, forward, end = gather_ops(place, dev, lambda owner: pieces.at[owner], refs[:5])
    if first:
        rows_loc = wout_in.shape[1]
        w_start, w_forward, w_end = gather_ops(
            place, wout_in.at[0], lambda owner: wout.at[pl.ds(pl.multiple_of(owner * rows_loc, 8), rows_loc)], refs[5:10]
        )
    count, inner = z_o.shape
    blocks = count // block
    dim = inner // heads
    wide_bc = 2 * STATE
    gain = gains[layer : layer + 1, :]
    ggain = ggains[layer : layer + 1, :]
    if first:
        pl.semaphore_wait(pltpu.get_barrier_semaphore(), expected)
        w_start()
    t = normed_of(tail[...], gain)
    raw_o[0:8, :inner] = mm(t, wx[...])
    raw_o[0:8, inner:] = mm(t, wside[:, :wide_bc])
    lower = lower_of(block)
    lower_f = lower.astype(jnp.float32)
    carry_o[...] = jnp.zeros_like(carry_o)
    state = decay = None

    def step_of(own):
        return softplus(dt_o[own, :] + hp[0:1, :])

    for b in range(blocks):
        at = b * block
        own = slice(at, at + block)
        n = normed_of(hidden[own, :], gain)
        nrm[own, :] = n
        raw_o[8 + at : 8 + at + block, :inner] = mm(n, wx[...])
        side = mm(n, wside[...])
        raw_o[8 + at : 8 + at + block, inner:] = side[:, :wide_bc]
        dt_o[own, :] = side[:, wide_bc:]
        total = conv_total(raw_o, cw, masks, at, block)
        act = total * sigmoid(total)
        act_o[own, :] = act
        step = step_of(own)
        cum = mm(lower_f, -step * jnp.exp(hp[1:2, :]), precision=EXACT)
        cum_o[own, :] = cum
        last = cum[block - 1 : block, :]
        leave = step * jnp.exp(last - cum) * masks[own, 4:5]
        states = mm(act[:, :inner] * spread_heads(leave, heads, dim), act[:, inner : inner + STATE], COLS_T)
        st[b * inner : (b + 1) * inner, :] = states
        carry = jnp.exp(last) * cmask[b : b + 1, :]
        carry_o[b : b + 1, :] = carry
        state = states if b == 0 else scaled_rows(state, carry, heads) + states
        decay = carry if b == 0 else decay * carry
    dev[:inner, :] = state
    dev[inner:, :] = jnp.broadcast_to(decay, (8, WIDE))
    if first:
        w_forward()
    else:
        pl.semaphore_wait(pltpu.get_barrier_semaphore(), expected)
    start()
    for b in range(blocks):
        at = b * block
        own = slice(at, at + block)
        z = mm(nrm[own, :], wz[...])
        z_o[own, :] = z
        lv[own, :] = z * sigmoid(z)
        values, bm, cm = act_o[own, :inner], act_o[own, inner : inner + STATE], act_o[own, inner + STATE :]
        step, cum = step_of(own), cum_o[own, :]
        cum_t = cum.T
        allowed = lower & (masks[own, 5:6] == segrow[0:1, own])
        scores = mm(cm, bm, ROWS_T)
        ys = []
        for h in range(heads):
            v = values[:, h * dim : (h + 1) * dim]
            spans = cum[:, h : h + 1] - cum_t[h : h + 1, :]
            s = jnp.exp(jnp.where(allowed, spans, NEG_FILL)) * scores
            ys.append(mm(s, v * step[:, h : h + 1]) + hp[2:3, h : h + 1] * v)
        y[own, :] = jnp.concatenate(ys, axis=1)
    forward()
    if first:
        w_end()
    end()
    state = jnp.zeros((inner, STATE), jnp.float32)
    for j in range(n_seq):
        decay = pieces[j, inner : inner + 1, :]
        decays_o[j : j + 1, :] = decay
        later = scaled_rows(state, decay, heads) + pieces[j, :inner, :]
        state = jnp.where(before[j : j + 1, :] > 0.5, later, state)
    for b in range(blocks):
        at = b * block
        own = slice(at, at + block)
        entry_o[b * inner : (b + 1) * inner, :] = state
        enter = jnp.exp(cum_o[own, :]) * masks[own, 3:4]
        mixed = y[own, :] + spread_heads(enter, heads, dim) * mm(act_o[own, inner + STATE :], state, ROWS_T)
        mixed_o[own, :] = mixed
        gated = mixed * lv[own, :]
        out = mm(gated * ggain, wout[...], ROWS_T)
        done = 0
        for part in rows_o:
            low, high = max(at, done), min(at + block, done + part.shape[0])
            if low < high:
                part[low - done : high - done, :] = out[low - at : high - at]
            done = done + part.shape[0]
        squares = jnp.sum(gated * gated, axis=1, keepdims=True)
        if last_layer:
            dots = jnp.sum(grad[own, :] * out, axis=1, keepdims=True)
        else:
            dots = jnp.zeros_like(squares)
        lane = lax.broadcasted_iota(jnp.int32, (block, WIDE), 1)
        both = jnp.where(lane == 0, squares, jnp.where(lane == 1, dots, 0.0))
        e_o[:, own] = both.T[0:8, :]
        state = scaled_rows(state, carry_o[b : b + 1, :], heads) + st[b * inner : (b + 1) * inner, :]


def backward_kernel(layer, heads, block, inner_all, last_layer, n_seq, n_head, grad, e, sums, act, cum, masks, carry, z, ggains, wout, mixed, entry, decays, after, raw, dt, segrow, cw, hp, *refs):
    refs = list(refs)
    dz_o, draw_o, ddt_o, dcw_o, dhp_o, dwout_o, dgg_o = refs[:7]
    refs = refs[7:]
    if last_layer:
        esum = refs.pop(0)
    wide, dmix, de, dc, dentry, dstate, gpieces, dtot, dxi, dbi = refs[:10]
    refs = refs[10:]
    place = seq_place(n_seq)
    expected = signal_peers(place, n_head if last_layer else 0)
    start, forward, end = gather_ops(place, dstate, lambda owner: gpieces.at[owner], refs[:5])
    if last_layer:
        egot, es, er, el = refs[5:9]
        zi = lax.axis_index("head")
        near = pltpu.make_async_copy(e, egot.at[zi], el)
        far = [
            pltpu.make_async_remote_copy(src_ref=e, dst_ref=egot.at[zi], send_sem=es.at[k], recv_sem=er.at[k],
                device_id={"head": lax.rem(zi + k, n_head)}, device_id_type=MESHID)
            for k in range(1, n_head)
        ]
        pl.semaphore_wait(pltpu.get_barrier_semaphore(), expected)
        near.start()
        for copy in far:
            copy.start()
    count, inner = z.shape
    blocks = count // block
    dim = inner // heads
    ggain = ggains[layer : layer + 1, :]
    for b in range(blocks):
        own = slice(b * block, (b + 1) * block)
        wide[own, :] = mm(grad[own, :], wout[...])
    if last_layer:
        near.wait()
        for copy in far:
            copy.wait()
        total = egot[0]
        for k in range(1, n_head):
            total = total + egot[k]
        esum[...] = total
        e = esum

    def columns(own):
        return jnp.concatenate([e[:, own], jnp.zeros((WIDE - 8, block), jnp.float32)], axis=0).T

    def enter_of(own):
        return spread_heads(jnp.exp(cum[own, :]) * masks[own, 3:4], heads, dim)

    ggain_sum = jnp.zeros((1, inner), jnp.float32)
    for b in range(blocks):
        own = slice(b * block, (b + 1) * block)
        et = columns(own)
        scale = lax.rsqrt(et[:, 0:1] / inner_all + EPS)
        gs = et[:, 1:2] if last_layer else jnp.sum(grad[own, :] * sums[own, :], axis=1, keepdims=True)
        dsq = gs * (-0.5 / inner_all) * scale * scale * scale
        dgg = scale * wide[own, :]
        zz = z[own, :]
        sg = sigmoid(zz)
        sil = zz * sg
        mx = mixed[own, :]
        gated = mx * sil
        ggain_sum = ggain_sum + jnp.sum(dgg * gated, axis=0, keepdims=True)
        dgated = dgg * ggain + 2.0 * dsq * gated
        dm = dgated * sil
        dmix[own, :] = dm
        dz_o[own, :] = dgated * mx * (sg * (1.0 + zz * (1.0 - sg)))
        wide[own, :] = scale * (gated * ggain)
        dentry[b * inner : (b + 1) * inner, :] = mm(dm * enter_of(own), act[own, inner + STATE :], COLS_T)
    dgg_o[...] = jnp.broadcast_to(ggain_sum, dgg_o.shape)
    g = dentry[(blocks - 1) * inner :, :]
    for b in range(blocks - 2, -1, -1):
        g = dentry[b * inner : (b + 1) * inner, :] + scaled_rows(g, carry[b : b + 1, :], heads)
    dstate[...] = g
    if not last_layer:
        pl.semaphore_wait(pltpu.get_barrier_semaphore(), expected)
    start()
    lower = lower_of(block)
    lower_f = lower.astype(jnp.float32)
    pad = jnp.zeros((block, WIDE - heads), jnp.float32)
    for b in range(blocks):
        at = b * block
        own = slice(at, at + block)
        part = mm(grad[own, :], wide[own, :], COLS_T)
        if b == 0:
            dwout_o[...] = part
        else:
            dwout_o[...] += part
        values, bm, cm = act[own, :inner], act[own, inner : inner + STATE], act[own, inner + STATE :]
        en = entry[b * inner : (b + 1) * inner, :]
        dread = dmix[own, :] * enter_of(own)
        step = softplus(dt[own, :] + hp[0:1, :])
        cum_b = cum[own, :]
        cum_t = cum_b.T
        allowed = lower & (masks[own, 5:6] == segrow[0:1, own])
        scores = mm(cm, bm, ROWS_T)
        dscores = jnp.zeros((block, block), jnp.float32)
        dxs, rowsums, colsums = [], [], []
        for h in range(heads):
            cut = slice(h * dim, (h + 1) * dim)
            x = values[:, cut] * step[:, h : h + 1]
            dy = dmix[own, cut]
            spans = cum_b[:, h : h + 1] - cum_t[h : h + 1, :]
            decay = jnp.exp(jnp.where(allowed, spans, NEG_FILL))
            s = decay * scores
            ds = mm(dy, x, ROWS_T)
            dscores = dscores + ds * decay
            dspan = ds * s
            rowsums.append(jnp.sum(dspan, axis=1, keepdims=True))
            colsums.append(jnp.sum(dspan, axis=0, keepdims=True))
            dxs.append(mm(s, dy, COLS_T))
        rowsum = jnp.concatenate(rowsums + [pad], axis=1)
        colsum = jnp.concatenate(colsums + [jnp.zeros((WIDE - heads, block), jnp.float32)], axis=0).T
        de[own, :] = head_sums(dread * mm(cm, en, ROWS_T), heads) + rowsum - colsum
        dxi[own, :] = jnp.concatenate(dxs, axis=1)
        dc[own, :] = mm(dread, en) + mm(dscores, bm)
        dbi[own, :] = mm(dscores, cm, COLS_T)
        if b == 0:
            forward()
    end()
    g = jnp.zeros((inner, STATE), jnp.float32)
    for j in range(n_seq - 1, -1, -1):
        later = scaled_rows(g, decays[j : j + 1, :], heads) + gpieces[j]
        g = jnp.where(after[j : j + 1, :] > 0.5, later, g)
    sub = lax.broadcasted_iota(jnp.int32, (block, WIDE), 0)
    a_exp = jnp.exp(hp[1:2, :])
    bias_sum = alog_sum = skip_sum = jnp.zeros((1, WIDE), jnp.float32)
    for b in range(blocks - 1, -1, -1):
        at = b * block
        own = slice(at, at + block)
        values, bm = act[own, :inner], act[own, inner : inner + STATE]
        shifted = dt[own, :] + hp[0:1, :]
        step = softplus(shifted)
        step_wide = spread_heads(step, heads, dim)
        cum_b = cum[own, :]
        last = cum_b[block - 1 : block, :]
        leave = spread_heads(jnp.exp(last - cum_b) * masks[own, 4:5], heads, dim)
        carry_b = carry[b : b + 1, :]
        ge = g * entry[b * inner : (b + 1) * inner, :]
        dcs = [jnp.sum(jnp.sum(ge[h * dim : (h + 1) * dim], axis=0, keepdims=True), axis=1, keepdims=True) for h in range(heads)]
        dcarry = jnp.concatenate(dcs + [jnp.zeros((1, WIDE - heads), jnp.float32)], axis=1)
        dw = mm(bm, g, ROWS_T) * leave
        dx = dxi[own, :] + dw
        x = values * step_wide
        dleave = head_sums(dw * x, heads)
        dlast = jnp.sum(dleave, axis=0, keepdims=True) + dcarry * carry_b
        dcum = de[own, :] - dleave + jnp.where(sub == block - 1, dlast, 0.0)
        dld = mm(lower_f, dcum, COLS_T, EXACT)
        ddt = (head_sums(dx * values, heads) - dld * a_exp) * sigmoid(shifted)
        alog_sum = alog_sum - jnp.sum(dld * step, axis=0, keepdims=True) * a_exp
        ddt_o[own, :] = ddt
        bias_sum = bias_sum + jnp.sum(ddt, axis=0, keepdims=True)
        dy = dmix[own, :]
        skip_sum = skip_sum + jnp.sum(head_sums(dy * values, heads), axis=0, keepdims=True)
        total = conv_total(raw, cw, masks, at, block)
        sg = sigmoid(total)
        dsil = sg * (1.0 + total * (1.0 - sg))
        dtot[own, :inner] = (dx * step_wide + dy * spread_heads(hp[2:3, :], heads, dim)) * dsil[:, :inner]
        dtot[own, inner : inner + STATE] = (dbi[own, :] + mm(x * leave, g)) * dsil[:, inner : inner + STATE]
        dtot[own, inner + STATE :] = dc[own, :] * dsil[:, inner + STATE :]
        g = dentry[b * inner : (b + 1) * inner, :] + scaled_rows(g, carry_b, heads)
    dhp_o[...] = jnp.concatenate([bias_sum, alog_sum, skip_sum, jnp.zeros((5, WIDE), jnp.float32)], axis=0)
    conv_back(dtot, raw, masks, cw, draw_o, dcw_o)


def conv_back(dtot, raw, masks, cw, draw_o, dcw_o):
    count = dtot.shape[0]
    dall = dtot[...]
    draw_o[0:8, :] = jnp.zeros_like(draw_o[0:8, :])
    draw_o[8:, :] = cw[KERNEL - 1 : KERNEL, :] * dall
    dk = []
    for k in range(KERNEL - 1):
        kept = dall * masks[:, k : k + 1]
        first = 8 - (KERNEL - 1) + k
        dk.append(jnp.sum(kept * raw[first : first + count, :], axis=0, keepdims=True))
        draw_o[first : first + count, :] = draw_o[first : first + count, :] + cw[k : k + 1, :] * kept
    dk.append(jnp.sum(dall * raw[8:, :], axis=0, keepdims=True))
    dk.append(jnp.sum(dall, axis=0, keepdims=True))
    dcw_o[...] = jnp.concatenate(dk + [jnp.zeros((7 - KERNEL, dall.shape[1]), jnp.float32)], axis=0)


def f32(*shape):
    return jax.ShapeDtypeStruct(shape, jnp.float32)


def kernel_call(kernel, name, outs, args, scratch=(), cid=None, specs=None, out_specs=None):
    params = {} if cid is None else dict(collective_id=cid, has_side_effects=True)
    return pl.pallas_call(
        kernel,
        out_shape=outs,
        in_specs=specs or [VM] * len(args),
        out_specs=out_specs or [VM] * len(outs),
        scratch_shapes=list(scratch),
        cost_estimate=pl.CostEstimate(flops=1, bytes_accessed=1, transcendentals=0),
        compiler_params=pltpu.CompilerParams(vmem_limit_bytes=56 * 1024 * 1024, **params),
        name=name,
    )(*args)


def greet(peers, axis):
    bar = pltpu.get_barrier_semaphore()
    for p in peers:
        pl.semaphore_signal(bar, inc=1, device_id={axis: p}, device_id_type=MESHID)
    pl.semaphore_wait(bar, len(peers))


def exchange_kernel(spec, *refs):
    n, seq, ats, ns, bc_loc, inner_all, step, (d1, d2, window), (layer, block) = spec
    ng = len(ats)
    forward = inner_all > 0
    full = bc_loc > 0
    refs = list(refs)

    def take(number):
        out = refs[:number]
        del refs[:number]
        return out

    if forward:
        x_ref, e_ref, base = take(3)
    else:
        hidden, tail, gains, wz, wx, wside, dz, draw, ddt, dcw, dhp, dggain, dwout, base = take(14)
    gx = take(ng)
    if full:
        sidex, earlier = take(2)
    o_ref = take(1)[0]
    if forward:
        eo_ref = take(1)[0]
    go, so = take(ng), take(ns)
    if forward:
        hidden_o, tail_o = take(2)
    elif full:
        bco, fo_ref = take(2)
    else:
        f_ref = take(1)[0]
    inl, inr = take(2)
    if not forward:
        x_ref, nrm, e_ref, eo_ref, tailgot, dwside, dwz, dwx = take(8)
        sx = [dwside, dwz, dwx, dwout]
    if full:
        f_ref = take(1)[0]
    egot, mids, gots = take(1)[0], take(ns), take(ns)
    if full:
        fgot, shgot, sh, bcs, bcgot = take(5)
    sl, sr, rl, rr, es, er, el, ts, tr = take(9)
    if ng:
        gs, gr, gfs, gfr, gl = take(5)
    if ns:
        cs, cr, ss, rs = take(4)
    if full:
        fs, fr, bs, br, bl, hs, hr, hl = take(8)
    z = lax.axis_index("head")
    me, chips, core, chip, sib = seq_place(seq)
    count = x_ref.shape[0] // step
    bar = pltpu.get_barrier_semaphore()
    for k in range(1, n):
        pl.semaphore_signal(bar, inc=1, device_id={"head": lax.rem(z + k, n)}, device_id_type=MESHID)
    for k in range(1, seq):
        pl.semaphore_signal(bar, inc=1, device_id={"seq": lax.rem(me + k, seq)}, device_id_type=MESHID)
    planned = []
    if not forward:
        inner = dz.shape[1]
        wide_bc = 2 * STATE
        gain = gains[layer : layer + 1, :]

        def back_norm(h, dn):
            r = lax.rsqrt(jnp.mean(h * h, axis=1, keepdims=True) + EPS)
            hr = h * r
            g = dn * gain
            return r * (g - hr * jnp.mean(g * hr, axis=1, keepdims=True)), jnp.sum(dn * hr, axis=0, keepdims=True), hr * gain

        dr = draw[0:8, :]
        dn = mm(dr[:, :inner], wx[...], ROWS_T) + mm(dr[:, inner:], wside[:, :wide_bc], ROWS_T)
        e_ref[...], dgain, nrm[0:8, :] = back_norm(tail[...], dn)
        tokens = dz.shape[0]
        cuts = [slice(b * block, (b + 1) * block) for b in range(tokens // block)]
        shifted_cuts = [slice(8 + c.start, 8 + c.stop) for c in cuts]

        def side_of(c, d):
            return jnp.concatenate([draw[d, inner:], ddt[c, :]], axis=1)

        for c, d in zip(cuts, shifted_cuts):
            dn = mm(dz[c, :], wz[...], ROWS_T) + mm(draw[d, :inner], wx[...], ROWS_T) + mm(side_of(c, d), wside[...], ROWS_T)
            x_ref[c, :], dg, nrm[d, :] = back_norm(hidden[c, :], dn)
            dgain = dgain + dg
        f_ref[0:8, :] = jnp.zeros((8, f_ref.shape[1]), jnp.float32)
        f_ref[0 : KERNEL + 1, :wide_bc] = dcw[0 : KERNEL + 1, inner:]
        f_ref[0 : KERNEL + 1, wide_bc : wide_bc + inner] = dcw[0 : KERNEL + 1, :inner]
        f_ref[0:3, -WIDE:] = dhp[0:3, :]
        f_ref[5:6, wide_bc : wide_bc + inner] = dggain[0:1, :]
        for i in range(hidden.shape[1] // wide_bc):
            f_ref[5 + i : 6 + i, :wide_bc] = dgain[:, i * wide_bc : (i + 1) * wide_bc]
        if full:
            f_ref[8:, :] = earlier[...]

        def side_grads():
            dwside[:, :wide_bc] = mm(nrm[0:8, :], draw[0:8, inner:], COLS_T)
            dwside[:, wide_bc:] = jnp.zeros_like(dwside[:, wide_bc:])
            for c, d in zip(cuts, shifted_cuts):
                dwside[...] += mm(nrm[d, :], side_of(c, d), COLS_T)
            s_start(0)

        def z_grads():
            dwz[...] = mm(nrm[8:, :], dz[...], COLS_T)
            s_start(1)

        def x_grads():
            dwx[...] = mm(nrm[0:8, :], draw[0:8, :inner], COLS_T) + mm(nrm[8:, :], draw[8:, :inner], COLS_T)
            s_start(2)

        planned = [(1, side_grads), (3, z_grads), (5, x_grads)]
    pl.semaphore_wait(bar, n - 1 + seq - 1)

    def head_sum(src, got, dst, send, recv, near):
        own = pltpu.make_async_copy(src, got.at[z], near)
        far = [
            pltpu.make_async_remote_copy(src_ref=src, dst_ref=got.at[z], send_sem=send.at[k], recv_sem=recv.at[k],
                device_id={"head": lax.rem(z + k, n)}, device_id_type=MESHID)
            for k in range(1, n)
        ]

        def start():
            own.start()
            for copy in far:
                copy.start()

        def end():
            own.wait()
            for copy in far:
                copy.wait()
            total = got[0]
            for k in range(1, n):
                total = total + got[k]
            dst[...] = total

        return start, end

    start_extra, end_extra = head_sum(e_ref, egot, eo_ref, es, er, el)

    def tail_copy():
        if forward:
            return pltpu.make_async_remote_copy(src_ref=hidden_o.at[pl.ds(x_ref.shape[0] - 8, 8)], dst_ref=tail_o, send_sem=ts, recv_sem=tr,
                device_id={"seq": me + 1}, device_id_type=MESHID)
        return pltpu.make_async_remote_copy(src_ref=eo_ref, dst_ref=tailgot, send_sem=ts, recv_sem=tr,
            device_id={"seq": me - 1}, device_id_type=MESHID)

    def back_tail():
        end_extra()

        @pl.when(me > 0)
        def _():
            tail_copy().start()

    if full:
        start_shared, end_shared = head_sum(sh, shgot, sh, hs, hr, hl)

    def small(k):
        return pltpu.make_async_remote_copy(src_ref=f_ref, dst_ref=fgot.at[me], send_sem=fs.at[k], recv_sem=fr.at[k],
            device_id={"seq": lax.rem(me + k, seq)}, device_id_type=MESHID)

    def end_small():
        for k in range(1, seq):
            small(k).wait()
        total = fgot[0]
        for k in range(1, seq):
            total = total + fgot[k]
        fo_ref[...] = total
        sh[...] = total[:, : sh.shape[1]]
        start_shared()

    def peer(k):
        return {"seq": lax.rem(chip + k, chips) * 2 + core}

    def source(i):
        return gx[i] if ats[i] is None else gx[i].at[ats[i]]

    def g_at(i, owner):
        rows = go[i].shape[0] // seq
        return go[i].at[pl.ds(pl.multiple_of(owner * rows, 8), rows)]

    def back(k):
        return lax.rem(chip - k + chips, chips) * 2 + core

    def g_local(i):
        return pltpu.make_async_copy(source(i), g_at(i, me), gl.at[i])

    def g_across(i, k):
        return pltpu.make_async_remote_copy(src_ref=source(i), dst_ref=g_at(i, me), send_sem=gs.at[i, k], recv_sem=gr.at[i, k],
            device_id=peer(k), device_id_type=MESHID)

    def g_over(i, k):
        return pltpu.make_async_remote_copy(src_ref=source(i) if k == 0 else g_at(i, back(k)), dst_ref=g_at(i, back(k)),
            send_sem=gfs.at[i, k], recv_sem=gfr.at[i, k], device_id={"seq": sib}, device_id_type=MESHID)

    g_pairs = [(i, k) for k in range(1, chips) for i in range(ng)]

    def g_start():
        for i, k in g_pairs:
            g_across(i, k).start()
        for i in range(ng):
            g_over(i, 0).start()
            g_local(i).start()

    def g_forward():
        for i, k in g_pairs:
            g_across(i, k).wait_recv()
            g_over(i, k).start()

    def g_end():
        for i in range(ng):
            for k in range(chips):
                g_over(i, k).wait()
            g_local(i).wait()
        for i, k in g_pairs:
            g_across(i, k).wait_send()

    def block(i, k, c):
        rows = so[i].shape[0]
        return pl.ds(pl.multiple_of((lax.rem(chip + k, chips) * 2 + c) * rows, 8), rows)

    def s_over(i, k):
        return pltpu.make_async_remote_copy(src_ref=sx[i].at[block(i, k, 1 - core)], dst_ref=mids[i].at[k], send_sem=cs.at[i, k], recv_sem=cr.at[i, k],
            device_id={"seq": sib}, device_id_type=MESHID)

    def s_across(i, k):
        return pltpu.make_async_remote_copy(src_ref=mids[i].at[k], dst_ref=gots[i].at[k], send_sem=ss.at[i, k], recv_sem=rs.at[i, k],
            device_id=peer(k), device_id_type=MESHID)

    def s_start(i):
        for k in range(chips):
            s_over(i, k).start()

    def s_middle(i):
        for k in list(range(1, chips)) + [0]:
            s_over(i, k).wait_recv()
            mids[i][k] = mids[i][k] + sx[i][block(i, k, core), :]
            if k:
                s_across(i, k).start()

    def s_final(i):
        total = mids[i][0]
        for k in range(1, chips):
            s_across(i, k).wait_recv()
            total = total + gots[i][k]
        so[i][...] = total

    def s_drain():
        for i in range(ns):
            for k in range(chips):
                s_over(i, k).wait_send()
                if k:
                    s_across(i, k).wait_send()

    def b_own():
        return pltpu.make_async_copy(bcs.at[z], bcgot.at[z], bl)

    def b_across(k):
        to = lax.rem(z + k, n)
        return pltpu.make_async_remote_copy(src_ref=bcs.at[to], dst_ref=bcgot.at[z], send_sem=bs.at[k], recv_sem=br.at[k],
            device_id={"head": to}, device_id_type=MESHID)

    def b_start():
        s_final(0)
        for p in range(n):
            cut = slice(p * bc_loc, (p + 1) * bc_loc)
            bcs[p] = jnp.concatenate([so[0][:, cut], sidex[:, cut]], axis=1)
        b_own().start()
        for k in range(1, n):
            b_across(k).start()

    def b_end():
        b_own().wait()
        for k in range(1, n):
            b_across(k).wait()
        total = bcgot[0]
        for k in range(1, n):
            total = total + bcgot[k]
        bco[...] = total

    low = (n - 1) // 2
    def rows(c):
        return pl.ds(pl.multiple_of(c * step, 8), step)
    def root(c):
        return low + lax.rem(c, 2) if n % 2 == 0 else jnp.int32(low)
    def right(src, dst, c):
        return pltpu.make_async_remote_copy(src_ref=src.at[rows(c)], dst_ref=dst.at[rows(c)], send_sem=sr.at[c], recv_sem=rl.at[c],
            device_id={"head": z + 1}, device_id_type=MESHID)
    def left(src, dst, c):
        return pltpu.make_async_remote_copy(src_ref=src.at[rows(c)], dst_ref=dst.at[rows(c)], send_sem=sl.at[c], recv_sem=rr.at[c],
            device_id={"head": z - 1}, device_id_type=MESHID)
    def forward_step(c):
        r = root(c)
        @pl.when((z < r) & (z == 0))
        def _():
            right(x_ref, inl, c).start()
        @pl.when((z < r) & (z > 0))
        def _():
            right(x_ref, inl, c).wait_recv()
            inl[rows(c), :] = inl[rows(c), :] + x_ref[rows(c), :]
            right(inl, inl, c).start()
        @pl.when((z > r) & (z == n - 1))
        def _():
            left(x_ref, inr, c).start()
        @pl.when((z > r) & (z < n - 1))
        def _():
            left(x_ref, inr, c).wait_recv()
            inr[rows(c), :] = inr[rows(c), :] + x_ref[rows(c), :]
            left(inr, inr, c).start()
    def root_step(c):
        @pl.when(z == root(c))
        def _():
            @pl.when(z > 0)
            def _():
                right(x_ref, inl, c).wait_recv()
            @pl.when(z == 0)
            def _():
                inl[rows(c), :] = jnp.zeros_like(inl[rows(c), :])
            @pl.when(z < n - 1)
            def _():
                left(x_ref, inr, c).wait_recv()
            @pl.when(z == n - 1)
            def _():
                inr[rows(c), :] = jnp.zeros_like(inr[rows(c), :])
            total = x_ref[rows(c), :] + inl[rows(c), :] + inr[rows(c), :]
            o_ref[rows(c), :] = total if forward else total + base[rows(c), :]
            @pl.when(z > 0)
            def _():
                left(o_ref, o_ref, c).start()
            @pl.when(z < n - 1)
            def _():
                right(o_ref, o_ref, c).start()
    def spread_step(c):
        r = root(c)
        @pl.when((z < r) & (z > 0))
        def _():
            left(o_ref, o_ref, c).wait_recv()
            left(o_ref, o_ref, c).start()
        @pl.when((z > r) & (z < n - 1))
        def _():
            right(o_ref, o_ref, c).wait_recv()
            right(o_ref, o_ref, c).start()

    def end_step(c, carry):
        r = root(c)
        @pl.when((z < r) & (z == 0))
        def _():
            left(o_ref, o_ref, c).wait_recv()
        @pl.when((z > r) & (z == n - 1))
        def _():
            right(o_ref, o_ref, c).wait_recv()
        return carry

    def sent(c, to_right, to_left):
        @pl.when(to_right & (z < n - 1))
        def _():
            right(o_ref, o_ref, c).wait_send()
        @pl.when(to_left & (z > 0))
        def _():
            left(o_ref, o_ref, c).wait_send()
    stages = [
        (0, forward_step, lambda c: sent(c, z < root(c), z > root(c))),
        (d1, root_step, lambda c: sent(c, z == root(c), z == root(c))),
        (d2, spread_step, lambda c: sent(c, z > root(c), z < root(c))),
    ]
    start_extra()
    if not forward:
        planned.append((6, back_tail))
    if full:
        fgot_own = pltpu.make_async_copy(f_ref, fgot.at[me], hl)
        fgot_own.start()
        for k in range(1, seq):
            small(k).start()
        fgot_own.wait()
        planned.append((7, end_small))
    if ng:
        g_start()
        planned.append((count, g_forward))
    if ns:
        s_start(3)
        for i, when in ((3, 2), (0, 3), (1, 5), (2, 7)):
            planned.append((when, functools.partial(s_middle, i)))
        if full:
            planned.append((min(13, count), b_start))

    def nth(i):
        return jnp.where(z <= low, i + 1 - 2 * lax.rem(i, 2), i)

    def body(t, carry):
        for lag, step_of, sent_of in stages:
            i = t - lag
            @pl.when((i >= window) & (i < count + window))
            def _():
                sent_of(nth(i - window))
            @pl.when((i >= 0) & (i < count))
            def _():
                step_of(nth(i))
        for when, run in planned:
            pl.when(t == when)(run)
        return carry
    lax.fori_loop(0, count + d2 + window, body, 0)
    for i in range(1 if full else 0, ns):
        s_final(i)
    lax.fori_loop(0, count, end_step, 0)
    if ng:
        g_end()
    s_drain()
    if full:
        b_end()
        end_shared()
        fo_ref[:, : sh.shape[1]] = sh[...]
    if forward:
        end_extra()
        size = x_ref.shape[0]
        square = jnp.concatenate([eo_ref[...], jnp.zeros((WIDE - 8, size), jnp.float32)], axis=0).T
        hidden_o[...] = base[...] + lax.rsqrt(square[:, 0:1] / inner_all + EPS) * o_ref[...]

        @pl.when(me < seq - 1)
        def _():
            tail_copy().start()

        @pl.when(me == 0)
        def _():
            tail_o[...] = jnp.zeros_like(tail_o)

        @pl.when(me > 0)
        def _():
            tail_copy().wait_recv()

        @pl.when(me < seq - 1)
        def _():
            tail_copy().wait_send()
    else:
        @pl.when(me < seq - 1)
        def _():
            tail_copy().wait_recv()
            last = pl.ds(x_ref.shape[0] - 8, 8)
            o_ref[last, :] = o_ref[last, :] + tailgot[...]

        @pl.when(me > 0)
        def _():
            tail_copy().wait_send()


def exchange(ins, cid, gathers=(), full=(), bc_loc=0, inner_all=0, layer=0, parts=16, order=(2, 5, 3)):
    n, seq = lax.axis_size("head"), lax.axis_size("seq")
    chips = seq // 2
    back = not inner_all
    ng, ns = len(gathers), 4 if back else 0
    base = ins[-1]
    rows, width = base.shape
    e_shape = (8, width) if back else ins[1].shape
    g_shapes = [g.shape[-2:] for g, _ in gathers]
    vm = lambda *shape: pltpu.VMEM(shape, jnp.float32)
    dma = pltpu.SemaphoreType.DMA
    scratch = [vm(rows, width)] * 2
    outs = []
    if back:
        inner, side = ins[6].shape[1], ins[5].shape[1]
        outs = [(width // seq, side)] + [(width // seq, inner)] * 3
        small = (full[1].shape[0] + 8 if full else 8, max(width, side + inner))
        shapes = [(rows, width)] + outs + ([(outs[0][0], 2 * bc_loc), small] if full else [small])
        spaces = [VM] * len(shapes)
        scratch += [vm(rows, width), vm(rows + 8, width), vm(8, width), vm(8, width), vm(8, width), vm(width, side), vm(width, inner), vm(width, inner)]
        if full:
            scratch += [vm(*small)]
    else:
        shapes = [(rows, width), e_shape] + [(seq * r, c) for r, c in g_shapes] + [(rows, width), (8, width)]
        spaces = [VM] * 2 + [HB] * ng + [VM] * 2
    scratch += [vm(n, *e_shape)] + [vm(chips, *o) for o in outs] * 2
    if full:
        shared, bc = (small[0], 2 * STATE), (outs[0][0], 2 * bc_loc)
        scratch += [vm(seq, *small), vm(n, *shared), vm(*shared), vm(n, *bc), vm(n, *bc)]
    scratch += [dma((parts,))] * 4 + [dma((n,))] * 2 + [dma] * 3
    if ng:
        scratch += [dma((ng, chips))] * 4 + [dma((ng,))]
    if ns:
        scratch += [dma((ns, chips))] * 4
    if full:
        scratch += [dma((seq,))] * 2 + [dma((n,))] * 2 + [dma] + [dma((n,))] * 2 + [dma]
    spec = (n, seq, tuple(at for _, at in gathers), ns, bc_loc, inner_all, rows // parts, order, (layer, min(BLOCK, rows)))
    return kernel_call(
        functools.partial(exchange_kernel, spec), "exchange", [f32(*s) for s in shapes],
        [*ins, *[g for g, _ in gathers], *full], scratch, cid=cid,
        specs=[VM] * len(ins) + [HB] * ng + [VM] * len(full), out_specs=spaces,
    )


def bookkeeping(me, lengths, block, masks_o, segrow_o, cmask_o, earlier_o, later_o):
    count = masks_o.shape[0]
    base = me * count

    def segment(position):
        start = jnp.int32(0)
        total = jnp.full(position.shape, -1, jnp.int32)
        for d in range(lengths.shape[0]):
            total = total + (position >= start).astype(jnp.int32)
            start = start + lengths[d]
        return total

    row = lax.broadcasted_iota(jnp.int32, masks_o.shape, 0)
    lane = lax.broadcasted_iota(jnp.int32, masks_o.shape, 1)
    first = row - lax.rem(row, block)
    margin = KERNEL - 1
    at = jnp.where(lane < margin, row - margin + lane, jnp.where(lane == 3, first - 1, jnp.where(lane == 4, first + block - 1, row)))
    seg = segment(base + at)
    own = segment(base + row)
    masks_o[...] = jnp.where(lane < 5, (seg == own).astype(jnp.float32), own.astype(jnp.float32))
    segrow_o[...] = segment(base + lax.broadcasted_iota(jnp.int32, segrow_o.shape, 1)).astype(jnp.float32)
    first = lax.broadcasted_iota(jnp.int32, cmask_o.shape, 0) * block
    cmask_o[...] = (segment(base + first - 1) == segment(base + first + block - 1)).astype(jnp.float32)
    place = lax.broadcasted_iota(jnp.int32, earlier_o.shape, 0)
    earlier_o[...] = (place < me).astype(jnp.float32)
    later_o[...] = (place > me).astype(jnp.float32)


def opening_kernel(n, seq, block, lengths, z_ref, x_ref, bc_ref, ck_ref, cb_ref, dt_ref, h_ref, cxk, cxb, dtb, alog, skip, *refs):
    wz_o, wx_o, side_o, own_o, tail_o, hp_o, cw_o, *books = refs[:12]
    bc_got, ck_got, cb_got, side, hs, hr, hl, ss, rs, fs, fr, ls, ts, tr = refs[12:]
    layers, rows, heads = dt_ref.shape
    z = lax.axis_index("head")
    me, chips, core, chip, sib = seq_place(seq)
    count = h_ref.shape[0]
    bar = pltpu.get_barrier_semaphore()
    for k in range(1, n):
        pl.semaphore_signal(bar, inc=1, device_id={"head": lax.rem(z + k, n)}, device_id_type=MESHID)
    for k in range(1, seq):
        pl.semaphore_signal(bar, inc=1, device_id={"seq": lax.rem(me + k, seq)}, device_id_type=MESHID)
    pl.semaphore_wait(bar, n - 1 + seq - 1)
    columns = [(bc_ref, bc_got), (ck_ref, ck_got), (cb_ref, cb_got)]

    def own(i):
        return pltpu.make_async_copy(columns[i][0], columns[i][1].at[z], hl.at[i])

    def head(i, k):
        return pltpu.make_async_remote_copy(src_ref=columns[i][0], dst_ref=columns[i][1].at[z], send_sem=hs.at[i, k], recv_sem=hr.at[i, k],
            device_id={"head": lax.rem(z + k, n)}, device_id_type=MESHID)

    srcs = [z_ref.at[0], x_ref.at[0], side]
    dsts = [wz_o, wx_o, side_o]
    number = len(srcs)

    def at(i, owner):
        return dsts[i].at[pl.ds(pl.multiple_of(owner * rows, 8), rows)]

    def back(k):
        return lax.rem(chip - k + chips, chips) * 2 + core

    def local(i):
        return pltpu.make_async_copy(srcs[i], at(i, me), ls.at[i])

    def across(i, k):
        return pltpu.make_async_remote_copy(src_ref=srcs[i], dst_ref=at(i, me), send_sem=ss.at[i, k], recv_sem=rs.at[i, k],
            device_id={"seq": lax.rem(chip + k, chips) * 2 + core}, device_id_type=MESHID)

    def over(i, k):
        return pltpu.make_async_remote_copy(src_ref=srcs[i] if k == 0 else at(i, back(k)), dst_ref=at(i, back(k)), send_sem=fs.at[i, k], recv_sem=fr.at[i, k],
            device_id={"seq": sib}, device_id_type=MESHID)

    def tail():
        return pltpu.make_async_remote_copy(src_ref=h_ref.at[pl.ds(count - 8, 8)], dst_ref=tail_o, send_sem=ts, recv_sem=tr,
            device_id={"seq": me + 1}, device_id_type=MESHID)

    def send(i):
        for k in range(1, chips):
            across(i, k).start()
        over(i, 0).start()
        local(i).start()

    for i in range(3):
        for k in range(1, n):
            head(i, k).start()
        own(i).start()

    @pl.when(me < seq - 1)
    def _():
        tail().start()

    @pl.when(me == 0)
    def _():
        tail_o[...] = jnp.zeros_like(tail_o)

    send(0)
    send(1)
    for i in range(3):
        own(i).wait()
        for k in range(1, n):
            head(i, k).wait()
    pad = jnp.zeros((rows, WIDE - heads), jnp.float32)
    for l in range(layers):
        whole = jnp.concatenate([bc_got[p, l] for p in range(n)] + [dt_ref[l], pad], axis=1)
        if l == 0:
            side[...] = whole
            send(2)
        else:
            own_o[(l - 1) * rows : l * rows, :] = whole
    inner = cxb.shape[1]
    for l in range(layers):
        taps = jnp.concatenate([cxk[l]] + [ck_got[p, l] for p in range(n)], axis=1)
        bias = jnp.concatenate([cxb[l : l + 1, :]] + [cb_got[p, l : l + 1, :] for p in range(n)], axis=1)
        cw_o[8 * l : 8 * l + 8, :] = jnp.concatenate([taps, bias, jnp.zeros((7 - KERNEL, inner + 2 * STATE), jnp.float32)], axis=0)
        heads_of = jnp.concatenate([dtb[l : l + 1, :], alog[l : l + 1, :], skip[l : l + 1, :], jnp.zeros((5, heads), jnp.float32)], axis=0)
        hp_o[8 * l : 8 * l + 8, :] = jnp.concatenate([heads_of, jnp.zeros((8, WIDE - heads), jnp.float32)], axis=1)
    bookkeeping(me, lengths, block, *books)
    pairs = [(i, k) for i in range(number) for k in range(1, chips)]
    for i, k in pairs:
        across(i, k).wait_recv()
        over(i, k).start()
    for i in range(number):
        for k in range(chips):
            over(i, k).wait()
        local(i).wait()
    for i, k in pairs:
        across(i, k).wait_send()

    @pl.when(me > 0)
    def _():
        tail().wait_recv()

    @pl.when(me < seq - 1)
    def _():
        tail().wait_send()


def opening(lengths, proj_z, proj_x, proj_bc, ck, cb, proj_dt, hidden, cxk, cxb, dtb, alog, skip, cid):
    n, seq = lax.axis_size("head"), lax.axis_size("seq")
    layers, rows, inner = proj_z.shape
    chips = seq // 2
    count, width = hidden.shape
    side = 2 * STATE + WIDE
    full = rows * seq
    dma = pltpu.SemaphoreType.DMA
    smem = pl.BlockSpec(memory_space=pltpu.SMEM)
    return pl.pallas_call(
        functools.partial(opening_kernel, n, seq, min(BLOCK, count)),
        out_shape=[f32(full, inner), f32(full, inner), f32(full, side), f32((layers - 1) * rows, side), f32(8, width),
                   f32(8 * layers, WIDE), f32(8 * layers, inner + 2 * STATE), f32(count, 8), f32(8, count), f32(8, WIDE), f32(seq, WIDE), f32(seq, WIDE)],
        in_specs=[smem, HB, HB, HB, HB, HB, VM, HB] + [VM] * 5,
        out_specs=[HB, HB, HB] + [VM] * 9,
        scratch_shapes=[pltpu.VMEM((n,) + a.shape, jnp.float32) for a in (proj_bc, ck, cb)] + [pltpu.VMEM((rows, side), jnp.float32)]
        + [dma((3, n))] * 2 + [dma((3,))] + [dma((3, chips))] * 4 + [dma((3,)), dma, dma],
        compiler_params=pltpu.CompilerParams(collective_id=cid, has_side_effects=True),
        name="opening",
    )(lengths, proj_z, proj_x, proj_bc, ck, cb, proj_dt, hidden, cxk, cxb, dtb, alog, skip)


def finish_kernel(n, inner_all, e, bcs, squares, hidden, half0, half1, grad, *refs):
    z = lax.axis_index("head")
    big = refs[:8]
    (hidden_o, grad_o, ngain_o, z_o, x_o, bc_o, dt_o, cxk_o, cxb_o, cbk_o, cbb_o, dtb_o, alog_o, skip_o, ggain_o, out_o) = refs[8:]
    half = half0.shape[0]
    size = hidden.shape[0]
    turned = jnp.concatenate([squares[...], jnp.zeros((WIDE - 8, size), jnp.float32)], axis=0).T
    scale = lax.rsqrt(turned[:, 0:1] / inner_all + EPS)
    hidden_o[0:half, :] = hidden[0:half, :] + scale[0:half] * half0[...]
    hidden_o[half:, :] = hidden[half:, :] + scale[half:] * half1[...]
    grad_o[...] = grad[...]
    inner, heads, bc_loc = z_o.shape[2], dt_o.shape[2], bc_o.shape[2]
    bc = 2 * STATE
    for l in range(2):
        side, gz, gx, gout = big[4 * l : 4 * l + 4]
        z_o[l], x_o[l], out_o[l] = gz[...], gx[...], gout[...]
        bc_o[l] = bcs[:, l * bc_loc : (l + 1) * bc_loc]
        dt_o[l] = side[:, bc : bc + heads]
        s = e[8 * l : 8 * l + 8, :]
        for i in range(ngain_o.shape[1] // bc):
            ngain_o[l : l + 1, i * bc : (i + 1) * bc] = s[5 + i : 6 + i, :bc]
        cxk_o[l] = s[0:KERNEL, bc : bc + inner]
        cxb_o[l : l + 1, :] = s[KERNEL : KERNEL + 1, bc : bc + inner]
        ggain_o[l : l + 1, :] = s[5:6, bc : bc + inner]
        mine = jnp.zeros((8, bc_loc), jnp.float32)
        for p in range(n):
            mine = jnp.where(z == p, s[:, p * bc_loc : (p + 1) * bc_loc], mine)
        cbk_o[l] = mine[0:KERNEL]
        cbb_o[l : l + 1, :] = mine[KERNEL : KERNEL + 1]
        last = s[:, -WIDE:]
        dtb_o[l : l + 1, :] = last[0:1, :heads]
        alog_o[l : l + 1, :] = last[1:2, :heads]
        skip_o[l : l + 1, :] = last[2:3, :heads]


def seq_place(n):
    me = lax.axis_index("seq")
    chips = n // 2
    core, chip = lax.rem(me, 2), me // 2
    return me, chips, core, chip, me + 1 - 2 * core


def body(
    hidden_in, grad_out, doc_lengths, norm_gain, proj_z, proj_x, proj_bc, proj_dt, conv_x_kernel, conv_x_bias,
    conv_bc_kernel, conv_bc_bias, dt_bias, a_log, skip_gain, gate_gain, proj_out,
):
    count, width = hidden_in.shape
    layers, rows_loc, inner = proj_z.shape
    bc_loc = proj_bc.shape[2]
    heads = proj_dt.shape[2]
    n_seq, n_head = lax.axis_size("seq"), lax.axis_size("head")
    inner_all = inner * n_head
    bc_all = 2 * STATE
    block = min(BLOCK, count)
    blocks = count // block
    mine = lax.axis_index("seq")

    (wz0, wx0, side0, side_own, tail, hp, cw, masks, segrow, cmask, earlier, following) = opening(
        doc_lengths, proj_z, proj_x, proj_bc, conv_bc_kernel, conv_bc_bias, proj_dt, hidden_in,
        conv_x_kernel, conv_x_bias, dt_bias, a_log, skip_gain, 2,
    )
    wz, wx, wside, wout = [wz0], [wx0], [side0], [proj_out]
    vm = lambda *shape: pltpu.VMEM(shape, jnp.float32)
    chips = n_seq // 2
    cws = [cw[8 * l : 8 * l + 8] for l in range(layers)]
    hps = [hp[8 * l : 8 * l + 8] for l in range(layers)]

    hidden = hidden_in
    saved = []
    more = count * 9 // 16 // 8 * 8
    for l in range(layers):
        final = l == layers - 1
        z, raw, dt, act, cum, carry, decays, e, mixed, entry, *rows = kernel_call(
            functools.partial(forward_kernel, l, heads, block, final, n_seq), "forward",
            [f32(count, inner), f32(count + 8, inner + bc_all), f32(count, WIDE), f32(count, inner + bc_all), f32(count, WIDE), f32(8, WIDE),
             f32(n_seq, WIDE), f32(8, count), f32(count, inner), f32(blocks * inner, STATE)]
            + ([f32(more, width), f32(count - more, width)] if final else [f32(count, width)])
            + ([f32(width, inner)] if l == 0 else []),
            [hidden, tail, norm_gain, wz[l], wx[l], wside[l], cws[l], hps[l], masks, segrow, cmask, earlier, gate_gain, wout[l], grad_out],
            [vm(count, width), vm(count, inner), vm(blocks * inner, STATE), vm(count, inner), vm(inner + 8, STATE), vm(n_seq, inner + 8, STATE)]
            + gather_sems(chips) * (2 if l == 0 else 1),
            cid=10 + 10 * l,
            specs=[VM] * 13 + [HB if l == 0 else VM, VM if final else HB],
        )
        if l == 0:
            wout[0] = rows.pop()
        hidden_l, tail_l = hidden, tail
        if final:
            last_rows = rows
            sums = grad_out
        else:
            sums, e, *weights, hidden, tail = exchange(
                [rows[0], e, hidden], 11 + 10 * l, inner_all=inner_all,
                gathers=[(proj_z, l + 1), (proj_x, l + 1), (proj_out, l + 1), (side_own[l * rows_loc : (l + 1) * rows_loc], None)],
            )
            for held, new in zip((wz, wx, wout, wside), weights):
                held.append(new)
        saved.append((hidden_l, tail_l, z, raw, dt, act, cum, carry, decays, mixed, entry, e, sums))

    grad = grad_out
    big = [None] * layers
    small, out_parts = [], []
    for l in reversed(range(layers)):
        final = l == layers - 1
        hidden_l, tail, z, raw, dt, act, cum, carry, decays, mixed, entry, e, sums = saved[l]
        dz, draw, ddt, dcw, dhp, dwout, dggain, *extra = kernel_call(
            functools.partial(backward_kernel, l, heads, block, inner_all, final, n_seq, n_head), "backward",
            [f32(count, inner), f32(count + 8, inner + bc_all), f32(count, WIDE), f32(8, inner + bc_all), f32(8, WIDE), f32(width, inner), f32(8, inner)]
            + [f32(8, count)] * (1 if final else 0),
            [grad, e, sums, act, cum, masks, carry, z, gate_gain, wout[l], mixed, entry, decays, following, raw, dt, segrow, cws[l], hps[l]],
            [vm(count, inner), vm(count, inner), vm(count, WIDE), vm(count, STATE), vm(blocks * inner, STATE), vm(inner, STATE),
             vm(n_seq, inner, STATE), vm(count, inner + bc_all), vm(count, inner), vm(count, STATE)]
            + gather_sems(chips)
            + ([vm(n_head, 8, count)] + [pltpu.SemaphoreType.DMA((n_head,))] * 2 + [pltpu.SemaphoreType.DMA] if final else []),
            cid=12 + 10 * l,
        )
        if final:
            squares = extra[0]
            out_parts.append(lax.psum(last_rows[0], "head"))
        ins = [hidden_l, tail, norm_gain, wz[l], wx[l], wside[l], dz, draw, ddt, dcw, dhp, dggain, dwout, grad]
        if l > 0:
            grad, *big[l], smalls = exchange(ins, 14 + 10 * l, layer=l)
            late, grad, out_parts = lax.optimization_barrier((last_rows[1], grad, out_parts))
            out_parts.append(lax.psum(late, "head"))
        else:
            grad, *big[l], bcs, e = exchange(ins, 14, full=(big[1][0], smalls), bc_loc=bc_loc)
    outs = [
        (count, width), (count, width), (layers, width), proj_z.shape, proj_x.shape, proj_bc.shape, proj_dt.shape, conv_x_kernel.shape,
        conv_x_bias.shape, conv_bc_kernel.shape, conv_bc_bias.shape, dt_bias.shape, a_log.shape, skip_gain.shape, gate_gain.shape, proj_out.shape,
    ]
    return tuple(
        kernel_call(
            functools.partial(finish_kernel, n_head, inner_all), "finish", [f32(*o) for o in outs],
            [e, bcs, squares, hidden, *out_parts, grad, *big[0], *big[1]],
        )
    )


def solution(mesh):
    in_specs = (
        P("seq", None),
        P("seq", None),
        P(),
        P(),
        P(None, "seq", "head"),
        P(None, "seq", "head"),
        P(None, "seq", "head"),
        P(None, "seq", "head"),
        P(None, None, "head"),
        P(None, "head"),
        P(None, None, "head"),
        P(None, "head"),
        P(None, "head"),
        P(None, "head"),
        P(None, "head"),
        P(None, "head"),
        P(None, "seq", "head"),
    )
    out_specs = (
        P("seq", None),
        P("seq", None),
        P(),
        P(None, "seq", "head"),
        P(None, "seq", "head"),
        P(None, "seq", "head"),
        P(None, "seq", "head"),
        P(None, None, "head"),
        P(None, "head"),
        P(None, None, "head"),
        P(None, "head"),
        P(None, "head"),
        P(None, "head"),
        P(None, "head"),
        P(None, "head"),
        P(None, "seq", "head"),
    )
    return jax.shard_map(body, mesh=mesh, in_specs=in_specs, out_specs=out_specs, check_vma=False)
```

```python
import functools

import jax
import jax.numpy as jnp
from jax import lax
from jax.experimental import pallas as pl
from jax.experimental.pallas import tpu as pltpu
from jax.sharding import PartitionSpec as P

STATE = 128
KERNEL = 4
BLOCK = 256
MESHID = pl.DeviceIdType.MESH
VM = pl.BlockSpec(memory_space=pltpu.VMEM)
HB = pl.BlockSpec(memory_space=pl.ANY)


EPS = 1e-05
NEG_FILL = -1e30
EXACT = lax.Precision.HIGHEST
FAST = lax.Precision.HIGH
WIDE = 128


def mm(left, right, dims=((1,), (0,)), precision=FAST):
    return lax.dot_general(left, right, (dims, ((), ())), precision=precision, preferred_element_type=jnp.float32)


ROWS_T = ((1,), (1,))
COLS_T = ((0,), (0,))


def sigmoid(v):
    return 1.0 / (1.0 + jnp.exp(-v))


def softplus(v):
    small = jnp.exp(-jnp.abs(v))
    one = 1.0 + small
    exact = jnp.where(one == 1.0, small, small * jnp.log(one) / jnp.where(one == 1.0, 1.0, one - 1.0))
    return jnp.maximum(v, 0.0) + exact


def spread_heads(per_head, heads, dim):
    rows = per_head.shape[0]
    return jnp.concatenate([jnp.broadcast_to(per_head[:, h : h + 1], (rows, dim)) for h in range(heads)], axis=1)


def scaled_rows(state, factors, heads):
    dim = state.shape[0] // heads
    return jnp.concatenate([state[h * dim : (h + 1) * dim] * factors[:, h : h + 1] for h in range(heads)], axis=0)


def head_sums(wide, heads):
    width = wide.shape[1]
    dim = width // heads
    row = lax.broadcasted_iota(jnp.int32, (width, WIDE), 0)
    col = lax.broadcasted_iota(jnp.int32, (width, WIDE), 1)
    pick = ((row >= col * dim) & (row < (col + 1) * dim)).astype(jnp.float32)
    return mm(wide, pick, precision=EXACT)


def lower_of(rows):
    return lax.broadcasted_iota(jnp.int32, (rows, rows), 0) >= lax.broadcasted_iota(jnp.int32, (rows, rows), 1)


def normed_of(h, gain):
    r = lax.rsqrt(jnp.mean(h * h, axis=1, keepdims=True) + EPS)
    return h * r * gain


def conv_total(raw_ref, cw_ref, masks_ref, at, rows):
    total = cw_ref[KERNEL : KERNEL + 1, :] + cw_ref[KERNEL - 1 : KERNEL, :] * raw_ref[8 + at : 8 + at + rows, :]
    for k in range(KERNEL - 1):
        first = 8 + at - (KERNEL - 1) + k
        total = total + cw_ref[k : k + 1, :] * (raw_ref[first : first + rows, :] * masks_ref[at : at + rows, k : k + 1])
    return total


def gather_ops(place, src, slot, sems):
    me, chips, core, chip, sib = place
    ss, rs, fs, fr, ls = sems

    def back(k):
        return lax.rem(chip - k + chips, chips) * 2 + core

    def across(k):
        return pltpu.make_async_remote_copy(src_ref=src, dst_ref=slot(me), send_sem=ss.at[k], recv_sem=rs.at[k],
            device_id={"seq": lax.rem(chip + k, chips) * 2 + core}, device_id_type=MESHID)

    def over(k):
        return pltpu.make_async_remote_copy(src_ref=src if k == 0 else slot(back(k)), dst_ref=slot(back(k)), send_sem=fs.at[k], recv_sem=fr.at[k],
            device_id={"seq": sib}, device_id_type=MESHID)

    local = pltpu.make_async_copy(src, slot(me), ls)

    def start():
        for k in range(1, chips):
            across(k).start()
        over(0).start()
        local.start()

    def forward():
        for k in range(1, chips):
            across(k).wait_recv()
            over(k).start()

    def end():
        for k in range(chips):
            over(k).wait()
        for k in range(1, chips):
            across(k).wait_send()
        local.wait()

    return start, forward, end


def gather_sems(chips):
    return [pltpu.SemaphoreType.DMA((chips,))] * 4 + [pltpu.SemaphoreType.DMA]


def signal_peers(place, heads):
    me, chips, core, chip, sib = place
    bar = pltpu.get_barrier_semaphore()
    pl.semaphore_signal(bar, inc=1, device_id={"seq": sib}, device_id_type=MESHID)
    for k in range(1, chips):
        pl.semaphore_signal(bar, inc=1, device_id={"seq": lax.rem(chip + k, chips) * 2 + core}, device_id_type=MESHID)
    if heads:
        z = lax.axis_index("head")
        for k in range(1, heads):
            pl.semaphore_signal(bar, inc=1, device_id={"head": lax.rem(z + k, heads)}, device_id_type=MESHID)
        return chips + heads - 1
    return chips


def forward_kernel(layer, heads, block, last_layer, n_seq, hidden, tail, gains, wz, wx, wside, cw, hp, masks, segrow, cmask, before, ggains, wout_in, grad, *refs):
    refs = list(refs)
    cw, hp = cw.at[pl.ds(8 * layer, 8)], hp.at[pl.ds(8 * layer, 8)]
    z_o, raw_o, dt_o, act_o, cum_o, carry_o, decays_o, e_o, mixed_o, entry_o, *rows_o = refs[: 12 if last_layer else 11]
    first = layer == 0
    refs = refs[12 if last_layer else 11 :]
    wout = refs.pop(0) if first else wout_in
    nrm, lv, st, y, dev, pieces = refs[:6]
    refs = refs[6:]
    place = seq_place(n_seq)
    expected = signal_peers(place, 0)
    start, forward, end = gather_ops(place, dev, lambda owner: pieces.at[owner], refs[:5])
    if first:
        rows_loc = wout_in.shape[1]
        w_start, w_forward, w_end = gather_ops(
            place, wout_in.at[0], lambda owner: wout.at[pl.ds(pl.multiple_of(owner * rows_loc, 8), rows_loc)], refs[5:10]
        )
    count, inner = z_o.shape
    blocks = count // block
    dim = inner // heads
    wide_bc = 2 * STATE
    gain = gains[layer : layer + 1, :]
    ggain = ggains[layer : layer + 1, :]
    if first:
        pl.semaphore_wait(pltpu.get_barrier_semaphore(), expected)
        w_start()
    t = normed_of(tail[...], gain)
    raw_o[0:8, :inner] = mm(t, wx[...])
    raw_o[0:8, inner:] = mm(t, wside[:, :wide_bc])
    lower = lower_of(block)
    lower_f = lower.astype(jnp.float32)
    carry_o[...] = jnp.zeros_like(carry_o)
    state = decay = None

    def step_of(own):
        return softplus(dt_o[own, :] + hp[0:1, :])

    for b in range(blocks):
        at = b * block
        own = slice(at, at + block)
        n = normed_of(hidden[own, :], gain)
        nrm[own, :] = n
        raw_o[8 + at : 8 + at + block, :inner] = mm(n, wx[...])
        side = mm(n, wside[...])
        raw_o[8 + at : 8 + at + block, inner:] = side[:, :wide_bc]
        dt_o[own, :] = side[:, wide_bc:]
        total = conv_total(raw_o, cw, masks, at, block)
        act = total * sigmoid(total)
        act_o[own, :] = act
        step = step_of(own)
        cum = mm(lower_f, -step * jnp.exp(hp[1:2, :]), precision=EXACT)
        cum_o[own, :] = cum
        last = cum[block - 1 : block, :]
        leave = step * jnp.exp(last - cum) * masks[own, 4:5]
        states = mm(act[:, :inner] * spread_heads(leave, heads, dim), act[:, inner : inner + STATE], COLS_T)
        st[b * inner : (b + 1) * inner, :] = states
        carry = jnp.exp(last) * cmask[b : b + 1, :]
        carry_o[b : b + 1, :] = carry
        state = states if b == 0 else scaled_rows(state, carry, heads) + states
        decay = carry if b == 0 else decay * carry
    dev[:inner, :] = state
    dev[inner:, :] = jnp.broadcast_to(decay, (8, WIDE))
    if first:
        w_forward()
    else:
        pl.semaphore_wait(pltpu.get_barrier_semaphore(), expected)
    start()
    for b in range(blocks):
        at = b * block
        own = slice(at, at + block)
        z = mm(nrm[own, :], wz[...])
        z_o[own, :] = z
        lv[own, :] = z * sigmoid(z)
        values, bm, cm = act_o[own, :inner], act_o[own, inner : inner + STATE], act_o[own, inner + STATE :]
        step, cum = step_of(own), cum_o[own, :]
        cum_t = cum.T
        allowed = lower & (masks[own, 5:6] == segrow[0:1, own])
        scores = mm(cm, bm, ROWS_T)
        ys = []
        for h in range(heads):
            v = values[:, h * dim : (h + 1) * dim]
            spans = cum[:, h : h + 1] - cum_t[h : h + 1, :]
            s = jnp.exp(jnp.where(allowed, spans, NEG_FILL)) * scores
            ys.append(mm(s, v * step[:, h : h + 1]) + hp[2:3, h : h + 1] * v)
        y[own, :] = jnp.concatenate(ys, axis=1)
    forward()
    if first:
        w_end()
    end()
    state = jnp.zeros((inner, STATE), jnp.float32)
    for j in range(n_seq):
        decay = pieces[j, inner : inner + 1, :]
        decays_o[j : j + 1, :] = decay
        later = scaled_rows(state, decay, heads) + pieces[j, :inner, :]
        state = jnp.where(before[j : j + 1, :] > 0.5, later, state)
    for b in range(blocks):
        at = b * block
        own = slice(at, at + block)
        entry_o[b * inner : (b + 1) * inner, :] = state
        enter = jnp.exp(cum_o[own, :]) * masks[own, 3:4]
        mixed = y[own, :] + spread_heads(enter, heads, dim) * mm(act_o[own, inner + STATE :], state, ROWS_T)
        mixed_o[own, :] = mixed
        gated = mixed * lv[own, :]
        out = mm(gated * ggain, wout[...], ROWS_T)
        done = 0
        for part in rows_o:
            low, high = max(at, done), min(at + block, done + part.shape[0])
            if low < high:
                part[low - done : high - done, :] = out[low - at : high - at]
            done = done + part.shape[0]
        squares = jnp.sum(gated * gated, axis=1, keepdims=True)
        if last_layer:
            dots = jnp.sum(grad[own, :] * out, axis=1, keepdims=True)
        else:
            dots = jnp.zeros_like(squares)
        lane = lax.broadcasted_iota(jnp.int32, (block, WIDE), 1)
        both = jnp.where(lane == 0, squares, jnp.where(lane == 1, dots, 0.0))
        e_o[:, own] = both.T[0:8, :]
        state = scaled_rows(state, carry_o[b : b + 1, :], heads) + st[b * inner : (b + 1) * inner, :]


def backward_kernel(layer, heads, block, inner_all, last_layer, n_seq, n_head, grad, e, sums, act, cum, masks, carry, z, ggains, wout, mixed, entry, decays, after, raw, dt, segrow, cw, hp, *refs):
    refs = list(refs)
    cw, hp = cw.at[pl.ds(8 * layer, 8)], hp.at[pl.ds(8 * layer, 8)]
    dz_o, draw_o, ddt_o, dcw_o, dhp_o, dwout_o, dgg_o = refs[:7]
    refs = refs[7:]
    if last_layer:
        esum = refs.pop(0)
    wide, dmix, de, dc, dentry, dstate, gpieces, dtot, dxi, dbi = refs[:10]
    refs = refs[10:]
    place = seq_place(n_seq)
    expected = signal_peers(place, n_head if last_layer else 0)
    start, forward, end = gather_ops(place, dstate, lambda owner: gpieces.at[owner], refs[:5])
    if last_layer:
        egot, es, er, el = refs[5:9]
        zi = lax.axis_index("head")
        near = pltpu.make_async_copy(e, egot.at[zi], el)
        far = [
            pltpu.make_async_remote_copy(src_ref=e, dst_ref=egot.at[zi], send_sem=es.at[k], recv_sem=er.at[k],
                device_id={"head": lax.rem(zi + k, n_head)}, device_id_type=MESHID)
            for k in range(1, n_head)
        ]
        pl.semaphore_wait(pltpu.get_barrier_semaphore(), expected)
        near.start()
        for copy in far:
            copy.start()
    count, inner = z.shape
    blocks = count // block
    dim = inner // heads
    ggain = ggains[layer : layer + 1, :]
    for b in range(blocks):
        own = slice(b * block, (b + 1) * block)
        wide[own, :] = mm(grad[own, :], wout[...])
    if last_layer:
        near.wait()
        for copy in far:
            copy.wait()
        total = egot[0]
        for k in range(1, n_head):
            total = total + egot[k]
        esum[...] = total
        e = esum

    def columns(own):
        return jnp.concatenate([e[:, own], jnp.zeros((WIDE - 8, block), jnp.float32)], axis=0).T

    def enter_of(own):
        return spread_heads(jnp.exp(cum[own, :]) * masks[own, 3:4], heads, dim)

    ggain_sum = jnp.zeros((1, inner), jnp.float32)
    for b in range(blocks):
        own = slice(b * block, (b + 1) * block)
        et = columns(own)
        scale = lax.rsqrt(et[:, 0:1] / inner_all + EPS)
        gs = et[:, 1:2] if last_layer else jnp.sum(grad[own, :] * sums[own, :], axis=1, keepdims=True)
        dsq = gs * (-0.5 / inner_all) * scale * scale * scale
        dgg = scale * wide[own, :]
        zz = z[own, :]
        sg = sigmoid(zz)
        sil = zz * sg
        mx = mixed[own, :]
        gated = mx * sil
        ggain_sum = ggain_sum + jnp.sum(dgg * gated, axis=0, keepdims=True)
        dgated = dgg * ggain + 2.0 * dsq * gated
        dm = dgated * sil
        dmix[own, :] = dm
        dz_o[own, :] = dgated * mx * (sg * (1.0 + zz * (1.0 - sg)))
        wide[own, :] = scale * (gated * ggain)
        dentry[b * inner : (b + 1) * inner, :] = mm(dm * enter_of(own), act[own, inner + STATE :], COLS_T)
    dgg_o[...] = jnp.broadcast_to(ggain_sum, dgg_o.shape)
    g = dentry[(blocks - 1) * inner :, :]
    for b in range(blocks - 2, -1, -1):
        g = dentry[b * inner : (b + 1) * inner, :] + scaled_rows(g, carry[b : b + 1, :], heads)
    dstate[...] = g
    if not last_layer:
        pl.semaphore_wait(pltpu.get_barrier_semaphore(), expected)
    start()
    lower = lower_of(block)
    lower_f = lower.astype(jnp.float32)
    pad = jnp.zeros((block, WIDE - heads), jnp.float32)
    for b in range(blocks):
        at = b * block
        own = slice(at, at + block)
        part = mm(grad[own, :], wide[own, :], COLS_T)
        if b == 0:
            dwout_o[...] = part
        else:
            dwout_o[...] += part
        values, bm, cm = act[own, :inner], act[own, inner : inner + STATE], act[own, inner + STATE :]
        en = entry[b * inner : (b + 1) * inner, :]
        dread = dmix[own, :] * enter_of(own)
        step = softplus(dt[own, :] + hp[0:1, :])
        cum_b = cum[own, :]
        cum_t = cum_b.T
        allowed = lower & (masks[own, 5:6] == segrow[0:1, own])
        scores = mm(cm, bm, ROWS_T)
        dscores = jnp.zeros((block, block), jnp.float32)
        dxs, rowsums, colsums = [], [], []
        for h in range(heads):
            cut = slice(h * dim, (h + 1) * dim)
            x = values[:, cut] * step[:, h : h + 1]
            dy = dmix[own, cut]
            spans = cum_b[:, h : h + 1] - cum_t[h : h + 1, :]
            decay = jnp.exp(jnp.where(allowed, spans, NEG_FILL))
            s = decay * scores
            ds = mm(dy, x, ROWS_T)
            dscores = dscores + ds * decay
            dspan = ds * s
            rowsums.append(jnp.sum(dspan, axis=1, keepdims=True))
            colsums.append(jnp.sum(dspan, axis=0, keepdims=True))
            dxs.append(mm(s, dy, COLS_T))
        rowsum = jnp.concatenate(rowsums + [pad], axis=1)
        colsum = jnp.concatenate(colsums + [jnp.zeros((WIDE - heads, block), jnp.float32)], axis=0).T
        de[own, :] = head_sums(dread * mm(cm, en, ROWS_T), heads) + rowsum - colsum
        dxi[own, :] = jnp.concatenate(dxs, axis=1)
        dc[own, :] = mm(dread, en) + mm(dscores, bm)
        dbi[own, :] = mm(dscores, cm, COLS_T)
        if b == 0:
            forward()
    end()
    g = jnp.zeros((inner, STATE), jnp.float32)
    for j in range(n_seq - 1, -1, -1):
        later = scaled_rows(g, decays[j : j + 1, :], heads) + gpieces[j]
        g = jnp.where(after[j : j + 1, :] > 0.5, later, g)
    sub = lax.broadcasted_iota(jnp.int32, (block, WIDE), 0)
    a_exp = jnp.exp(hp[1:2, :])
    bias_sum = alog_sum = skip_sum = jnp.zeros((1, WIDE), jnp.float32)
    for b in range(blocks - 1, -1, -1):
        at = b * block
        own = slice(at, at + block)
        values, bm = act[own, :inner], act[own, inner : inner + STATE]
        shifted = dt[own, :] + hp[0:1, :]
        step = softplus(shifted)
        step_wide = spread_heads(step, heads, dim)
        cum_b = cum[own, :]
        last = cum_b[block - 1 : block, :]
        leave = spread_heads(jnp.exp(last - cum_b) * masks[own, 4:5], heads, dim)
        carry_b = carry[b : b + 1, :]
        ge = g * entry[b * inner : (b + 1) * inner, :]
        dcs = [jnp.sum(jnp.sum(ge[h * dim : (h + 1) * dim], axis=0, keepdims=True), axis=1, keepdims=True) for h in range(heads)]
        dcarry = jnp.concatenate(dcs + [jnp.zeros((1, WIDE - heads), jnp.float32)], axis=1)
        dw = mm(bm, g, ROWS_T) * leave
        dx = dxi[own, :] + dw
        x = values * step_wide
        dleave = head_sums(dw * x, heads)
        dlast = jnp.sum(dleave, axis=0, keepdims=True) + dcarry * carry_b
        dcum = de[own, :] - dleave + jnp.where(sub == block - 1, dlast, 0.0)
        dld = mm(lower_f, dcum, COLS_T, EXACT)
        ddt = (head_sums(dx * values, heads) - dld * a_exp) * sigmoid(shifted)
        alog_sum = alog_sum - jnp.sum(dld * step, axis=0, keepdims=True) * a_exp
        ddt_o[own, :] = ddt
        bias_sum = bias_sum + jnp.sum(ddt, axis=0, keepdims=True)
        dy = dmix[own, :]
        skip_sum = skip_sum + jnp.sum(head_sums(dy * values, heads), axis=0, keepdims=True)
        total = conv_total(raw, cw, masks, at, block)
        sg = sigmoid(total)
        dsil = sg * (1.0 + total * (1.0 - sg))
        dtot[own, :inner] = (dx * step_wide + dy * spread_heads(hp[2:3, :], heads, dim)) * dsil[:, :inner]
        dtot[own, inner : inner + STATE] = (dbi[own, :] + mm(x * leave, g)) * dsil[:, inner : inner + STATE]
        dtot[own, inner + STATE :] = dc[own, :] * dsil[:, inner + STATE :]
        g = dentry[b * inner : (b + 1) * inner, :] + scaled_rows(g, carry_b, heads)
    dhp_o[...] = jnp.concatenate([bias_sum, alog_sum, skip_sum, jnp.zeros((5, WIDE), jnp.float32)], axis=0)
    conv_back(dtot, raw, masks, cw, draw_o, dcw_o)


def conv_back(dtot, raw, masks, cw, draw_o, dcw_o):
    count = dtot.shape[0]
    dall = dtot[...]
    draw_o[0:8, :] = jnp.zeros_like(draw_o[0:8, :])
    draw_o[8:, :] = cw[KERNEL - 1 : KERNEL, :] * dall
    dk = []
    for k in range(KERNEL - 1):
        kept = dall * masks[:, k : k + 1]
        first = 8 - (KERNEL - 1) + k
        dk.append(jnp.sum(kept * raw[first : first + count, :], axis=0, keepdims=True))
        draw_o[first : first + count, :] = draw_o[first : first + count, :] + cw[k : k + 1, :] * kept
    dk.append(jnp.sum(dall * raw[8:, :], axis=0, keepdims=True))
    dk.append(jnp.sum(dall, axis=0, keepdims=True))
    dcw_o[...] = jnp.concatenate(dk + [jnp.zeros((7 - KERNEL, dall.shape[1]), jnp.float32)], axis=0)


def f32(*shape):
    return jax.ShapeDtypeStruct(shape, jnp.float32)


def kernel_call(kernel, name, outs, args, scratch=(), cid=None, specs=None, out_specs=None):
    params = {} if cid is None else dict(collective_id=cid, has_side_effects=True)
    return pl.pallas_call(
        kernel,
        out_shape=outs,
        in_specs=specs or [VM] * len(args),
        out_specs=out_specs or [VM] * len(outs),
        scratch_shapes=list(scratch),
        cost_estimate=pl.CostEstimate(flops=1, bytes_accessed=1, transcendentals=0),
        compiler_params=pltpu.CompilerParams(vmem_limit_bytes=56 * 1024 * 1024, **params),
        name=name,
    )(*args)


def greet(peers, axis):
    bar = pltpu.get_barrier_semaphore()
    for p in peers:
        pl.semaphore_signal(bar, inc=1, device_id={axis: p}, device_id_type=MESHID)
    pl.semaphore_wait(bar, len(peers))


def exchange_kernel(spec, *refs):
    n, seq, ats, ns, bc_loc, inner_all, step, (d1, d2, window), (layer, block) = spec
    ng = len(ats)
    forward = inner_all > 0
    full = bc_loc > 0
    refs = list(refs)

    def take(number):
        out = refs[:number]
        del refs[:number]
        return out

    if forward:
        x_ref, e_ref, base = take(3)
    else:
        hidden, tail, gains, wz, wx, wside, dz, draw, ddt, dcw, dhp, dggain, dwout, base = take(14)
    gx = take(ng)
    if full:
        sidex, earlier = take(2)
    o_ref = take(1)[0]
    if forward:
        eo_ref = take(1)[0]
    go, so = take(ng), take(ns)
    if forward:
        hidden_o, tail_o = take(2)
    elif full:
        bco, fo_ref = take(2)
    else:
        f_ref = take(1)[0]
    inl, inr = take(2)
    if not forward:
        x_ref, nrm, e_ref, eo_ref, tailgot, dwside, dwz, dwx = take(8)
        sx = [dwside, dwz, dwx, dwout]
    if full:
        f_ref = take(1)[0]
    egot, mids, gots = take(1)[0], take(ns), take(ns)
    if full:
        fgot, shgot, sh, bcs, bcgot = take(5)
    sl, sr, rl, rr, es, er, el, ts, tr = take(9)
    if ng:
        gs, gr, gfs, gfr, gl = take(5)
    if ns:
        cs, cr, ss, rs = take(4)
    if full:
        fs, fr, bs, br, bl, hs, hr, hl = take(8)
    z = lax.axis_index("head")
    me, chips, core, chip, sib = seq_place(seq)
    count = x_ref.shape[0] // step
    bar = pltpu.get_barrier_semaphore()
    for k in range(1, n):
        pl.semaphore_signal(bar, inc=1, device_id={"head": lax.rem(z + k, n)}, device_id_type=MESHID)
    for k in range(1, seq):
        pl.semaphore_signal(bar, inc=1, device_id={"seq": lax.rem(me + k, seq)}, device_id_type=MESHID)
    planned = []
    if not forward:
        inner = dz.shape[1]
        wide_bc = 2 * STATE
        gain = gains[layer : layer + 1, :]

        def back_norm(h, dn):
            r = lax.rsqrt(jnp.mean(h * h, axis=1, keepdims=True) + EPS)
            hr = h * r
            g = dn * gain
            return r * (g - hr * jnp.mean(g * hr, axis=1, keepdims=True)), jnp.sum(dn * hr, axis=0, keepdims=True), hr * gain

        dr = draw[0:8, :]
        dn = mm(dr[:, :inner], wx[...], ROWS_T) + mm(dr[:, inner:], wside[:, :wide_bc], ROWS_T)
        e_ref[...], dgain, nrm[0:8, :] = back_norm(tail[...], dn)
        tokens = dz.shape[0]
        cuts = [slice(b * block, (b + 1) * block) for b in range(tokens // block)]
        shifted_cuts = [slice(8 + c.start, 8 + c.stop) for c in cuts]

        def side_of(c, d):
            return jnp.concatenate([draw[d, inner:], ddt[c, :]], axis=1)

        for c, d in zip(cuts, shifted_cuts):
            dn = mm(dz[c, :], wz[...], ROWS_T) + mm(draw[d, :inner], wx[...], ROWS_T) + mm(side_of(c, d), wside[...], ROWS_T)
            x_ref[c, :], dg, nrm[d, :] = back_norm(hidden[c, :], dn)
            dgain = dgain + dg
        f_ref[0:8, :] = jnp.zeros((8, f_ref.shape[1]), jnp.float32)
        f_ref[0 : KERNEL + 1, :wide_bc] = dcw[0 : KERNEL + 1, inner:]
        f_ref[0 : KERNEL + 1, wide_bc : wide_bc + inner] = dcw[0 : KERNEL + 1, :inner]
        f_ref[0:3, -WIDE:] = dhp[0:3, :]
        f_ref[5:6, wide_bc : wide_bc + inner] = dggain[0:1, :]
        for i in range(hidden.shape[1] // wide_bc):
            f_ref[5 + i : 6 + i, :wide_bc] = dgain[:, i * wide_bc : (i + 1) * wide_bc]
        if full:
            f_ref[8:, :] = earlier[...]

        def side_grads():
            dwside[:, :wide_bc] = mm(nrm[0:8, :], draw[0:8, inner:], COLS_T)
            dwside[:, wide_bc:] = jnp.zeros_like(dwside[:, wide_bc:])
            for c, d in zip(cuts, shifted_cuts):
                dwside[...] += mm(nrm[d, :], side_of(c, d), COLS_T)
            s_start(0)

        def z_grads():
            dwz[...] = mm(nrm[8:, :], dz[...], COLS_T)
            s_start(1)

        def x_grads():
            dwx[...] = mm(nrm[0:8, :], draw[0:8, :inner], COLS_T) + mm(nrm[8:, :], draw[8:, :inner], COLS_T)
            s_start(2)

        planned = [(1, side_grads), (3, z_grads), (5, x_grads)]
    pl.semaphore_wait(bar, n - 1 + seq - 1)

    def head_sum(src, got, dst, send, recv, near):
        own = pltpu.make_async_copy(src, got.at[z], near)
        far = [
            pltpu.make_async_remote_copy(src_ref=src, dst_ref=got.at[z], send_sem=send.at[k], recv_sem=recv.at[k],
                device_id={"head": lax.rem(z + k, n)}, device_id_type=MESHID)
            for k in range(1, n)
        ]

        def start():
            own.start()
            for copy in far:
                copy.start()

        def end():
            own.wait()
            for copy in far:
                copy.wait()
            total = got[0]
            for k in range(1, n):
                total = total + got[k]
            dst[...] = total

        return start, end

    start_extra, end_extra = head_sum(e_ref, egot, eo_ref, es, er, el)

    def tail_copy():
        if forward:
            return pltpu.make_async_remote_copy(src_ref=hidden_o.at[pl.ds(x_ref.shape[0] - 8, 8)], dst_ref=tail_o, send_sem=ts, recv_sem=tr,
                device_id={"seq": me + 1}, device_id_type=MESHID)
        return pltpu.make_async_remote_copy(src_ref=eo_ref, dst_ref=tailgot, send_sem=ts, recv_sem=tr,
            device_id={"seq": me - 1}, device_id_type=MESHID)

    def back_tail():
        end_extra()

        @pl.when(me > 0)
        def _():
            tail_copy().start()

    if full:
        start_shared, end_shared = head_sum(sh, shgot, sh, hs, hr, hl)

    def small(k):
        return pltpu.make_async_remote_copy(src_ref=f_ref, dst_ref=fgot.at[me], send_sem=fs.at[k], recv_sem=fr.at[k],
            device_id={"seq": lax.rem(me + k, seq)}, device_id_type=MESHID)

    def end_small():
        for k in range(1, seq):
            small(k).wait()
        total = fgot[0]
        for k in range(1, seq):
            total = total + fgot[k]
        fo_ref[...] = total
        sh[...] = total[:, : sh.shape[1]]
        start_shared()

    def peer(k):
        return {"seq": lax.rem(chip + k, chips) * 2 + core}

    def source(i):
        return gx[i] if ats[i] is None else gx[i].at[ats[i]]

    def g_at(i, owner):
        rows = go[i].shape[0] // seq
        return go[i].at[pl.ds(pl.multiple_of(owner * rows, 8), rows)]

    def back(k):
        return lax.rem(chip - k + chips, chips) * 2 + core

    def g_local(i):
        return pltpu.make_async_copy(source(i), g_at(i, me), gl.at[i])

    def g_across(i, k):
        return pltpu.make_async_remote_copy(src_ref=source(i), dst_ref=g_at(i, me), send_sem=gs.at[i, k], recv_sem=gr.at[i, k],
            device_id=peer(k), device_id_type=MESHID)

    def g_over(i, k):
        return pltpu.make_async_remote_copy(src_ref=source(i) if k == 0 else g_at(i, back(k)), dst_ref=g_at(i, back(k)),
            send_sem=gfs.at[i, k], recv_sem=gfr.at[i, k], device_id={"seq": sib}, device_id_type=MESHID)

    g_pairs = [(i, k) for k in range(1, chips) for i in range(ng)]

    def g_start():
        for i, k in g_pairs:
            g_across(i, k).start()
        for i in range(ng):
            g_over(i, 0).start()
            g_local(i).start()

    def g_forward():
        for i, k in g_pairs:
            g_across(i, k).wait_recv()
            g_over(i, k).start()

    def g_end():
        for i in range(ng):
            for k in range(chips):
                g_over(i, k).wait()
            g_local(i).wait()
        for i, k in g_pairs:
            g_across(i, k).wait_send()

    def block(i, k, c):
        rows = so[i].shape[0]
        return pl.ds(pl.multiple_of((lax.rem(chip + k, chips) * 2 + c) * rows, 8), rows)

    def s_over(i, k):
        return pltpu.make_async_remote_copy(src_ref=sx[i].at[block(i, k, 1 - core)], dst_ref=mids[i].at[k], send_sem=cs.at[i, k], recv_sem=cr.at[i, k],
            device_id={"seq": sib}, device_id_type=MESHID)

    def s_across(i, k):
        return pltpu.make_async_remote_copy(src_ref=mids[i].at[k], dst_ref=gots[i].at[k], send_sem=ss.at[i, k], recv_sem=rs.at[i, k],
            device_id=peer(k), device_id_type=MESHID)

    def s_start(i):
        for k in range(chips):
            s_over(i, k).start()

    def s_middle(i):
        for k in list(range(1, chips)) + [0]:
            s_over(i, k).wait_recv()
            mids[i][k] = mids[i][k] + sx[i][block(i, k, core), :]
            if k:
                s_across(i, k).start()

    def s_final(i):
        total = mids[i][0]
        for k in range(1, chips):
            s_across(i, k).wait_recv()
            total = total + gots[i][k]
        so[i][...] = total

    def s_drain():
        for i in range(ns):
            for k in range(chips):
                s_over(i, k).wait_send()
                if k:
                    s_across(i, k).wait_send()

    def b_own():
        return pltpu.make_async_copy(bcs.at[z], bcgot.at[z], bl)

    def b_across(k):
        to = lax.rem(z + k, n)
        return pltpu.make_async_remote_copy(src_ref=bcs.at[to], dst_ref=bcgot.at[z], send_sem=bs.at[k], recv_sem=br.at[k],
            device_id={"head": to}, device_id_type=MESHID)

    def b_start():
        s_final(0)
        for p in range(n):
            cut = slice(p * bc_loc, (p + 1) * bc_loc)
            bcs[p] = jnp.concatenate([so[0][:, cut], sidex[:, cut]], axis=1)
        b_own().start()
        for k in range(1, n):
            b_across(k).start()

    def b_end():
        b_own().wait()
        for k in range(1, n):
            b_across(k).wait()
        total = bcgot[0]
        for k in range(1, n):
            total = total + bcgot[k]
        bco[...] = total

    low = (n - 1) // 2
    def rows(c):
        return pl.ds(pl.multiple_of(c * step, 8), step)
    def root(c):
        return low + lax.rem(c, 2) if n % 2 == 0 else jnp.int32(low)
    def right(src, dst, c):
        return pltpu.make_async_remote_copy(src_ref=src.at[rows(c)], dst_ref=dst.at[rows(c)], send_sem=sr.at[c], recv_sem=rl.at[c],
            device_id={"head": z + 1}, device_id_type=MESHID)
    def left(src, dst, c):
        return pltpu.make_async_remote_copy(src_ref=src.at[rows(c)], dst_ref=dst.at[rows(c)], send_sem=sl.at[c], recv_sem=rr.at[c],
            device_id={"head": z - 1}, device_id_type=MESHID)
    def forward_step(c):
        r = root(c)
        @pl.when((z < r) & (z == 0))
        def _():
            right(x_ref, inl, c).start()
        @pl.when((z < r) & (z > 0))
        def _():
            right(x_ref, inl, c).wait_recv()
            inl[rows(c), :] = inl[rows(c), :] + x_ref[rows(c), :]
            right(inl, inl, c).start()
        @pl.when((z > r) & (z == n - 1))
        def _():
            left(x_ref, inr, c).start()
        @pl.when((z > r) & (z < n - 1))
        def _():
            left(x_ref, inr, c).wait_recv()
            inr[rows(c), :] = inr[rows(c), :] + x_ref[rows(c), :]
            left(inr, inr, c).start()
    def root_step(c):
        @pl.when(z == root(c))
        def _():
            @pl.when(z > 0)
            def _():
                right(x_ref, inl, c).wait_recv()
            @pl.when(z == 0)
            def _():
                inl[rows(c), :] = jnp.zeros_like(inl[rows(c), :])
            @pl.when(z < n - 1)
            def _():
                left(x_ref, inr, c).wait_recv()
            @pl.when(z == n - 1)
            def _():
                inr[rows(c), :] = jnp.zeros_like(inr[rows(c), :])
            total = x_ref[rows(c), :] + inl[rows(c), :] + inr[rows(c), :]
            o_ref[rows(c), :] = total if forward else total + base[rows(c), :]
            @pl.when(z > 0)
            def _():
                left(o_ref, o_ref, c).start()
            @pl.when(z < n - 1)
            def _():
                right(o_ref, o_ref, c).start()
    def spread_step(c):
        r = root(c)
        @pl.when((z < r) & (z > 0))
        def _():
            left(o_ref, o_ref, c).wait_recv()
            left(o_ref, o_ref, c).start()
        @pl.when((z > r) & (z < n - 1))
        def _():
            right(o_ref, o_ref, c).wait_recv()
            right(o_ref, o_ref, c).start()

    def end_step(c, carry):
        r = root(c)
        @pl.when((z < r) & (z == 0))
        def _():
            left(o_ref, o_ref, c).wait_recv()
        @pl.when((z > r) & (z == n - 1))
        def _():
            right(o_ref, o_ref, c).wait_recv()
        return carry

    def sent(c, to_right, to_left):
        @pl.when(to_right & (z < n - 1))
        def _():
            right(o_ref, o_ref, c).wait_send()
        @pl.when(to_left & (z > 0))
        def _():
            left(o_ref, o_ref, c).wait_send()
    stages = [
        (0, forward_step, lambda c: sent(c, z < root(c), z > root(c))),
        (d1, root_step, lambda c: sent(c, z == root(c), z == root(c))),
        (d2, spread_step, lambda c: sent(c, z > root(c), z < root(c))),
    ]
    start_extra()
    if not forward:
        planned.append((6, back_tail))
    if full:
        fgot_own = pltpu.make_async_copy(f_ref, fgot.at[me], hl)
        fgot_own.start()
        for k in range(1, seq):
            small(k).start()
        fgot_own.wait()
        planned.append((7, end_small))
    if ng:
        g_start()
        planned.append((count, g_forward))
    if ns:
        s_start(3)
        for i, when in ((3, 2), (0, 3), (1, 5), (2, 7)):
            planned.append((when, functools.partial(s_middle, i)))
        if full:
            planned.append((min(13, count), b_start))

    def nth(i):
        return jnp.where(z <= low, i + 1 - 2 * lax.rem(i, 2), i)

    def body(t, carry):
        for lag, step_of, sent_of in stages:
            i = t - lag
            @pl.when((i >= window) & (i < count + window))
            def _():
                sent_of(nth(i - window))
            @pl.when((i >= 0) & (i < count))
            def _():
                step_of(nth(i))
        for when, run in planned:
            pl.when(t == when)(run)
        return carry
    lax.fori_loop(0, count + d2 + window, body, 0)
    for i in range(1 if full else 0, ns):
        s_final(i)
    lax.fori_loop(0, count, end_step, 0)
    if ng:
        g_end()
    s_drain()
    if full:
        b_end()
        end_shared()
        fo_ref[:, : sh.shape[1]] = sh[...]
    if forward:
        end_extra()
        size = x_ref.shape[0]
        square = jnp.concatenate([eo_ref[...], jnp.zeros((WIDE - 8, size), jnp.float32)], axis=0).T
        hidden_o[...] = base[...] + lax.rsqrt(square[:, 0:1] / inner_all + EPS) * o_ref[...]

        @pl.when(me < seq - 1)
        def _():
            tail_copy().start()

        @pl.when(me == 0)
        def _():
            tail_o[...] = jnp.zeros_like(tail_o)

        @pl.when(me > 0)
        def _():
            tail_copy().wait_recv()

        @pl.when(me < seq - 1)
        def _():
            tail_copy().wait_send()
    else:
        @pl.when(me < seq - 1)
        def _():
            tail_copy().wait_recv()
            last = pl.ds(x_ref.shape[0] - 8, 8)
            o_ref[last, :] = o_ref[last, :] + tailgot[...]

        @pl.when(me > 0)
        def _():
            tail_copy().wait_send()


def exchange(ins, cid, gathers=(), full=(), bc_loc=0, inner_all=0, layer=0, parts=16, order=(2, 5, 3)):
    n, seq = lax.axis_size("head"), lax.axis_size("seq")
    chips = seq // 2
    back = not inner_all
    ng, ns = len(gathers), 4 if back else 0
    base = ins[-1]
    rows, width = base.shape
    e_shape = (8, width) if back else ins[1].shape
    g_shapes = [g.shape[-2:] for g, _ in gathers]
    vm = lambda *shape: pltpu.VMEM(shape, jnp.float32)
    dma = pltpu.SemaphoreType.DMA
    scratch = [vm(rows, width)] * 2
    outs = []
    if back:
        inner, side = ins[6].shape[1], ins[5].shape[1]
        outs = [(width // seq, side)] + [(width // seq, inner)] * 3
        small = (full[1].shape[0] + 8 if full else 8, max(width, side + inner))
        shapes = [(rows, width)] + outs + ([(outs[0][0], 2 * bc_loc), small] if full else [small])
        spaces = [VM] * len(shapes)
        scratch += [vm(rows, width), vm(rows + 8, width), vm(8, width), vm(8, width), vm(8, width), vm(width, side), vm(width, inner), vm(width, inner)]
        if full:
            scratch += [vm(*small)]
    else:
        shapes = [(rows, width), e_shape] + [(seq * r, c) for r, c in g_shapes] + [(rows, width), (8, width)]
        spaces = [VM] * 2 + [HB] * ng + [VM] * 2
    scratch += [vm(n, *e_shape)] + [vm(chips, *o) for o in outs] * 2
    if full:
        shared, bc = (small[0], 2 * STATE), (outs[0][0], 2 * bc_loc)
        scratch += [vm(seq, *small), vm(n, *shared), vm(*shared), vm(n, *bc), vm(n, *bc)]
    scratch += [dma((parts,))] * 4 + [dma((n,))] * 2 + [dma] * 3
    if ng:
        scratch += [dma((ng, chips))] * 4 + [dma((ng,))]
    if ns:
        scratch += [dma((ns, chips))] * 4
    if full:
        scratch += [dma((seq,))] * 2 + [dma((n,))] * 2 + [dma] + [dma((n,))] * 2 + [dma]
    spec = (n, seq, tuple(at for _, at in gathers), ns, bc_loc, inner_all, rows // parts, order, (layer, min(BLOCK, rows)))
    return kernel_call(
        functools.partial(exchange_kernel, spec), "exchange", [f32(*s) for s in shapes],
        [*ins, *[g for g, _ in gathers], *full], scratch, cid=cid,
        specs=[VM] * len(ins) + [HB] * ng + [VM] * len(full), out_specs=spaces,
    )


def turned(array):
    rows, columns = array.shape
    up, across = -rows % WIDE, -columns % WIDE
    if across:
        array = jnp.concatenate([array, jnp.zeros((rows, across), jnp.float32)], axis=1)
    if up:
        array = jnp.concatenate([array, jnp.zeros((up, columns + across), jnp.float32)], axis=0)
    return array.T


def bookkeeping(me, lengths, block, masks_o, segrow_o, cmask_o, earlier_o, later_o):
    count = masks_o.shape[0]
    base = me * count

    def segment(position):
        start = jnp.int32(0)
        total = jnp.full(position.shape, -1, jnp.int32)
        for d in range(lengths.shape[0]):
            total = total + (position >= start).astype(jnp.int32)
            start = start + lengths[d]
        return total

    row = lax.broadcasted_iota(jnp.int32, masks_o.shape, 0)
    lane = lax.broadcasted_iota(jnp.int32, masks_o.shape, 1)
    first = row - lax.rem(row, block)
    margin = KERNEL - 1
    at = jnp.where(lane < margin, row - margin + lane, jnp.where(lane == 3, first - 1, jnp.where(lane == 4, first + block - 1, row)))
    seg = segment(base + at)
    own = segment(base + row)
    masks_o[...] = jnp.where(lane < 5, (seg == own).astype(jnp.float32), own.astype(jnp.float32))
    segrow_o[...] = segment(base + lax.broadcasted_iota(jnp.int32, segrow_o.shape, 1)).astype(jnp.float32)
    first = lax.broadcasted_iota(jnp.int32, cmask_o.shape, 0) * block
    cmask_o[...] = (segment(base + first - 1) == segment(base + first + block - 1)).astype(jnp.float32)
    place = lax.broadcasted_iota(jnp.int32, earlier_o.shape, 0)
    earlier_o[...] = (place < me).astype(jnp.float32)
    later_o[...] = (place > me).astype(jnp.float32)


def opening_kernel(n, seq, block, lengths, z_ref, x_ref, bc_ref, ck_ref, cb_ref, dt_ref, h_ref, cxk, cxb, dtb, alog, skip, *refs):
    wz_o, wx_o, side_o, own_o, tail_o, hp_o, cw_o, *books = refs[:12]
    bc_got, ck_got, cb_got, side, hs, hr, hl, ss, rs, fs, fr, ls, ts, tr = refs[12:]
    heads, layers, rows = dt_ref.shape
    z = lax.axis_index("head")
    me, chips, core, chip, sib = seq_place(seq)
    count = h_ref.shape[0]
    bar = pltpu.get_barrier_semaphore()
    for k in range(1, n):
        pl.semaphore_signal(bar, inc=1, device_id={"head": lax.rem(z + k, n)}, device_id_type=MESHID)
    for k in range(1, seq):
        pl.semaphore_signal(bar, inc=1, device_id={"seq": lax.rem(me + k, seq)}, device_id_type=MESHID)
    pl.semaphore_wait(bar, n - 1 + seq - 1)
    columns = [(bc_ref, bc_got), (ck_ref, ck_got), (cb_ref, cb_got)]

    def own(i):
        return pltpu.make_async_copy(columns[i][0], columns[i][1].at[z], hl.at[i])

    def head(i, k):
        return pltpu.make_async_remote_copy(src_ref=columns[i][0], dst_ref=columns[i][1].at[z], send_sem=hs.at[i, k], recv_sem=hr.at[i, k],
            device_id={"head": lax.rem(z + k, n)}, device_id_type=MESHID)

    srcs = [z_ref.at[0], x_ref.at[0], side]
    dsts = [wz_o, wx_o, side_o]
    number = len(srcs)

    def at(i, owner):
        return dsts[i].at[pl.ds(pl.multiple_of(owner * rows, 8), rows)]

    def back(k):
        return lax.rem(chip - k + chips, chips) * 2 + core

    def local(i):
        return pltpu.make_async_copy(srcs[i], at(i, me), ls.at[i])

    def across(i, k):
        return pltpu.make_async_remote_copy(src_ref=srcs[i], dst_ref=at(i, me), send_sem=ss.at[i, k], recv_sem=rs.at[i, k],
            device_id={"seq": lax.rem(chip + k, chips) * 2 + core}, device_id_type=MESHID)

    def over(i, k):
        return pltpu.make_async_remote_copy(src_ref=srcs[i] if k == 0 else at(i, back(k)), dst_ref=at(i, back(k)), send_sem=fs.at[i, k], recv_sem=fr.at[i, k],
            device_id={"seq": sib}, device_id_type=MESHID)

    def tail():
        return pltpu.make_async_remote_copy(src_ref=h_ref.at[pl.ds(count - 8, 8)], dst_ref=tail_o, send_sem=ts, recv_sem=tr,
            device_id={"seq": me + 1}, device_id_type=MESHID)

    def send(i):
        for k in range(1, chips):
            across(i, k).start()
        over(i, 0).start()
        local(i).start()

    for i in range(3):
        for k in range(1, n):
            head(i, k).start()
        own(i).start()

    @pl.when(me < seq - 1)
    def _():
        tail().start()

    @pl.when(me == 0)
    def _():
        tail_o[...] = jnp.zeros_like(tail_o)

    send(0)
    send(1)
    for i in range(3):
        own(i).wait()
        for k in range(1, n):
            head(i, k).wait()
    for l in range(layers):
        of_heads = turned(jnp.concatenate([dt_ref[h, l : l + 1, :] for h in range(heads)], axis=0))
        whole = jnp.concatenate([turned(jnp.concatenate([bc_got[p, l] for p in range(n)], axis=0))[:rows], of_heads[:rows]], axis=1)
        if l == 0:
            side[...] = whole
            send(2)
        else:
            own_o[(l - 1) * rows : l * rows, :] = whole
    inner = cxb.shape[1]
    for l in range(layers):
        taps = jnp.concatenate([cxk[l]] + [ck_got[p, l] for p in range(n)], axis=1)
        bias = jnp.concatenate([cxb[l : l + 1, :]] + [cb_got[p, l : l + 1, :] for p in range(n)], axis=1)
        cw_o[8 * l : 8 * l + 8, :] = jnp.concatenate([taps, bias, jnp.zeros((7 - KERNEL, inner + 2 * STATE), jnp.float32)], axis=0)
        heads_of = jnp.concatenate([dtb[l : l + 1, :], alog[l : l + 1, :], skip[l : l + 1, :], jnp.zeros((5, heads), jnp.float32)], axis=0)
        hp_o[8 * l : 8 * l + 8, :] = jnp.concatenate([heads_of, jnp.zeros((8, WIDE - heads), jnp.float32)], axis=1)
    bookkeeping(me, lengths, block, *books)
    pairs = [(i, k) for i in range(number) for k in range(1, chips)]
    for i, k in pairs:
        across(i, k).wait_recv()
        over(i, k).start()
    for i in range(number):
        for k in range(chips):
            over(i, k).wait()
        local(i).wait()
    for i, k in pairs:
        across(i, k).wait_send()

    @pl.when(me > 0)
    def _():
        tail().wait_recv()

    @pl.when(me < seq - 1)
    def _():
        tail().wait_send()


def opening(lengths, proj_z, proj_x, proj_bc, ck, cb, proj_dt, hidden, cxk, cxb, dtb, alog, skip, cid):
    n, seq = lax.axis_size("head"), lax.axis_size("seq")
    layers, rows, inner = proj_z.shape
    chips = seq // 2
    count, width = hidden.shape
    side = 2 * STATE + WIDE
    full = rows * seq
    dma = pltpu.SemaphoreType.DMA
    smem = pl.BlockSpec(memory_space=pltpu.SMEM)
    return pl.pallas_call(
        functools.partial(opening_kernel, n, seq, min(BLOCK, count)),
        out_shape=[f32(full, inner), f32(full, inner), f32(full, side), f32((layers - 1) * rows, side), f32(8, width),
                   f32(8 * layers, WIDE), f32(8 * layers, inner + 2 * STATE), f32(count, 8), f32(8, count), f32(8, WIDE), f32(seq, WIDE), f32(seq, WIDE)],
        in_specs=[smem, HB, HB, HB, HB, HB, VM, HB] + [VM] * 5,
        out_specs=[HB, HB, HB] + [VM] * 9,
        scratch_shapes=[pltpu.VMEM((n,) + a.shape, jnp.float32) for a in (proj_bc, ck, cb)] + [pltpu.VMEM((rows, side), jnp.float32)]
        + [dma((3, n))] * 2 + [dma((3,))] + [dma((3, chips))] * 4 + [dma((3,)), dma, dma],
        compiler_params=pltpu.CompilerParams(collective_id=cid, has_side_effects=True),
        name="opening",
    )(lengths, proj_z, proj_x, proj_bc, ck, cb, proj_dt, hidden, cxk, cxb, dtb, alog, skip)


def finish_kernel(n, inner_all, e, bcs, squares, hidden, half0, half1, grad, *refs):
    z = lax.axis_index("head")
    big = refs[:8]
    (hidden_o, grad_o, ngain_o, z_o, x_o, bc_o, dt_o, cxk_o, cxb_o, cbk_o, cbb_o, dtb_o, alog_o, skip_o, ggain_o, out_o) = refs[8:]
    half = half0.shape[0]
    size = hidden.shape[0]
    scale = lax.rsqrt(turned(squares[...])[:size, 0:1] / inner_all + EPS)
    hidden_o[0:half, :] = hidden[0:half, :] + scale[0:half] * half0[...]
    hidden_o[half:, :] = hidden[half:, :] + scale[half:] * half1[...]
    grad_o[...] = grad[...]
    inner, heads, bc_loc, rows = z_o.shape[2], dt_o.shape[0], bc_o.shape[1], bc_o.shape[2]
    bcs_t = turned(bcs[...])
    bc = 2 * STATE
    for l in range(2):
        side, gz, gx, gout = big[4 * l : 4 * l + 4]
        z_o[l], x_o[l], out_o[l] = gz[...], gx[...], gout[...]
        bc_o[l] = bcs_t[l * bc_loc : (l + 1) * bc_loc, :rows]
        of_heads = turned(side[:, bc:])
        for h in range(heads):
            dt_o[h, l : l + 1, :] = of_heads[h : h + 1, :rows]
        s = e[8 * l : 8 * l + 8, :]
        for i in range(ngain_o.shape[1] // bc):
            ngain_o[l : l + 1, i * bc : (i + 1) * bc] = s[5 + i : 6 + i, :bc]
        cxk_o[l] = s[0:KERNEL, bc : bc + inner]
        cxb_o[l : l + 1, :] = s[KERNEL : KERNEL + 1, bc : bc + inner]
        ggain_o[l : l + 1, :] = s[5:6, bc : bc + inner]
        mine = jnp.zeros((8, bc_loc), jnp.float32)
        for p in range(n):
            mine = jnp.where(z == p, s[:, p * bc_loc : (p + 1) * bc_loc], mine)
        cbk_o[l] = mine[0:KERNEL]
        cbb_o[l : l + 1, :] = mine[KERNEL : KERNEL + 1]
        last = s[:, -WIDE:]
        dtb_o[l : l + 1, :] = last[0:1, :heads]
        alog_o[l : l + 1, :] = last[1:2, :heads]
        skip_o[l : l + 1, :] = last[2:3, :heads]


def seq_place(n):
    me = lax.axis_index("seq")
    chips = n // 2
    core, chip = lax.rem(me, 2), me // 2
    return me, chips, core, chip, me + 1 - 2 * core


def body(
    hidden_in, grad_out, doc_lengths, norm_gain, proj_z, proj_x, proj_bc, proj_dt, conv_x_kernel, conv_x_bias,
    conv_bc_kernel, conv_bc_bias, dt_bias, a_log, skip_gain, gate_gain, proj_out,
):
    count, width = hidden_in.shape
    layers, rows_loc, inner = proj_z.shape
    bc_loc = proj_bc.shape[2]
    heads = proj_dt.shape[2]
    n_seq, n_head = lax.axis_size("seq"), lax.axis_size("head")
    inner_all = inner * n_head
    bc_all = 2 * STATE
    block = min(BLOCK, count)
    blocks = count // block
    mine = lax.axis_index("seq")

    (wz0, wx0, side0, side_own, tail, hp, cw, masks, segrow, cmask, earlier, following) = opening(
        doc_lengths, proj_z, proj_x, proj_bc.transpose(0, 2, 1), conv_bc_kernel, conv_bc_bias, proj_dt.transpose(2, 0, 1), hidden_in,
        conv_x_kernel, conv_x_bias, dt_bias, a_log, skip_gain, 2,
    )
    wz, wx, wside, wout = [wz0], [wx0], [side0], [proj_out]
    vm = lambda *shape: pltpu.VMEM(shape, jnp.float32)
    chips = n_seq // 2

    hidden = hidden_in
    saved = []
    more = count * 17 // 32 // 8 * 8
    for l in range(layers):
        final = l == layers - 1
        z, raw, dt, act, cum, carry, decays, e, mixed, entry, *rows = kernel_call(
            functools.partial(forward_kernel, l, heads, block, final, n_seq), "forward",
            [f32(count, inner), f32(count + 8, inner + bc_all), f32(count, WIDE), f32(count, inner + bc_all), f32(count, WIDE), f32(8, WIDE),
             f32(n_seq, WIDE), f32(8, count), f32(count, inner), f32(blocks * inner, STATE)]
            + ([f32(more, width), f32(count - more, width)] if final else [f32(count, width)])
            + ([f32(width, inner)] if l == 0 else []),
            [hidden, tail, norm_gain, wz[l], wx[l], wside[l], cw, hp, masks, segrow, cmask, earlier, gate_gain, wout[l], grad_out],
            [vm(count, width), vm(count, inner), vm(blocks * inner, STATE), vm(count, inner), vm(inner + 8, STATE), vm(n_seq, inner + 8, STATE)]
            + gather_sems(chips) * (2 if l == 0 else 1),
            cid=10 + 10 * l,
            specs=[VM] * 13 + [HB if l == 0 else VM, VM if final else HB],
        )
        if l == 0:
            wout[0] = rows.pop()
        hidden_l, tail_l = hidden, tail
        if final:
            last_rows = rows
            sums = grad_out
        else:
            sums, e, *weights, hidden, tail = exchange(
                [rows[0], e, hidden], 11 + 10 * l, inner_all=inner_all,
                gathers=[(proj_z, l + 1), (proj_x, l + 1), (proj_out, l + 1), (side_own[l * rows_loc : (l + 1) * rows_loc], None)],
            )
            for held, new in zip((wz, wx, wout, wside), weights):
                held.append(new)
        saved.append((hidden_l, tail_l, z, raw, dt, act, cum, carry, decays, mixed, entry, e, sums))

    grad = grad_out
    big = [None] * layers
    small, out_parts = [], []
    for l in reversed(range(layers)):
        final = l == layers - 1
        hidden_l, tail, z, raw, dt, act, cum, carry, decays, mixed, entry, e, sums = saved[l]
        dz, draw, ddt, dcw, dhp, dwout, dggain, *extra = kernel_call(
            functools.partial(backward_kernel, l, heads, block, inner_all, final, n_seq, n_head), "backward",
            [f32(count, inner), f32(count + 8, inner + bc_all), f32(count, WIDE), f32(8, inner + bc_all), f32(8, WIDE), f32(width, inner), f32(8, inner)]
            + [f32(8, count)] * (1 if final else 0),
            [grad, e, sums, act, cum, masks, carry, z, gate_gain, wout[l], mixed, entry, decays, following, raw, dt, segrow, cw, hp],
            [vm(count, inner), vm(count, inner), vm(count, WIDE), vm(count, STATE), vm(blocks * inner, STATE), vm(inner, STATE),
             vm(n_seq, inner, STATE), vm(count, inner + bc_all), vm(count, inner), vm(count, STATE)]
            + gather_sems(chips)
            + ([vm(n_head, 8, count)] + [pltpu.SemaphoreType.DMA((n_head,))] * 2 + [pltpu.SemaphoreType.DMA] if final else []),
            cid=12 + 10 * l,
        )
        if final:
            squares = extra[0]
            out_parts.append(lax.psum(last_rows[0], "head"))
        ins = [hidden_l, tail, norm_gain, wz[l], wx[l], wside[l], dz, draw, ddt, dcw, dhp, dggain, dwout, grad]
        if l > 0:
            grad, *big[l], smalls = exchange(ins, 14 + 10 * l, layer=l)
            late, grad, out_parts = lax.optimization_barrier((last_rows[1], grad, out_parts))
            out_parts.append(lax.psum(late, "head"))
        else:
            grad, *big[l], bcs, e = exchange(ins, 14, full=(big[1][0], smalls), bc_loc=bc_loc)
    outs = [
        (count, width), (count, width), (layers, width), proj_z.shape, proj_x.shape, (layers, bc_loc, rows_loc), (heads, layers, rows_loc), conv_x_kernel.shape,
        conv_x_bias.shape, conv_bc_kernel.shape, conv_bc_bias.shape, dt_bias.shape, a_log.shape, skip_gain.shape, gate_gain.shape, proj_out.shape,
    ]
    results = list(kernel_call(
        functools.partial(finish_kernel, n_head, inner_all), "finish", [f32(*o) for o in outs],
        [e, bcs, squares, hidden, *out_parts, grad, *big[0], *big[1]],
    ))
    results[5] = results[5].transpose(0, 2, 1)
    results[6] = results[6].transpose(1, 2, 0)
    return tuple(results)


def solution(mesh):
    in_specs = (
        P("seq", None),
        P("seq", None),
        P(),
        P(),
        P(None, "seq", "head"),
        P(None, "seq", "head"),
        P(None, "seq", "head"),
        P(None, "seq", "head"),
        P(None, None, "head"),
        P(None, "head"),
        P(None, None, "head"),
        P(None, "head"),
        P(None, "head"),
        P(None, "head"),
        P(None, "head"),
        P(None, "head"),
        P(None, "seq", "head"),
    )
    out_specs = (
        P("seq", None),
        P("seq", None),
        P(),
        P(None, "seq", "head"),
        P(None, "seq", "head"),
        P(None, "seq", "head"),
        P(None, "seq", "head"),
        P(None, None, "head"),
        P(None, "head"),
        P(None, None, "head"),
        P(None, "head"),
        P(None, "head"),
        P(None, "head"),
        P(None, "head"),
        P(None, "head"),
        P(None, "seq", "head"),
    )
    return jax.shard_map(body, mesh=mesh, in_specs=in_specs, out_specs=out_specs, check_vma=False)
```

```python
import functools

import jax
import jax.numpy as jnp
from jax import lax
from jax.experimental import pallas as pl
from jax.experimental.pallas import tpu as pltpu
from jax.sharding import PartitionSpec as P

STATE = 128
KERNEL = 4
BLOCK = 256
MESHID = pl.DeviceIdType.MESH
VM = pl.BlockSpec(memory_space=pltpu.VMEM)
HB = pl.BlockSpec(memory_space=pl.ANY)


EPS = 1e-05
NEG_FILL = -1e30
EXACT = lax.Precision.HIGHEST
FAST = lax.Precision.HIGH
WIDE = 128


def mm(left, right, dims=((1,), (0,)), precision=FAST):
    return lax.dot_general(left, right, (dims, ((), ())), precision=precision, preferred_element_type=jnp.float32)


ROWS_T = ((1,), (1,))
COLS_T = ((0,), (0,))


def sigmoid(v):
    return 1.0 / (1.0 + jnp.exp(-v))


def softplus(v):
    small = jnp.exp(-jnp.abs(v))
    one = 1.0 + small
    exact = jnp.where(one == 1.0, small, small * jnp.log(one) / jnp.where(one == 1.0, 1.0, one - 1.0))
    return jnp.maximum(v, 0.0) + exact


def spread_heads(per_head, heads, dim):
    rows = per_head.shape[0]
    return jnp.concatenate([jnp.broadcast_to(per_head[:, h : h + 1], (rows, dim)) for h in range(heads)], axis=1)


def scaled_rows(state, factors, heads):
    dim = state.shape[0] // heads
    return jnp.concatenate([state[h * dim : (h + 1) * dim] * factors[:, h : h + 1] for h in range(heads)], axis=0)


def head_sums(wide, heads):
    width = wide.shape[1]
    dim = width // heads
    row = lax.broadcasted_iota(jnp.int32, (width, WIDE), 0)
    col = lax.broadcasted_iota(jnp.int32, (width, WIDE), 1)
    pick = ((row >= col * dim) & (row < (col + 1) * dim)).astype(jnp.float32)
    return mm(wide, pick, precision=EXACT)


def lower_of(rows):
    return lax.broadcasted_iota(jnp.int32, (rows, rows), 0) >= lax.broadcasted_iota(jnp.int32, (rows, rows), 1)


def normed_of(h, gain):
    r = lax.rsqrt(jnp.mean(h * h, axis=1, keepdims=True) + EPS)
    return h * r * gain


def conv_total(raw_ref, cw_ref, masks_ref, at, rows):
    total = cw_ref[KERNEL : KERNEL + 1, :] + cw_ref[KERNEL - 1 : KERNEL, :] * raw_ref[8 + at : 8 + at + rows, :]
    for k in range(KERNEL - 1):
        first = 8 + at - (KERNEL - 1) + k
        total = total + cw_ref[k : k + 1, :] * (raw_ref[first : first + rows, :] * masks_ref[at : at + rows, k : k + 1])
    return total


def gather_ops(place, src, slot, sems):
    me, chips, core, chip, sib = place
    ss, rs, fs, fr, ls = sems

    def back(k):
        return lax.rem(chip - k + chips, chips) * 2 + core

    def across(k):
        return pltpu.make_async_remote_copy(src_ref=src, dst_ref=slot(me), send_sem=ss.at[k], recv_sem=rs.at[k],
            device_id={"seq": lax.rem(chip + k, chips) * 2 + core}, device_id_type=MESHID)

    def over(k):
        return pltpu.make_async_remote_copy(src_ref=src if k == 0 else slot(back(k)), dst_ref=slot(back(k)), send_sem=fs.at[k], recv_sem=fr.at[k],
            device_id={"seq": sib}, device_id_type=MESHID)

    local = pltpu.make_async_copy(src, slot(me), ls)

    def start():
        for k in range(1, chips):
            across(k).start()
        over(0).start()
        local.start()

    def forward():
        for k in range(1, chips):
            across(k).wait_recv()
            over(k).start()

    def end():
        for k in range(chips):
            over(k).wait()
        for k in range(1, chips):
            across(k).wait_send()
        local.wait()

    return start, forward, end


def gather_sems(chips):
    return [pltpu.SemaphoreType.DMA((chips,))] * 4 + [pltpu.SemaphoreType.DMA]


def signal_peers(place, heads):
    me, chips, core, chip, sib = place
    bar = pltpu.get_barrier_semaphore()
    pl.semaphore_signal(bar, inc=1, device_id={"seq": sib}, device_id_type=MESHID)
    for k in range(1, chips):
        pl.semaphore_signal(bar, inc=1, device_id={"seq": lax.rem(chip + k, chips) * 2 + core}, device_id_type=MESHID)
    if heads:
        z = lax.axis_index("head")
        for k in range(1, heads):
            pl.semaphore_signal(bar, inc=1, device_id={"head": lax.rem(z + k, heads)}, device_id_type=MESHID)
        return chips + heads - 1
    return chips


def forward_kernel(layer, heads, block, last_layer, n_seq, hidden, tail, gains, wz, wx, wside, cw, hp, masks, segrow, cmask, before, ggains, wout_in, grad, *refs):
    refs = list(refs)
    cw, hp = cw.at[pl.ds(8 * layer, 8)], hp.at[pl.ds(8 * layer, 8)]
    z_o, raw_o, dt_o, act_o, cum_o, carry_o, decays_o, e_o, mixed_o, entry_o, *rows_o = refs[: 12 if last_layer else 11]
    first = layer == 0
    refs = refs[12 if last_layer else 11 :]
    wout = refs.pop(0) if first else wout_in
    nrm, lv, st, y, dev, pieces = refs[:6]
    refs = refs[6:]
    place = seq_place(n_seq)
    expected = signal_peers(place, 0)
    start, forward, end = gather_ops(place, dev, lambda owner: pieces.at[owner], refs[:5])
    if first:
        rows_loc = wout_in.shape[1]
        w_start, w_forward, w_end = gather_ops(
            place, wout_in.at[0], lambda owner: wout.at[pl.ds(pl.multiple_of(owner * rows_loc, 8), rows_loc)], refs[5:10]
        )
    count, inner = z_o.shape
    blocks = count // block
    dim = inner // heads
    wide_bc = 2 * STATE
    gain = gains[layer : layer + 1, :]
    ggain = ggains[layer : layer + 1, :]
    if first:
        pl.semaphore_wait(pltpu.get_barrier_semaphore(), expected)
        w_start()
    t = normed_of(tail[...], gain)
    raw_o[0:8, :inner] = mm(t, wx[...])
    raw_o[0:8, inner:] = mm(t, wside[:, :wide_bc])
    lower = lower_of(block)
    lower_f = lower.astype(jnp.float32)
    carry_o[...] = jnp.zeros_like(carry_o)
    state = decay = None

    def step_of(own):
        return softplus(dt_o[own, :] + hp[0:1, :])

    for b in range(blocks):
        at = b * block
        own = slice(at, at + block)
        n = normed_of(hidden[own, :], gain)
        nrm[own, :] = n
        raw_o[8 + at : 8 + at + block, :inner] = mm(n, wx[...])
        side = mm(n, wside[...])
        raw_o[8 + at : 8 + at + block, inner:] = side[:, :wide_bc]
        dt_o[own, :] = side[:, wide_bc:]
        total = conv_total(raw_o, cw, masks, at, block)
        act = total * sigmoid(total)
        act_o[own, :] = act
        step = step_of(own)
        cum = mm(lower_f, -step * jnp.exp(hp[1:2, :]), precision=EXACT)
        cum_o[own, :] = cum
        last = cum[block - 1 : block, :]
        leave = step * jnp.exp(last - cum) * masks[own, 4:5]
        states = mm(act[:, :inner] * spread_heads(leave, heads, dim), act[:, inner : inner + STATE], COLS_T)
        st[b * inner : (b + 1) * inner, :] = states
        carry = jnp.exp(last) * cmask[b : b + 1, :]
        carry_o[b : b + 1, :] = carry
        state = states if b == 0 else scaled_rows(state, carry, heads) + states
        decay = carry if b == 0 else decay * carry
    dev[:inner, :] = state
    dev[inner:, :] = jnp.broadcast_to(decay, (8, WIDE))
    if first:
        w_forward()
    else:
        pl.semaphore_wait(pltpu.get_barrier_semaphore(), expected)
    start()
    for b in range(blocks):
        at = b * block
        own = slice(at, at + block)
        z = mm(nrm[own, :], wz[...])
        z_o[own, :] = z
        lv[own, :] = z * sigmoid(z)
        values, bm, cm = act_o[own, :inner], act_o[own, inner : inner + STATE], act_o[own, inner + STATE :]
        step, cum = step_of(own), cum_o[own, :]
        cum_t = cum.T
        allowed = lower & (masks[own, 5:6] == segrow[0:1, own])
        scores = mm(cm, bm, ROWS_T)
        ys = []
        for h in range(heads):
            v = values[:, h * dim : (h + 1) * dim]
            spans = cum[:, h : h + 1] - cum_t[h : h + 1, :]
            s = jnp.exp(jnp.where(allowed, spans, NEG_FILL)) * scores
            ys.append(mm(s, v * step[:, h : h + 1]) + hp[2:3, h : h + 1] * v)
        y[own, :] = jnp.concatenate(ys, axis=1)
    forward()
    if first:
        w_end()
    end()
    state = jnp.zeros((inner, STATE), jnp.float32)
    for j in range(n_seq):
        decay = pieces[j, inner : inner + 1, :]
        decays_o[j : j + 1, :] = decay
        later = scaled_rows(state, decay, heads) + pieces[j, :inner, :]
        state = jnp.where(before[j : j + 1, :] > 0.5, later, state)
    for b in range(blocks):
        at = b * block
        own = slice(at, at + block)
        entry_o[b * inner : (b + 1) * inner, :] = state
        enter = jnp.exp(cum_o[own, :]) * masks[own, 3:4]
        mixed = y[own, :] + spread_heads(enter, heads, dim) * mm(act_o[own, inner + STATE :], state, ROWS_T)
        mixed_o[own, :] = mixed
        gated = mixed * lv[own, :]
        out = mm(gated * ggain, wout[...], ROWS_T)
        done = 0
        for part in rows_o:
            low, high = max(at, done), min(at + block, done + part.shape[0])
            if low < high:
                part[low - done : high - done, :] = out[low - at : high - at]
            done = done + part.shape[0]
        squares = jnp.sum(gated * gated, axis=1, keepdims=True)
        if last_layer:
            dots = jnp.sum(grad[own, :] * out, axis=1, keepdims=True)
        else:
            dots = jnp.zeros_like(squares)
        lane = lax.broadcasted_iota(jnp.int32, (block, WIDE), 1)
        both = jnp.where(lane == 0, squares, jnp.where(lane == 1, dots, 0.0))
        e_o[:, own] = both.T[0:8, :]
        state = scaled_rows(state, carry_o[b : b + 1, :], heads) + st[b * inner : (b + 1) * inner, :]


def backward_kernel(layer, heads, block, inner_all, last_layer, n_seq, n_head, grad, e, sums, act, cum, masks, carry, z, ggains, wout, mixed, entry, decays, after, raw, dt, segrow, cw, hp, *refs):
    refs = list(refs)
    cw, hp = cw.at[pl.ds(8 * layer, 8)], hp.at[pl.ds(8 * layer, 8)]
    dz_o, draw_o, ddt_o, dcw_o, dhp_o, dwout_o, dgg_o = refs[:7]
    refs = refs[7:]
    if last_layer:
        esum = refs.pop(0)
    wide, dmix, de, dc, dentry, dstate, gpieces, dtot, dxi, dbi = refs[:10]
    refs = refs[10:]
    place = seq_place(n_seq)
    expected = signal_peers(place, n_head if last_layer else 0)
    start, forward, end = gather_ops(place, dstate, lambda owner: gpieces.at[owner], refs[:5])
    if last_layer:
        egot, es, er, el = refs[5:9]
        zi = lax.axis_index("head")
        near = pltpu.make_async_copy(e, egot.at[zi], el)
        far = [
            pltpu.make_async_remote_copy(src_ref=e, dst_ref=egot.at[zi], send_sem=es.at[k], recv_sem=er.at[k],
                device_id={"head": lax.rem(zi + k, n_head)}, device_id_type=MESHID)
            for k in range(1, n_head)
        ]
        pl.semaphore_wait(pltpu.get_barrier_semaphore(), expected)
        near.start()
        for copy in far:
            copy.start()
    count, inner = z.shape
    blocks = count // block
    dim = inner // heads
    ggain = ggains[layer : layer + 1, :]
    for b in range(blocks):
        own = slice(b * block, (b + 1) * block)
        wide[own, :] = mm(grad[own, :], wout[...])
    if last_layer:
        near.wait()
        for copy in far:
            copy.wait()
        total = egot[0]
        for k in range(1, n_head):
            total = total + egot[k]
        esum[...] = total
        e = esum

    def columns(own):
        return jnp.concatenate([e[:, own], jnp.zeros((WIDE - 8, block), jnp.float32)], axis=0).T

    def enter_of(own):
        return spread_heads(jnp.exp(cum[own, :]) * masks[own, 3:4], heads, dim)

    ggain_sum = jnp.zeros((1, inner), jnp.float32)
    for b in range(blocks):
        own = slice(b * block, (b + 1) * block)
        et = columns(own)
        scale = lax.rsqrt(et[:, 0:1] / inner_all + EPS)
        gs = et[:, 1:2] if last_layer else jnp.sum(grad[own, :] * sums[own, :], axis=1, keepdims=True)
        dsq = gs * (-0.5 / inner_all) * scale * scale * scale
        dgg = scale * wide[own, :]
        zz = z[own, :]
        sg = sigmoid(zz)
        sil = zz * sg
        mx = mixed[own, :]
        gated = mx * sil
        ggain_sum = ggain_sum + jnp.sum(dgg * gated, axis=0, keepdims=True)
        dgated = dgg * ggain + 2.0 * dsq * gated
        dm = dgated * sil
        dmix[own, :] = dm
        dz_o[own, :] = dgated * mx * (sg * (1.0 + zz * (1.0 - sg)))
        wide[own, :] = scale * (gated * ggain)
        dentry[b * inner : (b + 1) * inner, :] = mm(dm * enter_of(own), act[own, inner + STATE :], COLS_T)
    dgg_o[...] = jnp.broadcast_to(ggain_sum, dgg_o.shape)
    g = dentry[(blocks - 1) * inner :, :]
    for b in range(blocks - 2, -1, -1):
        g = dentry[b * inner : (b + 1) * inner, :] + scaled_rows(g, carry[b : b + 1, :], heads)
    dstate[...] = g
    if not last_layer:
        pl.semaphore_wait(pltpu.get_barrier_semaphore(), expected)
    start()
    lower = lower_of(block)
    lower_f = lower.astype(jnp.float32)
    pad = jnp.zeros((block, WIDE - heads), jnp.float32)
    for b in range(blocks):
        at = b * block
        own = slice(at, at + block)
        part = mm(grad[own, :], wide[own, :], COLS_T)
        if b == 0:
            dwout_o[...] = part
        else:
            dwout_o[...] += part
        values, bm, cm = act[own, :inner], act[own, inner : inner + STATE], act[own, inner + STATE :]
        en = entry[b * inner : (b + 1) * inner, :]
        dread = dmix[own, :] * enter_of(own)
        step = softplus(dt[own, :] + hp[0:1, :])
        cum_b = cum[own, :]
        cum_t = cum_b.T
        allowed = lower & (masks[own, 5:6] == segrow[0:1, own])
        scores = mm(cm, bm, ROWS_T)
        dscores = jnp.zeros((block, block), jnp.float32)
        dxs, rowsums, colsums = [], [], []
        for h in range(heads):
            cut = slice(h * dim, (h + 1) * dim)
            x = values[:, cut] * step[:, h : h + 1]
            dy = dmix[own, cut]
            spans = cum_b[:, h : h + 1] - cum_t[h : h + 1, :]
            decay = jnp.exp(jnp.where(allowed, spans, NEG_FILL))
            s = decay * scores
            ds = mm(dy, x, ROWS_T)
            dscores = dscores + ds * decay
            dspan = ds * s
            rowsums.append(jnp.sum(dspan, axis=1, keepdims=True))
            colsums.append(jnp.sum(dspan, axis=0, keepdims=True))
            dxs.append(mm(s, dy, COLS_T))
        rowsum = jnp.concatenate(rowsums + [pad], axis=1)
        colsum = jnp.concatenate(colsums + [jnp.zeros((WIDE - heads, block), jnp.float32)], axis=0).T
        de[own, :] = head_sums(dread * mm(cm, en, ROWS_T), heads) + rowsum - colsum
        dxi[own, :] = jnp.concatenate(dxs, axis=1)
        dc[own, :] = mm(dread, en) + mm(dscores, bm)
        dbi[own, :] = mm(dscores, cm, COLS_T)
        if b == 0:
            forward()
    end()
    g = jnp.zeros((inner, STATE), jnp.float32)
    for j in range(n_seq - 1, -1, -1):
        later = scaled_rows(g, decays[j : j + 1, :], heads) + gpieces[j]
        g = jnp.where(after[j : j + 1, :] > 0.5, later, g)
    sub = lax.broadcasted_iota(jnp.int32, (block, WIDE), 0)
    a_exp = jnp.exp(hp[1:2, :])
    bias_sum = alog_sum = skip_sum = jnp.zeros((1, WIDE), jnp.float32)
    for b in range(blocks - 1, -1, -1):
        at = b * block
        own = slice(at, at + block)
        values, bm = act[own, :inner], act[own, inner : inner + STATE]
        shifted = dt[own, :] + hp[0:1, :]
        step = softplus(shifted)
        step_wide = spread_heads(step, heads, dim)
        cum_b = cum[own, :]
        last = cum_b[block - 1 : block, :]
        leave = spread_heads(jnp.exp(last - cum_b) * masks[own, 4:5], heads, dim)
        carry_b = carry[b : b + 1, :]
        ge = g * entry[b * inner : (b + 1) * inner, :]
        dcs = [jnp.sum(jnp.sum(ge[h * dim : (h + 1) * dim], axis=0, keepdims=True), axis=1, keepdims=True) for h in range(heads)]
        dcarry = jnp.concatenate(dcs + [jnp.zeros((1, WIDE - heads), jnp.float32)], axis=1)
        dw = mm(bm, g, ROWS_T) * leave
        dx = dxi[own, :] + dw
        x = values * step_wide
        dleave = head_sums(dw * x, heads)
        dlast = jnp.sum(dleave, axis=0, keepdims=True) + dcarry * carry_b
        dcum = de[own, :] - dleave + jnp.where(sub == block - 1, dlast, 0.0)
        dld = mm(lower_f, dcum, COLS_T, EXACT)
        ddt = (head_sums(dx * values, heads) - dld * a_exp) * sigmoid(shifted)
        alog_sum = alog_sum - jnp.sum(dld * step, axis=0, keepdims=True) * a_exp
        ddt_o[own, :] = ddt
        bias_sum = bias_sum + jnp.sum(ddt, axis=0, keepdims=True)
        dy = dmix[own, :]
        skip_sum = skip_sum + jnp.sum(head_sums(dy * values, heads), axis=0, keepdims=True)
        total = conv_total(raw, cw, masks, at, block)
        sg = sigmoid(total)
        dsil = sg * (1.0 + total * (1.0 - sg))
        dtot[own, :inner] = (dx * step_wide + dy * spread_heads(hp[2:3, :], heads, dim)) * dsil[:, :inner]
        dtot[own, inner : inner + STATE] = (dbi[own, :] + mm(x * leave, g)) * dsil[:, inner : inner + STATE]
        dtot[own, inner + STATE :] = dc[own, :] * dsil[:, inner + STATE :]
        g = dentry[b * inner : (b + 1) * inner, :] + scaled_rows(g, carry_b, heads)
    dhp_o[...] = jnp.concatenate([bias_sum, alog_sum, skip_sum, jnp.zeros((5, WIDE), jnp.float32)], axis=0)
    conv_back(dtot, raw, masks, cw, draw_o, dcw_o)


def conv_back(dtot, raw, masks, cw, draw_o, dcw_o):
    count = dtot.shape[0]
    dall = dtot[...]
    draw_o[0:8, :] = jnp.zeros_like(draw_o[0:8, :])
    draw_o[8:, :] = cw[KERNEL - 1 : KERNEL, :] * dall
    dk = []
    for k in range(KERNEL - 1):
        kept = dall * masks[:, k : k + 1]
        first = 8 - (KERNEL - 1) + k
        dk.append(jnp.sum(kept * raw[first : first + count, :], axis=0, keepdims=True))
        draw_o[first : first + count, :] = draw_o[first : first + count, :] + cw[k : k + 1, :] * kept
    dk.append(jnp.sum(dall * raw[8:, :], axis=0, keepdims=True))
    dk.append(jnp.sum(dall, axis=0, keepdims=True))
    dcw_o[...] = jnp.concatenate(dk + [jnp.zeros((7 - KERNEL, dall.shape[1]), jnp.float32)], axis=0)


def f32(*shape):
    return jax.ShapeDtypeStruct(shape, jnp.float32)


def kernel_call(kernel, name, outs, args, scratch=(), cid=None, specs=None, out_specs=None):
    params = {} if cid is None else dict(collective_id=cid, has_side_effects=True)
    return pl.pallas_call(
        kernel,
        out_shape=outs,
        in_specs=specs or [VM] * len(args),
        out_specs=out_specs or [VM] * len(outs),
        scratch_shapes=list(scratch),
        cost_estimate=pl.CostEstimate(flops=1, bytes_accessed=1, transcendentals=0),
        compiler_params=pltpu.CompilerParams(vmem_limit_bytes=56 * 1024 * 1024, **params),
        name=name,
    )(*args)


def greet(peers, axis):
    bar = pltpu.get_barrier_semaphore()
    for p in peers:
        pl.semaphore_signal(bar, inc=1, device_id={axis: p}, device_id_type=MESHID)
    pl.semaphore_wait(bar, len(peers))


def exchange_kernel(spec, *refs):
    n, seq, ats, ns, bc_loc, inner_all, step, (d1, d2, window), (layer, block) = spec
    ng = len(ats)
    forward = inner_all > 0
    full = bc_loc > 0
    refs = list(refs)

    def take(number):
        out = refs[:number]
        del refs[:number]
        return out

    if forward:
        x_ref, e_ref, base = take(3)
    else:
        hidden, tail, gains, wz, wx, wside, dz, draw, ddt, dcw, dhp, dggain, dwout, base = take(14)
    gx = take(ng)
    if full:
        sidex, earlier = take(2)
    o_ref = take(1)[0]
    if forward:
        eo_ref = take(1)[0]
    go, so = take(ng), take(ns)
    if forward:
        hidden_o, tail_o = take(2)
    elif full:
        bco, fo_ref = take(2)
    else:
        f_ref = take(1)[0]
    inl, inr = take(2)
    if not forward:
        x_ref, nrm, e_ref, eo_ref, tailgot, dwside, dwz, dwx = take(8)
        sx = [dwside, dwz, dwx, dwout]
    if full:
        f_ref = take(1)[0]
    egot, mids, gots = take(1)[0], take(ns), take(ns)
    if full:
        fgot, shgot, sh, bcs, bcgot = take(5)
    sl, sr, rl, rr, es, er, el, ts, tr = take(9)
    if ng:
        gs, gr, gfs, gfr, gl = take(5)
    if ns:
        cs, cr, ss, rs = take(4)
    if full:
        fs, fr, bs, br, bl, hs, hr, hl = take(8)
    z = lax.axis_index("head")
    me, chips, core, chip, sib = seq_place(seq)
    count = x_ref.shape[0] // step
    bar = pltpu.get_barrier_semaphore()
    for k in range(1, n):
        pl.semaphore_signal(bar, inc=1, device_id={"head": lax.rem(z + k, n)}, device_id_type=MESHID)
    for k in range(1, seq):
        pl.semaphore_signal(bar, inc=1, device_id={"seq": lax.rem(me + k, seq)}, device_id_type=MESHID)
    planned = []
    if not forward:
        inner = dz.shape[1]
        wide_bc = 2 * STATE
        gain = gains[layer : layer + 1, :]

        def back_norm(h, dn):
            r = lax.rsqrt(jnp.mean(h * h, axis=1, keepdims=True) + EPS)
            hr = h * r
            g = dn * gain
            return r * (g - hr * jnp.mean(g * hr, axis=1, keepdims=True)), jnp.sum(dn * hr, axis=0, keepdims=True), hr * gain

        dr = draw[0:8, :]
        dn = mm(dr[:, :inner], wx[...], ROWS_T) + mm(dr[:, inner:], wside[:, :wide_bc], ROWS_T)
        e_ref[...], dgain, nrm[0:8, :] = back_norm(tail[...], dn)
        tokens = dz.shape[0]
        cuts = [slice(b * block, (b + 1) * block) for b in range(tokens // block)]
        shifted_cuts = [slice(8 + c.start, 8 + c.stop) for c in cuts]

        def side_of(c, d):
            return jnp.concatenate([draw[d, inner:], ddt[c, :]], axis=1)

        for c, d in zip(cuts, shifted_cuts):
            dn = mm(dz[c, :], wz[...], ROWS_T) + mm(draw[d, :inner], wx[...], ROWS_T) + mm(side_of(c, d), wside[...], ROWS_T)
            x_ref[c, :], dg, nrm[d, :] = back_norm(hidden[c, :], dn)
            dgain = dgain + dg
        f_ref[0:8, :] = jnp.zeros((8, f_ref.shape[1]), jnp.float32)
        f_ref[0 : KERNEL + 1, :wide_bc] = dcw[0 : KERNEL + 1, inner:]
        f_ref[0 : KERNEL + 1, wide_bc : wide_bc + inner] = dcw[0 : KERNEL + 1, :inner]
        f_ref[0:3, -WIDE:] = dhp[0:3, :]
        f_ref[5:6, wide_bc : wide_bc + inner] = dggain[0:1, :]
        for i in range(hidden.shape[1] // wide_bc):
            f_ref[5 + i : 6 + i, :wide_bc] = dgain[:, i * wide_bc : (i + 1) * wide_bc]
        if full:
            f_ref[8:, :] = earlier[...]

        def side_grads():
            dwside[:, :wide_bc] = mm(nrm[0:8, :], draw[0:8, inner:], COLS_T)
            dwside[:, wide_bc:] = jnp.zeros_like(dwside[:, wide_bc:])
            for c, d in zip(cuts, shifted_cuts):
                dwside[...] += mm(nrm[d, :], side_of(c, d), COLS_T)
            s_start(0)

        def z_grads():
            dwz[...] = mm(nrm[8:, :], dz[...], COLS_T)
            s_start(1)

        def x_grads():
            dwx[...] = mm(nrm[0:8, :], draw[0:8, :inner], COLS_T) + mm(nrm[8:, :], draw[8:, :inner], COLS_T)
            s_start(2)

        planned = [(1, side_grads), (3, z_grads), (5, x_grads)]
    pl.semaphore_wait(bar, n - 1 + seq - 1)

    def head_sum(src, got, dst, send, recv, near):
        own = pltpu.make_async_copy(src, got.at[z], near)
        far = [
            pltpu.make_async_remote_copy(src_ref=src, dst_ref=got.at[z], send_sem=send.at[k], recv_sem=recv.at[k],
                device_id={"head": lax.rem(z + k, n)}, device_id_type=MESHID)
            for k in range(1, n)
        ]

        def start():
            own.start()
            for copy in far:
                copy.start()

        def end():
            own.wait()
            for copy in far:
                copy.wait()
            total = got[0]
            for k in range(1, n):
                total = total + got[k]
            dst[...] = total

        return start, end

    start_extra, end_extra = head_sum(e_ref, egot, eo_ref, es, er, el)

    def tail_copy():
        if forward:
            return pltpu.make_async_remote_copy(src_ref=hidden_o.at[pl.ds(x_ref.shape[0] - 8, 8)], dst_ref=tail_o, send_sem=ts, recv_sem=tr,
                device_id={"seq": me + 1}, device_id_type=MESHID)
        return pltpu.make_async_remote_copy(src_ref=eo_ref, dst_ref=tailgot, send_sem=ts, recv_sem=tr,
            device_id={"seq": me - 1}, device_id_type=MESHID)

    def back_tail():
        end_extra()

        @pl.when(me > 0)
        def _():
            tail_copy().start()

    if full:
        start_shared, end_shared = head_sum(sh, shgot, sh, hs, hr, hl)

    def small(k):
        return pltpu.make_async_remote_copy(src_ref=f_ref, dst_ref=fgot.at[me], send_sem=fs.at[k], recv_sem=fr.at[k],
            device_id={"seq": lax.rem(me + k, seq)}, device_id_type=MESHID)

    def end_small():
        for k in range(1, seq):
            small(k).wait()
        total = fgot[0]
        for k in range(1, seq):
            total = total + fgot[k]
        fo_ref[...] = total
        sh[...] = total[:, : sh.shape[1]]
        start_shared()

    def peer(k):
        return {"seq": lax.rem(chip + k, chips) * 2 + core}

    def source(i):
        return gx[i] if ats[i] is None else gx[i].at[ats[i]]

    def g_at(i, owner):
        rows = go[i].shape[0] // seq
        return go[i].at[pl.ds(pl.multiple_of(owner * rows, 8), rows)]

    def back(k):
        return lax.rem(chip - k + chips, chips) * 2 + core

    def g_local(i):
        return pltpu.make_async_copy(source(i), g_at(i, me), gl.at[i])

    def g_across(i, k):
        return pltpu.make_async_remote_copy(src_ref=source(i), dst_ref=g_at(i, me), send_sem=gs.at[i, k], recv_sem=gr.at[i, k],
            device_id=peer(k), device_id_type=MESHID)

    def g_over(i, k):
        return pltpu.make_async_remote_copy(src_ref=source(i) if k == 0 else g_at(i, back(k)), dst_ref=g_at(i, back(k)),
            send_sem=gfs.at[i, k], recv_sem=gfr.at[i, k], device_id={"seq": sib}, device_id_type=MESHID)

    g_pairs = [(i, k) for k in range(1, chips) for i in range(ng)]

    def g_start():
        for i, k in g_pairs:
            g_across(i, k).start()
        for i in range(ng):
            g_over(i, 0).start()
            g_local(i).start()

    def g_forward():
        for i, k in g_pairs:
            g_across(i, k).wait_recv()
            g_over(i, k).start()

    def g_end():
        for i in range(ng):
            for k in range(chips):
                g_over(i, k).wait()
            g_local(i).wait()
        for i, k in g_pairs:
            g_across(i, k).wait_send()

    def block(i, k, c):
        rows = so[i].shape[0]
        return pl.ds(pl.multiple_of((lax.rem(chip + k, chips) * 2 + c) * rows, 8), rows)

    def s_over(i, k):
        return pltpu.make_async_remote_copy(src_ref=sx[i].at[block(i, k, 1 - core)], dst_ref=mids[i].at[k], send_sem=cs.at[i, k], recv_sem=cr.at[i, k],
            device_id={"seq": sib}, device_id_type=MESHID)

    def s_across(i, k):
        return pltpu.make_async_remote_copy(src_ref=mids[i].at[k], dst_ref=gots[i].at[k], send_sem=ss.at[i, k], recv_sem=rs.at[i, k],
            device_id=peer(k), device_id_type=MESHID)

    def s_start(i):
        for k in range(chips):
            s_over(i, k).start()

    def s_middle(i):
        for k in list(range(1, chips)) + [0]:
            s_over(i, k).wait_recv()
            mids[i][k] = mids[i][k] + sx[i][block(i, k, core), :]
            if k:
                s_across(i, k).start()

    def s_final(i):
        total = mids[i][0]
        for k in range(1, chips):
            s_across(i, k).wait_recv()
            total = total + gots[i][k]
        so[i][...] = total

    def s_drain():
        for i in range(ns):
            for k in range(chips):
                s_over(i, k).wait_send()
                if k:
                    s_across(i, k).wait_send()

    def b_own():
        return pltpu.make_async_copy(bcs.at[z], bcgot.at[z], bl)

    def b_across(k):
        to = lax.rem(z + k, n)
        return pltpu.make_async_remote_copy(src_ref=bcs.at[to], dst_ref=bcgot.at[z], send_sem=bs.at[k], recv_sem=br.at[k],
            device_id={"head": to}, device_id_type=MESHID)

    def b_start():
        s_final(0)
        for p in range(n):
            cut = slice(p * bc_loc, (p + 1) * bc_loc)
            bcs[p] = jnp.concatenate([so[0][:, cut], sidex[:, cut]], axis=1)
        b_own().start()
        for k in range(1, n):
            b_across(k).start()

    def b_end():
        b_own().wait()
        for k in range(1, n):
            b_across(k).wait()
        total = bcgot[0]
        for k in range(1, n):
            total = total + bcgot[k]
        bco[...] = total

    low = (n - 1) // 2
    def rows(c):
        return pl.ds(pl.multiple_of(c * step, 8), step)
    def root(c):
        return low + lax.rem(c, 2) if n % 2 == 0 else jnp.int32(low)
    def right(src, dst, c):
        return pltpu.make_async_remote_copy(src_ref=src.at[rows(c)], dst_ref=dst.at[rows(c)], send_sem=sr.at[c], recv_sem=rl.at[c],
            device_id={"head": z + 1}, device_id_type=MESHID)
    def left(src, dst, c):
        return pltpu.make_async_remote_copy(src_ref=src.at[rows(c)], dst_ref=dst.at[rows(c)], send_sem=sl.at[c], recv_sem=rr.at[c],
            device_id={"head": z - 1}, device_id_type=MESHID)
    def forward_step(c):
        r = root(c)
        @pl.when((z < r) & (z == 0))
        def _():
            right(x_ref, inl, c).start()
        @pl.when((z < r) & (z > 0))
        def _():
            right(x_ref, inl, c).wait_recv()
            inl[rows(c), :] = inl[rows(c), :] + x_ref[rows(c), :]
            right(inl, inl, c).start()
        @pl.when((z > r) & (z == n - 1))
        def _():
            left(x_ref, inr, c).start()
        @pl.when((z > r) & (z < n - 1))
        def _():
            left(x_ref, inr, c).wait_recv()
            inr[rows(c), :] = inr[rows(c), :] + x_ref[rows(c), :]
            left(inr, inr, c).start()
    def root_step(c):
        @pl.when(z == root(c))
        def _():
            @pl.when(z > 0)
            def _():
                right(x_ref, inl, c).wait_recv()
            @pl.when(z == 0)
            def _():
                inl[rows(c), :] = jnp.zeros_like(inl[rows(c), :])
            @pl.when(z < n - 1)
            def _():
                left(x_ref, inr, c).wait_recv()
            @pl.when(z == n - 1)
            def _():
                inr[rows(c), :] = jnp.zeros_like(inr[rows(c), :])
            total = x_ref[rows(c), :] + inl[rows(c), :] + inr[rows(c), :]
            o_ref[rows(c), :] = total if forward else total + base[rows(c), :]
            @pl.when(z > 0)
            def _():
                left(o_ref, o_ref, c).start()
            @pl.when(z < n - 1)
            def _():
                right(o_ref, o_ref, c).start()
    def spread_step(c):
        r = root(c)
        @pl.when((z < r) & (z > 0))
        def _():
            left(o_ref, o_ref, c).wait_recv()
            left(o_ref, o_ref, c).start()
        @pl.when((z > r) & (z < n - 1))
        def _():
            right(o_ref, o_ref, c).wait_recv()
            right(o_ref, o_ref, c).start()

    def end_step(c, carry):
        r = root(c)
        @pl.when((z < r) & (z == 0))
        def _():
            left(o_ref, o_ref, c).wait_recv()
        @pl.when((z > r) & (z == n - 1))
        def _():
            right(o_ref, o_ref, c).wait_recv()
        return carry

    def sent(c, to_right, to_left):
        @pl.when(to_right & (z < n - 1))
        def _():
            right(o_ref, o_ref, c).wait_send()
        @pl.when(to_left & (z > 0))
        def _():
            left(o_ref, o_ref, c).wait_send()
    stages = [
        (0, forward_step, lambda c: sent(c, z < root(c), z > root(c))),
        (d1, root_step, lambda c: sent(c, z == root(c), z == root(c))),
        (d2, spread_step, lambda c: sent(c, z > root(c), z < root(c))),
    ]
    start_extra()
    if not forward:
        planned.append((6, back_tail))
    if full:
        fgot_own = pltpu.make_async_copy(f_ref, fgot.at[me], hl)
        fgot_own.start()
        for k in range(1, seq):
            small(k).start()
        fgot_own.wait()
        planned.append((7, end_small))
    if ng:
        g_start()
        planned.append((count, g_forward))
    if ns:
        s_start(3)
        for i, when in ((3, 2), (0, 3), (1, 5), (2, 7)):
            planned.append((when, functools.partial(s_middle, i)))
        if full:
            planned.append((count + 1, b_start))

    def nth(i):
        return jnp.where(z <= low, i + 1 - 2 * lax.rem(i, 2), i)

    def body(t, carry):
        for lag, step_of, sent_of in stages:
            i = t - lag
            @pl.when((i >= window) & (i < count + window))
            def _():
                sent_of(nth(i - window))
            @pl.when((i >= 0) & (i < count))
            def _():
                step_of(nth(i))
        for when, run in planned:
            pl.when(t == when)(run)
        return carry
    lax.fori_loop(0, count + d2 + window, body, 0)
    for i in range(1 if full else 0, ns):
        s_final(i)
    lax.fori_loop(0, count, end_step, 0)
    if ng:
        g_end()
    s_drain()
    if full:
        b_end()
        end_shared()
        fo_ref[:, : sh.shape[1]] = sh[...]
    if forward:
        end_extra()
        size = x_ref.shape[0]
        square = jnp.concatenate([eo_ref[...], jnp.zeros((WIDE - 8, size), jnp.float32)], axis=0).T
        hidden_o[...] = base[...] + lax.rsqrt(square[:, 0:1] / inner_all + EPS) * o_ref[...]

        @pl.when(me < seq - 1)
        def _():
            tail_copy().start()

        @pl.when(me == 0)
        def _():
            tail_o[...] = jnp.zeros_like(tail_o)

        @pl.when(me > 0)
        def _():
            tail_copy().wait_recv()

        @pl.when(me < seq - 1)
        def _():
            tail_copy().wait_send()
    else:
        @pl.when(me < seq - 1)
        def _():
            tail_copy().wait_recv()
            last = pl.ds(x_ref.shape[0] - 8, 8)
            o_ref[last, :] = o_ref[last, :] + tailgot[...]

        @pl.when(me > 0)
        def _():
            tail_copy().wait_send()


def exchange(ins, cid, gathers=(), full=(), bc_loc=0, inner_all=0, layer=0, parts=16, order=(2, 5, 3)):
    n, seq = lax.axis_size("head"), lax.axis_size("seq")
    chips = seq // 2
    back = not inner_all
    ng, ns = len(gathers), 4 if back else 0
    base = ins[-1]
    rows, width = base.shape
    e_shape = (8, width) if back else ins[1].shape
    g_shapes = [g.shape[-2:] for g, _ in gathers]
    vm = lambda *shape: pltpu.VMEM(shape, jnp.float32)
    dma = pltpu.SemaphoreType.DMA
    scratch = [vm(rows, width)] * 2
    outs = []
    if back:
        inner, side = ins[6].shape[1], ins[5].shape[1]
        outs = [(width // seq, side)] + [(width // seq, inner)] * 3
        small = (full[1].shape[0] + 8 if full else 8, max(width, side + inner))
        shapes = [(rows, width)] + outs + ([(outs[0][0], 2 * bc_loc), small] if full else [small])
        spaces = [VM] * len(shapes)
        scratch += [vm(rows, width), vm(rows + 8, width), vm(8, width), vm(8, width), vm(8, width), vm(width, side), vm(width, inner), vm(width, inner)]
        if full:
            scratch += [vm(*small)]
    else:
        shapes = [(rows, width), e_shape] + [(seq * r, c) for r, c in g_shapes] + [(rows, width), (8, width)]
        spaces = [VM] * 2 + [HB] * ng + [VM] * 2
    scratch += [vm(n, *e_shape)] + [vm(chips, *o) for o in outs] * 2
    if full:
        shared, bc = (small[0], 2 * STATE), (outs[0][0], 2 * bc_loc)
        scratch += [vm(seq, *small), vm(n, *shared), vm(*shared), vm(n, *bc), vm(n, *bc)]
    scratch += [dma((parts,))] * 4 + [dma((n,))] * 2 + [dma] * 3
    if ng:
        scratch += [dma((ng, chips))] * 4 + [dma((ng,))]
    if ns:
        scratch += [dma((ns, chips))] * 4
    if full:
        scratch += [dma((seq,))] * 2 + [dma((n,))] * 2 + [dma] + [dma((n,))] * 2 + [dma]
    spec = (n, seq, tuple(at for _, at in gathers), ns, bc_loc, inner_all, rows // parts, order, (layer, min(BLOCK, rows)))
    return kernel_call(
        functools.partial(exchange_kernel, spec), "exchange", [f32(*s) for s in shapes],
        [*ins, *[g for g, _ in gathers], *full], scratch, cid=cid,
        specs=[VM] * len(ins) + [HB] * ng + [VM] * len(full), out_specs=spaces,
    )


def turned(array):
    rows, columns = array.shape
    up, across = -rows % WIDE, -columns % WIDE
    if across:
        array = jnp.concatenate([array, jnp.zeros((rows, across), jnp.float32)], axis=1)
    if up:
        array = jnp.concatenate([array, jnp.zeros((up, columns + across), jnp.float32)], axis=0)
    return array.T


def bookkeeping(me, lengths, block, masks_o, segrow_o, cmask_o, earlier_o, later_o):
    count = masks_o.shape[0]
    base = me * count

    def segment(position):
        start = jnp.int32(0)
        total = jnp.full(position.shape, -1, jnp.int32)
        for d in range(lengths.shape[0]):
            total = total + (position >= start).astype(jnp.int32)
            start = start + lengths[d]
        return total

    row = lax.broadcasted_iota(jnp.int32, masks_o.shape, 0)
    lane = lax.broadcasted_iota(jnp.int32, masks_o.shape, 1)
    first = row - lax.rem(row, block)
    margin = KERNEL - 1
    at = jnp.where(lane < margin, row - margin + lane, jnp.where(lane == 3, first - 1, jnp.where(lane == 4, first + block - 1, row)))
    seg = segment(base + at)
    own = segment(base + row)
    masks_o[...] = jnp.where(lane < 5, (seg == own).astype(jnp.float32), own.astype(jnp.float32))
    segrow_o[...] = segment(base + lax.broadcasted_iota(jnp.int32, segrow_o.shape, 1)).astype(jnp.float32)
    first = lax.broadcasted_iota(jnp.int32, cmask_o.shape, 0) * block
    cmask_o[...] = (segment(base + first - 1) == segment(base + first + block - 1)).astype(jnp.float32)
    place = lax.broadcasted_iota(jnp.int32, earlier_o.shape, 0)
    earlier_o[...] = (place < me).astype(jnp.float32)
    later_o[...] = (place > me).astype(jnp.float32)


def opening_kernel(n, seq, block, lengths, z_ref, x_ref, bc_ref, ck_ref, cb_ref, dt_ref, h_ref, cxk, cxb, dtb, alog, skip, *refs):
    wz_o, wx_o, side_o, own_o, tail_o, hp_o, cw_o, *books = refs[:12]
    bc_got, ck_got, cb_got, side, hs, hr, hl, ss, rs, fs, fr, ls, ts, tr = refs[12:]
    heads, layers, rows = dt_ref.shape
    z = lax.axis_index("head")
    me, chips, core, chip, sib = seq_place(seq)
    count = h_ref.shape[0]
    bar = pltpu.get_barrier_semaphore()
    for k in range(1, n):
        pl.semaphore_signal(bar, inc=1, device_id={"head": lax.rem(z + k, n)}, device_id_type=MESHID)
    for k in range(1, seq):
        pl.semaphore_signal(bar, inc=1, device_id={"seq": lax.rem(me + k, seq)}, device_id_type=MESHID)
    pl.semaphore_wait(bar, n - 1 + seq - 1)
    columns = [(bc_ref, bc_got), (ck_ref, ck_got), (cb_ref, cb_got)]

    def own(i):
        return pltpu.make_async_copy(columns[i][0], columns[i][1].at[z], hl.at[i])

    def head(i, k):
        return pltpu.make_async_remote_copy(src_ref=columns[i][0], dst_ref=columns[i][1].at[z], send_sem=hs.at[i, k], recv_sem=hr.at[i, k],
            device_id={"head": lax.rem(z + k, n)}, device_id_type=MESHID)

    srcs = [z_ref.at[0], x_ref.at[0], side]
    dsts = [wz_o, wx_o, side_o]
    number = len(srcs)

    def at(i, owner):
        return dsts[i].at[pl.ds(pl.multiple_of(owner * rows, 8), rows)]

    def back(k):
        return lax.rem(chip - k + chips, chips) * 2 + core

    def local(i):
        return pltpu.make_async_copy(srcs[i], at(i, me), ls.at[i])

    def across(i, k):
        return pltpu.make_async_remote_copy(src_ref=srcs[i], dst_ref=at(i, me), send_sem=ss.at[i, k], recv_sem=rs.at[i, k],
            device_id={"seq": lax.rem(chip + k, chips) * 2 + core}, device_id_type=MESHID)

    def over(i, k):
        return pltpu.make_async_remote_copy(src_ref=srcs[i] if k == 0 else at(i, back(k)), dst_ref=at(i, back(k)), send_sem=fs.at[i, k], recv_sem=fr.at[i, k],
            device_id={"seq": sib}, device_id_type=MESHID)

    def tail():
        return pltpu.make_async_remote_copy(src_ref=h_ref.at[pl.ds(count - 8, 8)], dst_ref=tail_o, send_sem=ts, recv_sem=tr,
            device_id={"seq": me + 1}, device_id_type=MESHID)

    def send(i):
        for k in range(1, chips):
            across(i, k).start()
        over(i, 0).start()
        local(i).start()

    for i in range(3):
        for k in range(1, n):
            head(i, k).start()
        own(i).start()

    @pl.when(me < seq - 1)
    def _():
        tail().start()

    @pl.when(me == 0)
    def _():
        tail_o[...] = jnp.zeros_like(tail_o)

    send(0)
    send(1)
    for i in range(3):
        own(i).wait()
        for k in range(1, n):
            head(i, k).wait()
    for l in range(layers):
        of_heads = turned(jnp.concatenate([dt_ref[h, l : l + 1, :] for h in range(heads)], axis=0))
        whole = jnp.concatenate([turned(jnp.concatenate([bc_got[p, l] for p in range(n)], axis=0))[:rows], of_heads[:rows]], axis=1)
        if l == 0:
            side[...] = whole
            send(2)
        else:
            own_o[(l - 1) * rows : l * rows, :] = whole
    inner = cxb.shape[1]
    for l in range(layers):
        taps = jnp.concatenate([cxk[l]] + [ck_got[p, l] for p in range(n)], axis=1)
        bias = jnp.concatenate([cxb[l : l + 1, :]] + [cb_got[p, l : l + 1, :] for p in range(n)], axis=1)
        cw_o[8 * l : 8 * l + 8, :] = jnp.concatenate([taps, bias, jnp.zeros((7 - KERNEL, inner + 2 * STATE), jnp.float32)], axis=0)
        heads_of = jnp.concatenate([dtb[l : l + 1, :], alog[l : l + 1, :], skip[l : l + 1, :], jnp.zeros((5, heads), jnp.float32)], axis=0)
        hp_o[8 * l : 8 * l + 8, :] = jnp.concatenate([heads_of, jnp.zeros((8, WIDE - heads), jnp.float32)], axis=1)
    bookkeeping(me, lengths, block, *books)
    pairs = [(i, k) for i in range(number) for k in range(1, chips)]
    for i, k in pairs:
        across(i, k).wait_recv()
        over(i, k).start()
    for i in range(number):
        for k in range(chips):
            over(i, k).wait()
        local(i).wait()
    for i, k in pairs:
        across(i, k).wait_send()

    @pl.when(me > 0)
    def _():
        tail().wait_recv()

    @pl.when(me < seq - 1)
    def _():
        tail().wait_send()


def opening(lengths, proj_z, proj_x, proj_bc, ck, cb, proj_dt, hidden, cxk, cxb, dtb, alog, skip, cid):
    n, seq = lax.axis_size("head"), lax.axis_size("seq")
    layers, rows, inner = proj_z.shape
    chips = seq // 2
    count, width = hidden.shape
    side = 2 * STATE + WIDE
    full = rows * seq
    dma = pltpu.SemaphoreType.DMA
    smem = pl.BlockSpec(memory_space=pltpu.SMEM)
    return pl.pallas_call(
        functools.partial(opening_kernel, n, seq, min(BLOCK, count)),
        out_shape=[f32(full, inner), f32(full, inner), f32(full, side), f32((layers - 1) * rows, side), f32(8, width),
                   f32(8 * layers, WIDE), f32(8 * layers, inner + 2 * STATE), f32(count, 8), f32(8, count), f32(8, WIDE), f32(seq, WIDE), f32(seq, WIDE)],
        in_specs=[smem, HB, HB, HB, HB, HB, VM, HB] + [VM] * 5,
        out_specs=[HB, HB, HB] + [VM] * 9,
        scratch_shapes=[pltpu.VMEM((n,) + a.shape, jnp.float32) for a in (proj_bc, ck, cb)] + [pltpu.VMEM((rows, side), jnp.float32)]
        + [dma((3, n))] * 2 + [dma((3,))] + [dma((3, chips))] * 4 + [dma((3,)), dma, dma],
        compiler_params=pltpu.CompilerParams(collective_id=cid, has_side_effects=True),
        name="opening",
    )(lengths, proj_z, proj_x, proj_bc, ck, cb, proj_dt, hidden, cxk, cxb, dtb, alog, skip)


def finish_kernel(n, inner_all, e, bcs, squares, hidden, half0, half1, grad, *refs):
    z = lax.axis_index("head")
    big = refs[:8]
    (hidden_o, grad_o, ngain_o, z_o, x_o, bc_o, dt_o, cxk_o, cxb_o, cbk_o, cbb_o, dtb_o, alog_o, skip_o, ggain_o, out_o) = refs[8:]
    half = half0.shape[0]
    size = hidden.shape[0]
    scale = lax.rsqrt(turned(squares[...])[:size, 0:1] / inner_all + EPS)
    hidden_o[0:half, :] = hidden[0:half, :] + scale[0:half] * half0[...]
    hidden_o[half:, :] = hidden[half:, :] + scale[half:] * half1[...]
    grad_o[...] = grad[...]
    inner, heads, bc_loc, rows = z_o.shape[2], dt_o.shape[0], bc_o.shape[1], bc_o.shape[2]
    bcs_t = turned(bcs[...])
    bc = 2 * STATE
    for l in range(2):
        side, gz, gx, gout = big[4 * l : 4 * l + 4]
        z_o[l], x_o[l], out_o[l] = gz[...], gx[...], gout[...]
        bc_o[l] = bcs_t[l * bc_loc : (l + 1) * bc_loc, :rows]
        of_heads = turned(side[:, bc:])
        for h in range(heads):
            dt_o[h, l : l + 1, :] = of_heads[h : h + 1, :rows]
        s = e[8 * l : 8 * l + 8, :]
        for i in range(ngain_o.shape[1] // bc):
            ngain_o[l : l + 1, i * bc : (i + 1) * bc] = s[5 + i : 6 + i, :bc]
        cxk_o[l] = s[0:KERNEL, bc : bc + inner]
        cxb_o[l : l + 1, :] = s[KERNEL : KERNEL + 1, bc : bc + inner]
        ggain_o[l : l + 1, :] = s[5:6, bc : bc + inner]
        mine = jnp.zeros((8, bc_loc), jnp.float32)
        for p in range(n):
            mine = jnp.where(z == p, s[:, p * bc_loc : (p + 1) * bc_loc], mine)
        cbk_o[l] = mine[0:KERNEL]
        cbb_o[l : l + 1, :] = mine[KERNEL : KERNEL + 1]
        last = s[:, -WIDE:]
        dtb_o[l : l + 1, :] = last[0:1, :heads]
        alog_o[l : l + 1, :] = last[1:2, :heads]
        skip_o[l : l + 1, :] = last[2:3, :heads]


def seq_place(n):
    me = lax.axis_index("seq")
    chips = n // 2
    core, chip = lax.rem(me, 2), me // 2
    return me, chips, core, chip, me + 1 - 2 * core


def body(
    hidden_in, grad_out, doc_lengths, norm_gain, proj_z, proj_x, proj_bc, proj_dt, conv_x_kernel, conv_x_bias,
    conv_bc_kernel, conv_bc_bias, dt_bias, a_log, skip_gain, gate_gain, proj_out,
):
    count, width = hidden_in.shape
    layers, rows_loc, inner = proj_z.shape
    bc_loc = proj_bc.shape[2]
    heads = proj_dt.shape[2]
    n_seq, n_head = lax.axis_size("seq"), lax.axis_size("head")
    inner_all = inner * n_head
    bc_all = 2 * STATE
    block = min(BLOCK, count)
    blocks = count // block
    mine = lax.axis_index("seq")

    (wz0, wx0, side0, side_own, tail, hp, cw, masks, segrow, cmask, earlier, following) = opening(
        doc_lengths, proj_z, proj_x, proj_bc.transpose(0, 2, 1), conv_bc_kernel, conv_bc_bias, proj_dt.transpose(2, 0, 1), hidden_in,
        conv_x_kernel, conv_x_bias, dt_bias, a_log, skip_gain, 2,
    )
    wz, wx, wside, wout = [wz0], [wx0], [side0], [proj_out]
    vm = lambda *shape: pltpu.VMEM(shape, jnp.float32)
    chips = n_seq // 2

    hidden = hidden_in
    saved = []
    more = count * 17 // 32 // 8 * 8
    for l in range(layers):
        final = l == layers - 1
        z, raw, dt, act, cum, carry, decays, e, mixed, entry, *rows = kernel_call(
            functools.partial(forward_kernel, l, heads, block, final, n_seq), "forward",
            [f32(count, inner), f32(count + 8, inner + bc_all), f32(count, WIDE), f32(count, inner + bc_all), f32(count, WIDE), f32(8, WIDE),
             f32(n_seq, WIDE), f32(8, count), f32(count, inner), f32(blocks * inner, STATE)]
            + ([f32(more, width), f32(count - more, width)] if final else [f32(count, width)])
            + ([f32(width, inner)] if l == 0 else []),
            [hidden, tail, norm_gain, wz[l], wx[l], wside[l], cw, hp, masks, segrow, cmask, earlier, gate_gain, wout[l], grad_out],
            [vm(count, width), vm(count, inner), vm(blocks * inner, STATE), vm(count, inner), vm(inner + 8, STATE), vm(n_seq, inner + 8, STATE)]
            + gather_sems(chips) * (2 if l == 0 else 1),
            cid=10 + 10 * l,
            specs=[VM] * 13 + [HB if l == 0 else VM, VM if final else HB],
        )
        if l == 0:
            wout[0] = rows.pop()
        hidden_l, tail_l = hidden, tail
        if final:
            last_rows = rows
            sums = grad_out
        else:
            sums, e, *weights, hidden, tail = exchange(
                [rows[0], e, hidden], 11 + 10 * l, inner_all=inner_all,
                gathers=[(proj_z, l + 1), (proj_x, l + 1), (proj_out, l + 1), (side_own[l * rows_loc : (l + 1) * rows_loc], None)],
            )
            for held, new in zip((wz, wx, wout, wside), weights):
                held.append(new)
        saved.append((hidden_l, tail_l, z, raw, dt, act, cum, carry, decays, mixed, entry, e, sums))

    grad = grad_out
    big = [None] * layers
    small, out_parts = [], []
    for l in reversed(range(layers)):
        final = l == layers - 1
        hidden_l, tail, z, raw, dt, act, cum, carry, decays, mixed, entry, e, sums = saved[l]
        dz, draw, ddt, dcw, dhp, dwout, dggain, *extra = kernel_call(
            functools.partial(backward_kernel, l, heads, block, inner_all, final, n_seq, n_head), "backward",
            [f32(count, inner), f32(count + 8, inner + bc_all), f32(count, WIDE), f32(8, inner + bc_all), f32(8, WIDE), f32(width, inner), f32(8, inner)]
            + [f32(8, count)] * (1 if final else 0),
            [grad, e, sums, act, cum, masks, carry, z, gate_gain, wout[l], mixed, entry, decays, following, raw, dt, segrow, cw, hp],
            [vm(count, inner), vm(count, inner), vm(count, WIDE), vm(count, STATE), vm(blocks * inner, STATE), vm(inner, STATE),
             vm(n_seq, inner, STATE), vm(count, inner + bc_all), vm(count, inner), vm(count, STATE)]
            + gather_sems(chips)
            + ([vm(n_head, 8, count)] + [pltpu.SemaphoreType.DMA((n_head,))] * 2 + [pltpu.SemaphoreType.DMA] if final else []),
            cid=12 + 10 * l,
        )
        if final:
            squares = extra[0]
            out_parts.append(lax.psum(last_rows[0], "head"))
        ins = [hidden_l, tail, norm_gain, wz[l], wx[l], wside[l], dz, draw, ddt, dcw, dhp, dggain, dwout, grad]
        if l > 0:
            grad, *big[l], smalls = exchange(ins, 14 + 10 * l, layer=l)
            late, grad, out_parts = lax.optimization_barrier((last_rows[1], grad, out_parts))
            out_parts.append(lax.psum(late, "head"))
        else:
            grad, *big[l], bcs, e = exchange(ins, 14, full=(big[1][0], smalls), bc_loc=bc_loc)
    outs = [
        (count, width), (count, width), (layers, width), proj_z.shape, proj_x.shape, (layers, bc_loc, rows_loc), (heads, layers, rows_loc), conv_x_kernel.shape,
        conv_x_bias.shape, conv_bc_kernel.shape, conv_bc_bias.shape, dt_bias.shape, a_log.shape, skip_gain.shape, gate_gain.shape, proj_out.shape,
    ]
    results = list(kernel_call(
        functools.partial(finish_kernel, n_head, inner_all), "finish", [f32(*o) for o in outs],
        [e, bcs, squares, hidden, *out_parts, grad, *big[0], *big[1]],
    ))
    results[5] = results[5].transpose(0, 2, 1)
    results[6] = results[6].transpose(1, 2, 0)
    return tuple(results)


def solution(mesh):
    in_specs = (
        P("seq", None),
        P("seq", None),
        P(),
        P(),
        P(None, "seq", "head"),
        P(None, "seq", "head"),
        P(None, "seq", "head"),
        P(None, "seq", "head"),
        P(None, None, "head"),
        P(None, "head"),
        P(None, None, "head"),
        P(None, "head"),
        P(None, "head"),
        P(None, "head"),
        P(None, "head"),
        P(None, "head"),
        P(None, "seq", "head"),
    )
    out_specs = (
        P("seq", None),
        P("seq", None),
        P(),
        P(None, "seq", "head"),
        P(None, "seq", "head"),
        P(None, "seq", "head"),
        P(None, "seq", "head"),
        P(None, None, "head"),
        P(None, "head"),
        P(None, None, "head"),
        P(None, "head"),
        P(None, "head"),
        P(None, "head"),
        P(None, "head"),
        P(None, "head"),
        P(None, "seq", "head"),
    )
    return jax.shard_map(body, mesh=mesh, in_specs=in_specs, out_specs=out_specs, check_vma=False)
```
